32 devices in a mesh: groups: 2 (over y), dp: 8 (over z, x), mp: 2 (over core).
Axes of the slice: x: 2, y: 2, z: 4, core: 2. Of those that a mesh axis runs over, the one named last changes fastest.
Arguments:
- tokens: bfloat16 [2048, 4096], P(('groups', 'dp'), 'mp'), parts along dimension 0, may hold values from -6 to 6
- cotangent: bfloat16 [2048, 4096], P(('groups', 'dp'), 'mp'), parts along dimension 0, may hold values from -6 to 6
- gate_spectra: bfloat16 [28, 8, 512], P('mp'), may hold values from -1.5 to 1.5
- up_spectra: bfloat16 [28, 8, 512], P('mp'), may hold values from -1.5 to 1.5
- down_spectra: bfloat16 [8, 28, 512], P('mp'), may hold values from -0.75 to 0.75
Outputs:
- grad_tokens: bfloat16 [2048, 4096], P(('groups', 'dp'), 'mp'), parts along dimension 0
- grad_gate: float32 [56, 8, 512], P(('groups', 'mp')), parts along dimension 0
- grad_up: float32 [56, 8, 512], P(('groups', 'mp')), parts along dimension 0
- grad_down: float32 [16, 28, 512], P(('groups', 'mp')), parts along dimension 0
The draws below stay inside these ranges and needn't reach their ends.
There are 2 independent parts, one for each index of `groups`. The reference program is written for one: setup_inputs(seed, part) draws one part's arguments, and reference() takes and returns one part's arrays. A program takes and returns all parts, laid end to end along the dimension named above; an argument that names none is the same for every part. Nothing has to cross between parts.
All inputs are finite; a program needn't handle non-finite values.
Results may differ from the reference program's by a relative error of at most 0.012.
The reference program's roundings to bfloat16 on the way count: a program that leaves them out, or rounds other values in their place, can miss the bound.
Values may be sent and summed in bfloat16 or wider, within the bound.
No kernel may reach another device: no remote copies, remote signals or barrier semaphores. Data moves between devices by JAX's collectives and lax.ppermute only.
A program may use at most 128 MiB of HBM per device.

```python
import math
import jax
import jax.numpy as jnp
from jax import lax

BLOCK = 512
D = 4096
DB = 8
FB = 28
TOK_DEV = 128
TOKENS = 1024
N_DP = 8


def block_levels(key, dims, shards, low, top_value):
    loudness, own = 1.0, jax.random.fold_in(key, 6)
    for axis_at, blocks in shards:
        steps = jnp.exp(jax.random.uniform(jax.random.fold_in(own, axis_at), (blocks,), jnp.float32, low / len(shards), top_value / len(shards)))
        loudness = loudness * jnp.repeat(steps, dims[axis_at] // blocks).reshape([-1 if axis == axis_at else 1 for axis in range(len(dims))])
    return loudness


def normal_values(stream_key, extent, deviation, limit, split=(), held_as=jnp.bfloat16):
    entries = deviation * jax.random.normal(stream_key, extent, jnp.float32)
    if split:
        entries = entries * block_levels(stream_key, extent, split, -0.22, 0.18)
    return jnp.clip(entries, -limit, limit).astype(held_as)


def setup_inputs(seed: int = 0, part: int = 0) -> dict:
    arg_keys = jax.random.split(jax.random.key(seed), 6)
    own_keys = jax.random.split(jax.random.fold_in(arg_keys[5], part), 6)
    return {
        "tokens": normal_values(own_keys[0], (TOKENS, D), 1.0, 6.0, ((0, 8), (1, 2))),
        "cotangent": normal_values(own_keys[1], (TOKENS, D), 1.0, 6.0, ((0, 8), (1, 2))),
        "gate_spectra": normal_values(arg_keys[2], (FB, DB, BLOCK), (2 * DB) ** -0.5, 1.5, ((0, 2),)),
        "up_spectra": normal_values(arg_keys[3], (FB, DB, BLOCK), (2 * DB) ** -0.5, 1.5, ((0, 2),)),
        "down_spectra": normal_values(arg_keys[4], (DB, FB, BLOCK), (2 * FB) ** -0.5, 0.75, ((0, 2),)),
    }


def transform_tables(block_size):
    half_size = block_size // 2
    positions = jnp.arange(block_size, dtype=jnp.int32)
    frequency = jnp.arange(half_size, dtype=jnp.int32)
    phase_index = positions[:, None] * frequency[None, :] % block_size
    angles = phase_index.astype(jnp.float32) * (2.0 * math.pi / block_size)
    cosine = jnp.cos(angles)
    sine_table = jnp.sin(angles)
    parity = (1 - 2 * (positions % 2)).astype(jnp.float32)
    norm_factor = 1.0 / math.sqrt(block_size)
    forward_table = jnp.concatenate([cosine, parity[:, None], -sine_table[:, 1:]], axis=1) * norm_factor
    doubling = jnp.where(frequency >= 1, 2.0, 1.0).astype(jnp.float32)
    inverse_table = jnp.concatenate([(cosine * doubling[None, :]).T, parity[None, :], -2.0 * sine_table[:, 1:].T], axis=0) * norm_factor
    return (forward_table.astype(jnp.bfloat16), inverse_table.astype(jnp.bfloat16))

def to_spectra(values, table):
    row_count = values.shape[0]
    flat = jnp.dot(values.reshape(-1, table.shape[0]), table, preferred_element_type=jnp.float32)
    return flat.reshape(row_count, -1, table.shape[0]).astype(jnp.bfloat16)

def from_spectra(spectra, table):
    row_count = spectra.shape[0]
    flat = jnp.dot(spectra.reshape(-1, table.shape[0]), table, preferred_element_type=jnp.float32)
    return flat.reshape(row_count, -1)

def product(pattern, left_operand, right_operand):
    return jnp.einsum(pattern, left_operand.astype(jnp.float32), right_operand.astype(jnp.float32), precision=lax.Precision.HIGHEST)

def keep_mask(half_size):
    return (jnp.arange(half_size) >= 1).astype(jnp.float32)

def weight_forms(weight):
    half_size = weight.shape[-1] // 2
    mask_values = keep_mask(half_size)
    real_part = weight[..., :half_size].astype(jnp.float32)
    imag_part = weight[..., half_size:].astype(jnp.float32)
    return (real_part, imag_part * mask_values, real_part * mask_values + imag_part * (1.0 - mask_values))

def forward_apply(spectra, forms):
    half_size = spectra.shape[-1] // 2
    spec_real, spec_imag = (spectra[..., :half_size], spectra[..., half_size:])
    real_part, imag_masked, cross_part = forms
    out_real = product('tik,oik->tok', spec_real, real_part) - product('tik,oik->tok', spec_imag, imag_masked)
    out_imag = product('tik,oik->tok', spec_real, imag_masked) + product('tik,oik->tok', spec_imag, cross_part)
    return jnp.concatenate([out_real, out_imag], axis=-1)

def adjoint_apply(spectra, forms):
    half_size = spectra.shape[-1] // 2
    spec_real, spec_imag = (spectra[..., :half_size], spectra[..., half_size:])
    real_part, imag_masked, cross_part = forms
    out_real = product('tok,oik->tik', spec_real, real_part) + product('tok,oik->tik', spec_imag, imag_masked)
    out_imag = product('tok,oik->tik', spec_imag, cross_part) - product('tok,oik->tik', spec_real, imag_masked)
    return jnp.concatenate([out_real, out_imag], axis=-1)

def weight_grad(source_spec, target_spec):
    half_size = source_spec.shape[-1] // 2
    mask_values = keep_mask(half_size)
    source_real, source_imag = (source_spec[..., :half_size], source_spec[..., half_size:])
    target_real, target_imag = (target_spec[..., :half_size], target_spec[..., half_size:])
    both_real = product('tik,tok->oik', source_real, target_real)
    both_imag = product('tik,tok->oik', source_imag, target_imag)
    real_imag = product('tik,tok->oik', source_real, target_imag)
    imag_real = product('tik,tok->oik', source_imag, target_real)
    grad_real = (1.0 + mask_values) * (both_real + mask_values * both_imag)
    grad_imag = 2.0 * mask_values * (real_imag - imag_real) + (1.0 - mask_values) * both_imag
    return jnp.concatenate([grad_real, grad_imag], axis=-1)

def swiglu_back(gate_values, up_values, hidden_grad):
    sigmoid_gate = jax.nn.sigmoid(gate_values)
    gate_grad = (hidden_grad * up_values * sigmoid_gate * (1.0 + gate_values * (1.0 - sigmoid_gate))).astype(jnp.bfloat16)
    up_grad = (hidden_grad * gate_values * sigmoid_gate).astype(jnp.bfloat16)
    return (gate_grad, up_grad)

def reference(tokens, cotangent, gate_spectra, up_spectra, down_spectra):
    forward_table, inverse_table = transform_tables(BLOCK)
    gate_forms = weight_forms(gate_spectra)
    up_forms = weight_forms(up_spectra)
    down_forms = weight_forms(down_spectra)
    block_rows = TOK_DEV * min(N_DP, 8)
    block_count = TOKENS // block_rows
    token_blocks = tokens.reshape(block_count, block_rows, D)
    cotangent_blocks = cotangent.reshape(block_count, block_rows, D)

    def advance(carry, inputs):
        token_block, cotangent_block = inputs
        token_spec = to_spectra(token_block, forward_table)
        gate_values = from_spectra(forward_apply(token_spec, gate_forms).astype(jnp.bfloat16), inverse_table)
        up_values = from_spectra(forward_apply(token_spec, up_forms).astype(jnp.bfloat16), inverse_table)
        hidden = (gate_values * jax.nn.sigmoid(gate_values) * up_values).astype(jnp.bfloat16)
        hidden_spec = to_spectra(hidden, forward_table)
        cotangent_spec = to_spectra(cotangent_block, forward_table)
        hidden_grad = from_spectra(adjoint_apply(cotangent_spec, down_forms).astype(jnp.bfloat16), inverse_table)
        gate_grad, up_grad = swiglu_back(gate_values, up_values, hidden_grad)
        gate_grad_spec = to_spectra(gate_grad, forward_table)
        up_grad_spec = to_spectra(up_grad, forward_table)
        input_spec = (adjoint_apply(gate_grad_spec, gate_forms) + adjoint_apply(up_grad_spec, up_forms)).astype(jnp.bfloat16)
        grad_rows = from_spectra(input_spec, inverse_table).astype(jnp.bfloat16)
        sums = (carry[0] + weight_grad(token_spec, gate_grad_spec), carry[1] + weight_grad(token_spec, up_grad_spec), carry[2] + weight_grad(hidden_spec, cotangent_spec))
        return (sums, grad_rows)
    zero_sums = (jnp.zeros((FB, DB, BLOCK), jnp.float32), jnp.zeros((FB, DB, BLOCK), jnp.float32), jnp.zeros((DB, FB, BLOCK), jnp.float32))
    sums, grad_blocks = lax.scan(advance, zero_sums, (token_blocks, cotangent_blocks))
    grad_scale = 1.0 / math.sqrt(TOKENS)
    return (grad_blocks.reshape(TOKENS, D), sums[0] * grad_scale, sums[1] * grad_scale, sums[2] * grad_scale)
```

```python
import functools
import math

import jax
import jax.numpy as jnp
import numpy as np
from jax import lax
from jax.experimental import pallas as pl
from jax.experimental.pallas import tpu as pltpu
from jax.sharding import PartitionSpec as P

F = 16
LANES = 128
ROWS = 16


def transform_tables(block):
    half = block // 2
    n = np.arange(block)
    k = np.arange(half)
    angles = ((n[:, None] * k[None, :]) % block).astype(np.float32) * np.float32(2.0 * math.pi / block)
    cosine = np.cos(angles.astype(np.float64)).astype(np.float32)
    sine = np.sin(angles.astype(np.float64)).astype(np.float32)
    parity = (1 - 2 * (n % 2)).astype(np.float32)
    norm = np.float32(1.0 / math.sqrt(block))
    forward = np.concatenate([cosine, parity[:, None], -sine[:, 1:]], axis=1) * norm
    doubling = np.where(k >= 1, 2.0, 1.0).astype(np.float32)
    inverse = np.concatenate([(cosine * doubling).T, parity[None, :], -2.0 * sine[:, 1:].T], axis=0) * norm
    order = np.arange(block).reshape(2, half // F, F).transpose(1, 0, 2).reshape(-1)
    return (
        jnp.asarray(forward.T[order], jnp.bfloat16),
        jnp.asarray(inverse.T[:, order], jnp.bfloat16),
    )


def nt_dot(a, b):
    return lax.dot_general(a, b, (((1,), (1,)), ((), ())), preferred_element_type=jnp.float32)


def swap_blocks(tiles):
    tiles = list(tiles)
    lane_block = lax.broadcasted_iota(jnp.int32, tiles[0].shape, 1) // F
    step = len(tiles) // 2
    while step:
        high = (lane_block & step) != 0
        for i in range(len(tiles)):
            if i & step:
                continue
            low_tile, high_tile = tiles[i], tiles[i + step]
            tiles[i] = jnp.where(high, pltpu.roll(high_tile, F * step, 1), low_tile)
            tiles[i + step] = jnp.where(high, high_tile, pltpu.roll(low_tile, LANES - F * step, 1))
        step //= 2
    return tiles


def weight_rows(read, write, conj, groups):
    half = groups * F
    for part in range(half // LANES):
        at = part * LANES
        re = swap_blocks([read(i, at) for i in range(8)])
        im = swap_blocks([read(i, half + at) for i in range(8)])
        for i in range(8):
            g = part * 8 + i
            cross, wim = re[i], im[i]
            if g == 0:
                first = lax.broadcasted_iota(jnp.int32, wim.shape, 1) % F == 0
                cross = jnp.where(first, wim, cross)
                wim = jnp.where(first, 0.0, wim)
            sign = 1.0 if conj else -1.0
            write(g, 0, 0, re[i])
            write(g, 0, 1, sign * wim)
            write(g, 1, 0, -sign * wim)
            write(g, 1, 1, cross)


def diagonal(width):
    row = lax.broadcasted_iota(jnp.int32, (F, width), 0)
    lane = lax.broadcasted_iota(jnp.int32, (F, width), 1)
    return lane % F == row


def main_kernel(groups, fb, x_own, x_other, c_own, c_other, pt_ref, qt_ref, wg_ref, wu_ref, wd_ref,
                d_ref, gg_ref, ug_ref, sx, sc, gs, us, hs, hid, rg, ru, rd, wexp, flat):
    core = lax.axis_index("mp")
    db = 8
    per = db // 2
    block = pt_ref.shape[0]

    for source, target in ((wg_ref, rg), (wu_ref, ru)):
        for tile in range(block // LANES):
            flat[tile] = source[:, tile * LANES : (tile + 1) * LANES].astype(jnp.float32)

        def read(i, at):
            return flat[at // LANES, pl.ds(i, fb, stride=db), :]

        def write(g, ri, tile, rows, target=target):
            target[tile, g * 2 * ROWS + ri * ROWS : g * 2 * ROWS + ri * ROWS + fb, :] = rows

        weight_rows(read, write, False, groups)

    def read_down(o, at):
        return wd_ref[o, :, at : at + LANES].astype(jnp.float32)

    def write_down(g, ri, tile, rows):
        rd[tile, g * 2 * ROWS + ri * ROWS : g * 2 * ROWS + ri * ROWS + fb, :] = rows

    weight_rows(read_down, write_down, True, groups)

    for own, other, target in ((x_own, x_other, sx), (c_own, c_other, sc)):
        for source, first in ((own, core * per), (other, (1 - core) * per)):
            for j in range(0, per, 2):
                pair = jnp.concatenate(
                    [source[:, j * block : (j + 1) * block], source[:, (j + 1) * block : (j + 2) * block]], axis=0
                )
                result = nt_dot(pt_ref[...], pair).astype(jnp.bfloat16)
                for u in range(2):
                    target[:, :, first + j + u] = result[:, u * LANES : (u + 1) * LANES].reshape(groups, 2, F, LANES)

    mask = diagonal(LANES)

    @pl.loop(0, groups)
    def _(g):
        for w, rows in enumerate((rg, ru, rd)):
            for ri in range(2):
                for o in range(fb):
                    at = ((w * 2 + ri) * fb + o) * F
                    for tile in range(2):
                        row = rows[tile, pl.ds(g * 2 * ROWS + ri * ROWS + o, F, stride=0), :]
                        wexp[at : at + F, tile * LANES : (tile + 1) * LANES] = jnp.where(mask, row, 0.0).astype(
                            jnp.bfloat16
                        )
        span = 2 * fb * F
        forward = jnp.dot(
            wexp[0 : 2 * span, :], sx[g].reshape(2 * LANES, LANES), preferred_element_type=jnp.float32
        ).astype(jnp.bfloat16)
        forward = forward.reshape(2, 2, fb, F, LANES)
        back = jnp.dot(
            wexp[2 * span : 3 * span, :], sc[g].reshape(2 * LANES, LANES), preferred_element_type=jnp.float32
        ).astype(jnp.bfloat16)
        back = back.reshape(2, fb, F, LANES)
        for ri in range(2):
            gs[:, g, ri] = forward[0, ri]
            us[:, g, ri] = forward[1, ri]
            hs[:, g, ri] = back[ri]

    for target in (gg_ref, ug_ref, hid):
        target[:, :, fb:] = jnp.zeros((groups, 2, ROWS - fb, F, LANES), jnp.bfloat16)

    @pl.loop(0, fb)
    def _(o):
        spectra = jnp.concatenate([ref[o].reshape(block, LANES) for ref in (gs, us, hs)], axis=1)
        values = jnp.dot(qt_ref[...], spectra, preferred_element_type=jnp.float32)
        gate, up, grad = (values[:, u * LANES : (u + 1) * LANES] for u in range(3))
        sig = 1.0 / (1.0 + jnp.exp(-gate))
        gated = gate * sig
        hidden = (gated * up).astype(jnp.bfloat16)
        gate_grad = (grad * up * sig * (1.0 + gate * (1.0 - sig))).astype(jnp.bfloat16)
        up_grad = (grad * gated).astype(jnp.bfloat16)
        result = jnp.dot(
            pt_ref[...], jnp.concatenate([hidden, gate_grad, up_grad], axis=1), preferred_element_type=jnp.float32
        ).astype(jnp.bfloat16)
        for u, target in enumerate((hid, gg_ref, ug_ref)):
            target[:, :, o] = result[:, u * LANES : (u + 1) * LANES].reshape(groups, 2, F, LANES)

    keep = diagonal(LANES)
    lane = lax.broadcasted_iota(jnp.int32, (F, LANES), 1)
    row = lax.broadcasted_iota(jnp.int32, (F, LANES), 0)

    @pl.loop(0, groups)
    def _(g):
        first = (lane % F == 0) & (row == 0) & (g == 0)
        weight = jnp.where(keep, jnp.where(first, 1.0, 2.0), 0.0)
        weight_pair = jnp.where(first, 0.0, weight)
        weight_first = jnp.where(first, 1.0, 0.0)
        span = 2 * ROWS * F
        for w, (rows, cols, sign) in enumerate(((gg_ref, sx, 1.0), (ug_ref, sx, 1.0), (hid, sc, -1.0))):
            m = nt_dot(rows[g].reshape(span, LANES), cols[g].reshape(2 * LANES, LANES)).reshape(2, ROWS, F, 2 * LANES)
            rr, ri = m[0, :, :, :LANES], m[0, :, :, LANES:]
            ir, ii = m[1, :, :, :LANES], m[1, :, :, LANES:]
            re = jnp.sum(rr * weight + ii * weight_pair, axis=1)
            im = jnp.sum((ir - ri) * (sign * weight_pair) + ii * weight_first, axis=1)
            d_ref[g, w * ROWS : (w + 1) * ROWS, :LANES] = re.astype(jnp.bfloat16)
            d_ref[g, w * ROWS : (w + 1) * ROWS, LANES:] = im.astype(jnp.bfloat16)


def adjoint_kernel(groups, fb, gg_ref, ug_ref, wg_ref, wu_ref, own_ref, other_ref, ra, rb, wexp, part):
    core = lax.axis_index("mp")
    db = 8
    per = db // 2
    for source, target in ((wg_ref, ra), (wu_ref, rb)):
        for upper in range(2):
            def read(o, at, source=source, upper=upper):
                o = upper * 8 + o
                if o >= fb:
                    return jnp.zeros((db, LANES), jnp.float32)
                return source[o, :, at : at + LANES].astype(jnp.float32)

            def write(g, ri, tile, rows, target=target, upper=upper):
                target[tile * 2 + upper, g * 2 * db + ri * db : g * 2 * db + (ri + 1) * db, :] = rows

            weight_rows(read, write, True, groups)
    mask = diagonal(LANES)
    span = 4 * LANES

    @pl.loop(0, groups)
    def _(g):
        for w, rows in enumerate((ra, rb)):
            for r in range(2 * db):
                for tile in range(4):
                    row = rows[tile, pl.ds(g * 2 * db + r, F, stride=0), :]
                    at = w * span + tile * LANES
                    wexp[r * F : (r + 1) * F, at : at + LANES] = jnp.where(mask, row, 0.0).astype(jnp.bfloat16)
        grads = jnp.concatenate([gg_ref[g].reshape(span, LANES), ug_ref[g].reshape(span, LANES)], axis=0)
        part[...] = jnp.dot(wexp[...], grads, preferred_element_type=jnp.float32).reshape(2, db, F, LANES)
        for ri in range(2):
            own_ref[g, ri] = part[ri, pl.ds(core * per, per)]
            other_ref[g, ri] = part[ri, pl.ds((1 - core) * per, per)].astype(jnp.bfloat16)


def input_kernel(own_ref, got_ref, qt_ref, out_ref):
    block = qt_ref.shape[0]
    for j in range(own_ref.shape[2]):
        spectrum = (own_ref[:, :, j] + got_ref[:, :, j].astype(jnp.float32)).astype(jnp.bfloat16)
        values = jnp.dot(qt_ref[...], spectrum.reshape(block, LANES), preferred_element_type=jnp.float32)
        out_ref[:, j * block : (j + 1) * block] = values.T.astype(jnp.bfloat16)


def reduce_kernel(r_ref, sum_ref, keep_ref, send_ref):
    core = lax.axis_index("mp")
    total = r_ref[0].astype(jnp.float32)
    for d in range(1, r_ref.shape[0]):
        total = total + r_ref[d].astype(jnp.float32)
    sum_ref[...] = total[:, : 2 * ROWS].astype(jnp.bfloat16)
    low = lax.broadcasted_iota(jnp.int32, (ROWS, LANES), 1) < LANES // 2
    for g in range(total.shape[0]):
        re, im = total[g, 2 * ROWS :, :LANES], total[g, 2 * ROWS :, LANES:]
        lower = jnp.where(low, re, pltpu.roll(im, LANES // 2, 1))
        upper = jnp.where(low, pltpu.roll(re, LANES // 2, 1), im)
        keep_ref[g] = jnp.where(core == 0, lower, upper).astype(jnp.bfloat16)
        send_ref[g] = jnp.where(core == 0, upper, lower).astype(jnp.bfloat16)


def layout_kernel(scale, fb, s_ref, a_ref, b_ref, gate_ref, up_ref, down_ref, flat):
    groups = s_ref.shape[0]
    half = groups * F
    for w, target in enumerate((gate_ref, up_ref)):
        for ri in range(2):
            for part in range(half // LANES):
                tiles = swap_blocks(
                    [
                        s_ref[part * 8 + i, w * ROWS : (w + 1) * ROWS, ri * LANES : (ri + 1) * LANES].astype(jnp.float32)
                        for i in range(8)
                    ]
                )
                at = ri * half + part * LANES
                for i in range(8):
                    flat[pl.ds(i, fb, stride=8), :] = tiles[i][:fb] * scale
                target[:, at : at + LANES] = flat[...]
    outputs = down_ref.shape[0]
    for h, source in enumerate((a_ref, b_ref)):
        for part in range(half // LANES):
            tiles = swap_blocks([source[part * 8 + i].astype(jnp.float32) for i in range(8)])
            for ri in range(2):
                at = ri * half + part * LANES
                for o in range(outputs):
                    down_ref[o, h * fb : (h + 1) * fb, at : at + LANES] = tiles[ri * outputs + o][:fb] * scale


def params(mib):
    return pltpu.CompilerParams(vmem_limit_bytes=mib << 20)


VMEM = pl.BlockSpec(memory_space=pltpu.VMEM)


def call(kernel, out_shape, args, scratch=(), mib=16, flops=0, moved=0):
    return pl.pallas_call(
        kernel,
        out_shape=out_shape,
        in_specs=[VMEM] * len(args),
        out_specs=jax.tree.map(lambda _: VMEM, out_shape),
        scratch_shapes=list(scratch),
        compiler_params=params(mib),
        cost_estimate=pl.CostEstimate(flops=flops, bytes_accessed=moved, transcendentals=0),
    )(*args)


def shards(tokens, cotangent, gate_spectra, up_spectra, down_spectra):
    n_dp = lax.axis_size("dp")
    core = lax.axis_index("mp")
    swap = [(0, 1), (1, 0)]
    fb, db, block = gate_spectra.shape
    assert db == 8 and fb <= ROWS and tokens.shape[0] == LANES and lax.axis_size("mp") == 2
    groups = block // 2 // F
    per = db // 2
    bf16, f32 = jnp.bfloat16, jnp.float32
    shape = jax.ShapeDtypeStruct
    pt, qt = transform_tables(block)

    tokens_other = lax.ppermute(tokens, "mp", swap)
    cotangent_other = lax.ppermute(cotangent, "mp", swap)
    down = down_spectra.reshape(per, 2, fb, block)
    down_own = jnp.where(core == 0, down[:, 0], down[:, 1])
    down_got = lax.ppermute(jnp.where(core == 0, down[:, 1], down[:, 0]), "mp", swap)
    down_all = jnp.where(
        core == 0, jnp.concatenate([down_own, down_got], 0), jnp.concatenate([down_got, down_own], 0)
    )
    wg = gate_spectra.reshape(fb * db, block)
    wu = up_spectra.reshape(fb * db, block)

    spec = shape((groups, 2, ROWS, F, LANES), bf16)
    d_all, gg, ug = call(
        functools.partial(main_kernel, groups, fb),
        (shape((groups, 3 * ROWS, 2 * LANES), bf16), spec, spec),
        (tokens, tokens_other, cotangent, cotangent_other, pt, qt, wg, wu, down_all),
        [pltpu.VMEM((groups, 2, db, F, LANES), bf16)] * 2
        + [pltpu.VMEM((fb, groups, 2, F, LANES), bf16)] * 3
        + [pltpu.VMEM(spec.shape, bf16)]
        + [pltpu.VMEM((2, groups * 2 * ROWS, LANES), f32)] * 3
        + [pltpu.VMEM((3 * 2 * fb * F, 2 * LANES), bf16), pltpu.VMEM((block // LANES, fb * db, LANES), f32)],
        mib=40,
        flops=10**10,
        moved=10**7,
    )

    if groups % n_dp == 0:
        share = groups // n_dp
        got = lax.all_to_all(d_all.reshape(n_dp, share, 3 * ROWS, 2 * LANES), "dp", 0, 0, tiled=True)
    else:
        share = groups
        got = lax.psum(d_all.astype(f32), "dp")[None]

    own, other = call(
        functools.partial(adjoint_kernel, groups, fb),
        (shape((groups, 2, per, F, LANES), f32), shape((groups, 2, per, F, LANES), bf16)),
        (gg, ug, gate_spectra, up_spectra),
        [pltpu.VMEM((4, groups * 2 * db, LANES), f32)] * 2
        + [pltpu.VMEM((2 * LANES, 8 * LANES), bf16), pltpu.VMEM((2, db, F, LANES), f32)],
        flops=2 * 10**9,
        moved=10**7,
    )
    partner = lax.ppermute(other, "mp", swap)
    grad_tokens = call(
        input_kernel, shape(tokens.shape, bf16), (own, partner, qt), flops=5 * 10**8, moved=4 * 10**6
    )

    total, keep, send = call(
        reduce_kernel,
        (
            shape((share, 2 * ROWS, 2 * LANES), bf16),
            shape((share, ROWS, LANES), bf16),
            shape((share, ROWS, LANES), bf16),
        ),
        (got,),
        moved=10**6,
    )
    partner_rows = lax.ppermute(send, "mp", swap)
    lower = jnp.where(core == 0, keep, partner_rows)
    upper = jnp.where(core == 0, partner_rows, keep)
    if groups % n_dp == 0:
        packed = jnp.concatenate([total, jnp.concatenate([lower, upper], axis=-1)], axis=1)
        every = jnp.broadcast_to(packed[None], (n_dp,) + packed.shape)
        packed = lax.all_to_all(every, "dp", 0, 0, tiled=True).reshape(groups, 3 * ROWS, 2 * LANES)
    else:
        packed = jnp.concatenate([total, jnp.concatenate([lower, upper], axis=-1)], axis=1)
    scale = 1.0 / math.sqrt(tokens.shape[0] * n_dp)
    gate_grad, up_grad, down_grad = call(
        functools.partial(layout_kernel, scale, fb),
        (shape((fb * db, block), f32), shape((fb * db, block), f32), shape((per, 2 * fb, block), f32)),
        (packed[:, : 2 * ROWS], packed[:, 2 * ROWS :, :LANES], packed[:, 2 * ROWS :, LANES:]),
        [pltpu.VMEM((fb * db, LANES), f32)],
        moved=10**6,
    )
    return (grad_tokens, gate_grad.reshape(fb, db, block), up_grad.reshape(fb, db, block), down_grad)


def solution(mesh):
    in_specs = (
        P(("groups", "dp"), "mp"),
        P(("groups", "dp"), "mp"),
        P("mp", None, None),
        P("mp", None, None),
        P("mp", None, None),
    )
    out_specs = (
        P(("groups", "dp"), "mp"),
        P(("groups", "mp"), None, None),
        P(("groups", "mp"), None, None),
        P(("groups", "mp"), None, None),
    )
    return jax.shard_map(shards, mesh=mesh, in_specs=in_specs, out_specs=out_specs, check_vma=False)
```

```python
import functools
import math

import jax
import jax.numpy as jnp
import numpy as np
from jax import lax
from jax.experimental import pallas as pl
from jax.experimental.pallas import tpu as pltpu
from jax.sharding import PartitionSpec as P

F = 16
LANES = 128
ROWS = 16


def transform_tables(block):
    half = block // 2
    n = np.arange(block)
    k = np.arange(half)
    angles = ((n[:, None] * k[None, :]) % block).astype(np.float32) * np.float32(2.0 * math.pi / block)
    cosine = np.cos(angles.astype(np.float64)).astype(np.float32)
    sine = np.sin(angles.astype(np.float64)).astype(np.float32)
    parity = (1 - 2 * (n % 2)).astype(np.float32)
    norm = np.float32(1.0 / math.sqrt(block))
    forward = np.concatenate([cosine, parity[:, None], -sine[:, 1:]], axis=1) * norm
    doubling = np.where(k >= 1, 2.0, 1.0).astype(np.float32)
    inverse = np.concatenate([(cosine * doubling).T, parity[None, :], -2.0 * sine[:, 1:].T], axis=0) * norm
    order = np.arange(block).reshape(2, half // F, F).transpose(1, 0, 2).reshape(-1)
    return (
        jnp.asarray(forward.T[order], jnp.bfloat16),
        jnp.asarray(inverse.T[:, order], jnp.bfloat16),
    )


def nt_dot(a, b):
    return lax.dot_general(a, b, (((1,), (1,)), ((), ())), preferred_element_type=jnp.float32)


def swap_blocks(tiles):
    tiles = list(tiles)
    lane_block = lax.broadcasted_iota(jnp.int32, tiles[0].shape, 1) // F
    step = len(tiles) // 2
    while step:
        high = (lane_block & step) != 0
        for i in range(len(tiles)):
            if i & step:
                continue
            low_tile, high_tile = tiles[i], tiles[i + step]
            tiles[i] = jnp.where(high, pltpu.roll(high_tile, F * step, 1), low_tile)
            tiles[i + step] = jnp.where(high, high_tile, pltpu.roll(low_tile, LANES - F * step, 1))
        step //= 2
    return tiles


def weight_rows(read, write, conj, groups):
    half = groups * F
    for part in range(half // LANES):
        at = part * LANES
        re = swap_blocks([read(i, at) for i in range(8)])
        im = swap_blocks([read(i, half + at) for i in range(8)])
        for i in range(8):
            g = part * 8 + i
            cross, wim = re[i], im[i]
            if g == 0:
                first = lax.broadcasted_iota(jnp.int32, wim.shape, 1) % F == 0
                cross = jnp.where(first, wim, cross)
                wim = jnp.where(first, 0.0, wim)
            sign = 1.0 if conj else -1.0
            write(g, 0, 0, re[i])
            write(g, 0, 1, sign * wim)
            write(g, 1, 0, -sign * wim)
            write(g, 1, 1, cross)


def diagonal(width):
    row = lax.broadcasted_iota(jnp.int32, (F, width), 0)
    lane = lax.broadcasted_iota(jnp.int32, (F, width), 1)
    return lane % F == row


def main_kernel(groups, fb, wg_in, wu_in, wd_in, pt_in, x_own_in, c_own_in, x_other_in, c_other_in, qt_in,
                d_ref, gg_out, ug_out, wg_ref, wu_ref, wd_ref, pt_ref, x_own, c_own, x_other, c_other, qt_ref,
                sx, sc, gs, us, hs, hid, gg_ref, ug_ref, rg, ru, rd, wexp, flat, in_sem, out_sem):
    core = lax.axis_index("mp")
    db = 8
    per = db // 2
    block = pt_ref.shape[0]
    pairs = (
        (wg_in, wg_ref), (wu_in, wu_ref), (wd_in, wd_ref), (pt_in, pt_ref), (x_own_in, x_own), (c_own_in, c_own),
        (x_other_in, x_other), (c_other_in, c_other), (qt_in, qt_ref),
    )
    copies = [pltpu.make_async_copy(src, dst, in_sem.at[n]) for n, (src, dst) in enumerate(pairs)]
    for copy in copies:
        copy.start()
    for copy in copies[:3]:
        copy.wait()

    for source, target in ((wg_ref, rg), (wu_ref, ru)):
        for tile in range(block // LANES):
            flat[tile] = source[:, tile * LANES : (tile + 1) * LANES].astype(jnp.float32)

        def read(i, at):
            return flat[at // LANES, pl.ds(i, fb, stride=db), :]

        def write(g, ri, tile, rows, target=target):
            target[tile, g * 2 * ROWS + ri * ROWS : g * 2 * ROWS + ri * ROWS + fb, :] = rows

        weight_rows(read, write, False, groups)

    def read_down(o, at):
        return wd_ref[o, :, at : at + LANES].astype(jnp.float32)

    def write_down(g, ri, tile, rows):
        rd[tile, g * 2 * ROWS + ri * ROWS : g * 2 * ROWS + ri * ROWS + fb, :] = rows

    weight_rows(read_down, write_down, True, groups)

    copies[3].wait()
    for half, first in enumerate((core * per, (1 - core) * per)):
        for u, (source, target) in enumerate((((x_own, x_other)[half], sx), ((c_own, c_other)[half], sc))):
            copies[4 + 2 * half + u].wait()
            for j in range(0, per, 2):
                pair = jnp.concatenate(
                    [source[:, j * block : (j + 1) * block], source[:, (j + 1) * block : (j + 2) * block]], axis=0
                )
                result = nt_dot(pt_ref[...], pair).astype(jnp.bfloat16)
                for u in range(2):
                    target[:, :, first + j + u] = result[:, u * LANES : (u + 1) * LANES].reshape(groups, 2, F, LANES)

    mask = diagonal(LANES)

    @pl.loop(0, groups)
    def _(g):
        for w, rows in enumerate((rg, ru, rd)):
            for ri in range(2):
                for o in range(fb):
                    at = ((w * 2 + ri) * fb + o) * F
                    for tile in range(2):
                        row = rows[tile, pl.ds(g * 2 * ROWS + ri * ROWS + o, F, stride=0), :]
                        wexp[at : at + F, tile * LANES : (tile + 1) * LANES] = jnp.where(mask, row, 0.0).astype(
                            jnp.bfloat16
                        )
        span = 2 * fb * F
        forward = jnp.dot(
            wexp[0 : 2 * span, :], sx[g].reshape(2 * LANES, LANES), preferred_element_type=jnp.float32
        ).astype(jnp.bfloat16)
        forward = forward.reshape(2, 2, fb, F, LANES)
        back = jnp.dot(
            wexp[2 * span : 3 * span, :], sc[g].reshape(2 * LANES, LANES), preferred_element_type=jnp.float32
        ).astype(jnp.bfloat16)
        back = back.reshape(2, fb, F, LANES)
        for ri in range(2):
            gs[:, g, ri] = forward[0, ri]
            us[:, g, ri] = forward[1, ri]
            hs[:, g, ri] = back[ri]

    copies[8].wait()
    for target in (gg_ref, ug_ref, hid):
        target[:, :, fb:] = jnp.zeros((groups, 2, ROWS - fb, F, LANES), jnp.bfloat16)

    @pl.loop(0, fb)
    def _(o):
        spectra = jnp.concatenate([ref[o].reshape(block, LANES) for ref in (gs, us, hs)], axis=1)
        values = jnp.dot(qt_ref[...], spectra, preferred_element_type=jnp.float32)
        gate, up, grad = (values[:, u * LANES : (u + 1) * LANES] for u in range(3))
        sig = 1.0 / (1.0 + jnp.exp(-gate))
        gated = gate * sig
        hidden = (gated * up).astype(jnp.bfloat16)
        gate_grad = (grad * up * sig * (1.0 + gate * (1.0 - sig))).astype(jnp.bfloat16)
        up_grad = (grad * gated).astype(jnp.bfloat16)
        result = jnp.dot(
            pt_ref[...], jnp.concatenate([hidden, gate_grad, up_grad], axis=1), preferred_element_type=jnp.float32
        ).astype(jnp.bfloat16)
        for u, target in enumerate((hid, gg_ref, ug_ref)):
            target[:, :, o] = result[:, u * LANES : (u + 1) * LANES].reshape(groups, 2, F, LANES)

    stores = [
        pltpu.make_async_copy(src, dst, out_sem.at[n]) for n, (src, dst) in enumerate(((gg_ref, gg_out), (ug_ref, ug_out)))
    ]
    for copy in stores:
        copy.start()
    keep = diagonal(LANES)
    lane = lax.broadcasted_iota(jnp.int32, (F, LANES), 1)
    row = lax.broadcasted_iota(jnp.int32, (F, LANES), 0)

    @pl.loop(0, groups)
    def _(g):
        first = (lane % F == 0) & (row == 0) & (g == 0)
        weight = jnp.where(keep, jnp.where(first, 1.0, 2.0), 0.0)
        weight_pair = jnp.where(first, 0.0, weight)
        weight_first = jnp.where(first, 1.0, 0.0)
        span = 2 * ROWS * F
        for w, (rows, cols, sign) in enumerate(((gg_ref, sx, 1.0), (ug_ref, sx, 1.0), (hid, sc, -1.0))):
            m = nt_dot(rows[g].reshape(span, LANES), cols[g].reshape(2 * LANES, LANES)).reshape(2, ROWS, F, 2 * LANES)
            rr, ri = m[0, :, :, :LANES], m[0, :, :, LANES:]
            ir, ii = m[1, :, :, :LANES], m[1, :, :, LANES:]
            re = jnp.sum(rr * weight + ii * weight_pair, axis=1)
            im = jnp.sum((ir - ri) * (sign * weight_pair) + ii * weight_first, axis=1)
            d_ref[g, w * ROWS : (w + 1) * ROWS, :LANES] = re.astype(jnp.bfloat16)
            d_ref[g, w * ROWS : (w + 1) * ROWS, LANES:] = im.astype(jnp.bfloat16)

    for copy in stores:
        copy.wait()


def adjoint_kernel(groups, fb, wg_in, wu_in, gg_in, ug_in, own_ref, other_ref, wg_ref, wu_ref, gg_ref, ug_ref,
                   ra, rb, wexp, part, in_sem, g_sem):
    core = lax.axis_index("mp")
    db = 8
    per = db // 2
    weights = [
        pltpu.make_async_copy(src, dst, in_sem.at[n]) for n, (src, dst) in enumerate(((wg_in, wg_ref), (wu_in, wu_ref)))
    ]

    def group_copies(g):
        return [
            pltpu.make_async_copy(src.at[g], dst.at[g], g_sem.at[n, g])
            for n, (src, dst) in enumerate(((gg_in, gg_ref), (ug_in, ug_ref)))
        ]

    for copy in weights:
        copy.start()
    for g in range(groups):
        for copy in group_copies(g):
            copy.start()
    for copy in weights:
        copy.wait()
    for source, target in ((wg_ref, ra), (wu_ref, rb)):
        for upper in range(2):
            def read(o, at, source=source, upper=upper):
                o = upper * 8 + o
                if o >= fb:
                    return jnp.zeros((db, LANES), jnp.float32)
                return source[o, :, at : at + LANES].astype(jnp.float32)

            def write(g, ri, tile, rows, target=target, upper=upper):
                target[tile * 2 + upper, g * 2 * db + ri * db : g * 2 * db + (ri + 1) * db, :] = rows

            weight_rows(read, write, True, groups)
    mask = diagonal(LANES)
    span = 4 * LANES

    @pl.loop(0, groups)
    def _(g):
        for w, rows in enumerate((ra, rb)):
            for r in range(2 * db):
                for tile in range(4):
                    row = rows[tile, pl.ds(g * 2 * db + r, F, stride=0), :]
                    at = w * span + tile * LANES
                    wexp[r * F : (r + 1) * F, at : at + LANES] = jnp.where(mask, row, 0.0).astype(jnp.bfloat16)
        for copy in group_copies(g):
            copy.wait()
        grads = jnp.concatenate([gg_ref[g].reshape(span, LANES), ug_ref[g].reshape(span, LANES)], axis=0)
        part[...] = jnp.dot(wexp[...], grads, preferred_element_type=jnp.float32).reshape(2, db, F, LANES)
        for ri in range(2):
            own_ref[g, ri] = part[ri, pl.ds(core * per, per)]
            other_ref[g, ri] = part[ri, pl.ds((1 - core) * per, per)].astype(jnp.bfloat16)


def input_kernel(own_ref, got_ref, qt_ref, out_ref):
    block = qt_ref.shape[0]
    for j in range(own_ref.shape[2]):
        spectrum = (own_ref[:, :, j] + got_ref[:, :, j].astype(jnp.float32)).astype(jnp.bfloat16)
        values = jnp.dot(qt_ref[...], spectrum.reshape(block, LANES), preferred_element_type=jnp.float32)
        out_ref[:, j * block : (j + 1) * block] = values.T.astype(jnp.bfloat16)


def reduce_kernel(r_ref, out_ref):
    total = r_ref[0].astype(jnp.float32)
    for d in range(1, r_ref.shape[0]):
        total = total + r_ref[d].astype(jnp.float32)
    total = total.astype(jnp.bfloat16)
    for d in range(out_ref.shape[0]):
        out_ref[d] = total


def pack_kernel(s_ref, keep_ref, send_ref):
    core = lax.axis_index("mp")
    low = lax.broadcasted_iota(jnp.int32, (ROWS, LANES), 1) < LANES // 2
    for g in range(s_ref.shape[0]):
        re = s_ref[g, 2 * ROWS :, :LANES].astype(jnp.float32)
        im = s_ref[g, 2 * ROWS :, LANES:].astype(jnp.float32)
        lower = jnp.where(low, re, pltpu.roll(im, LANES // 2, 1))
        upper = jnp.where(low, pltpu.roll(re, LANES // 2, 1), im)
        keep_ref[g] = jnp.where(core == 0, lower, upper).astype(jnp.bfloat16)
        send_ref[g] = jnp.where(core == 0, upper, lower).astype(jnp.bfloat16)


def layout_kernel(scale, fb, s_ref, gate_ref, up_ref, flat):
    half = s_ref.shape[0] * F
    for w, target in enumerate((gate_ref, up_ref)):
        for ri in range(2):
            for part in range(half // LANES):
                tiles = swap_blocks(
                    [
                        s_ref[part * 8 + i, w * ROWS : (w + 1) * ROWS, ri * LANES : (ri + 1) * LANES].astype(jnp.float32)
                        for i in range(8)
                    ]
                )
                at = ri * half + part * LANES
                for i in range(8):
                    flat[pl.ds(i, fb, stride=8), :] = tiles[i][:fb] * scale
                target[:, at : at + LANES] = flat[...]


def down_layout_kernel(scale, fb, keep_ref, got_ref, down_ref):
    core = lax.axis_index("mp")
    half = keep_ref.shape[0] * F
    outputs = down_ref.shape[1]
    for source, h in ((keep_ref, core), (got_ref, 1 - core)):
        for part in range(half // LANES):
            tiles = swap_blocks([source[part * 8 + i].astype(jnp.float32) for i in range(8)])
            for ri in range(2):
                at = ri * half + part * LANES
                for o in range(outputs):
                    down_ref[pl.ds(h * fb, fb), o, at : at + LANES] = tiles[ri * outputs + o][:fb] * scale


def params(mib):
    return pltpu.CompilerParams(vmem_limit_bytes=mib << 20)


VMEM = pl.BlockSpec(memory_space=pltpu.VMEM)
HBM = pl.BlockSpec(memory_space=pltpu.HBM)


def call(kernel, out_shape, args, scratch=(), mib=16, flops=0, moved=0, in_specs=None, out_specs=None):
    return pl.pallas_call(
        kernel,
        out_shape=out_shape,
        in_specs=in_specs or [VMEM] * len(args),
        out_specs=out_specs or jax.tree.map(lambda _: VMEM, out_shape),
        scratch_shapes=list(scratch),
        compiler_params=params(mib),
        cost_estimate=pl.CostEstimate(flops=flops, bytes_accessed=moved, transcendentals=0),
    )(*args)


def shards(tokens, cotangent, gate_spectra, up_spectra, down_spectra):
    n_dp = lax.axis_size("dp")
    core = lax.axis_index("mp")
    swap = [(0, 1), (1, 0)]
    fb, db, block = gate_spectra.shape
    assert db == 8 and fb <= ROWS and tokens.shape[0] == LANES and lax.axis_size("mp") == 2
    groups = block // 2 // F
    per = db // 2
    bf16, f32 = jnp.bfloat16, jnp.float32
    shape = jax.ShapeDtypeStruct
    pt, qt = transform_tables(block)

    tokens_other = lax.ppermute(tokens, "mp", swap)
    cotangent_other = lax.ppermute(cotangent, "mp", swap)
    down = down_spectra.reshape(per, 2, fb, block)
    down_own = jnp.where(core == 0, down[:, 0], down[:, 1])
    down_got = lax.ppermute(jnp.where(core == 0, down[:, 1], down[:, 0]), "mp", swap)
    down_all = jnp.where(
        core == 0, jnp.concatenate([down_own, down_got], 0), jnp.concatenate([down_got, down_own], 0)
    )
    wg = gate_spectra.reshape(fb * db, block)
    wu = up_spectra.reshape(fb * db, block)

    spec = shape((groups, 2, ROWS, F, LANES), bf16)
    inputs = (wg, wu, down_all, pt, tokens, cotangent, tokens_other, cotangent_other, qt)
    d_all, gg, ug = call(
        functools.partial(main_kernel, groups, fb),
        (shape((groups, 3 * ROWS, 2 * LANES), bf16), spec, spec),
        inputs,
        [pltpu.VMEM(a.shape, a.dtype) for a in inputs]
        + [pltpu.VMEM((groups, 2, db, F, LANES), bf16)] * 2
        + [pltpu.VMEM((fb, groups, 2, F, LANES), bf16)] * 3
        + [pltpu.VMEM(spec.shape, bf16)] * 3
        + [pltpu.VMEM((2, groups * 2 * ROWS, LANES), f32)] * 3
        + [pltpu.VMEM((3 * 2 * fb * F, 2 * LANES), bf16), pltpu.VMEM((block // LANES, fb * db, LANES), f32)]
        + [pltpu.SemaphoreType.DMA((len(inputs),)), pltpu.SemaphoreType.DMA((2,))],
        mib=63,
        flops=10**10,
        moved=10**7,
        in_specs=[HBM] * len(inputs),
        out_specs=(VMEM, HBM, HBM),
    )

    direct = groups % n_dp == 0
    if direct:
        share = groups // n_dp
        got = lax.all_to_all(d_all.reshape(n_dp, share, 3 * ROWS, 2 * LANES), "dp", 0, 0, tiled=True)
    else:
        share = groups
        got = lax.psum(d_all.astype(f32), "dp")[None]

    own, other = call(
        functools.partial(adjoint_kernel, groups, fb),
        (shape((groups, 2, per, F, LANES), f32), shape((groups, 2, per, F, LANES), bf16)),
        (gate_spectra, up_spectra, gg, ug),
        [pltpu.VMEM(gate_spectra.shape, bf16)] * 2
        + [pltpu.VMEM(spec.shape, bf16)] * 2
        + [pltpu.VMEM((4, groups * 2 * db, LANES), f32)] * 2
        + [pltpu.VMEM((2 * LANES, 8 * LANES), bf16), pltpu.VMEM((2, db, F, LANES), f32)]
        + [pltpu.SemaphoreType.DMA((2,)), pltpu.SemaphoreType.DMA((2, groups))],
        mib=63,
        flops=2 * 10**9,
        moved=10**7,
        in_specs=[HBM] * 4,
    )
    total = call(reduce_kernel, shape((n_dp if direct else 1, share, 3 * ROWS, 2 * LANES), bf16), (got,), moved=10**6)
    total, own, other = lax.optimization_barrier((total, own, other))
    partner = lax.ppermute(other, "mp", swap)
    grad_tokens = call(
        input_kernel, shape(tokens.shape, bf16), (own, partner, qt), flops=5 * 10**8, moved=4 * 10**6
    )
    if direct:
        total = lax.all_to_all(total, "dp", 0, 0, tiled=True)
    total = total.reshape(groups, 3 * ROWS, 2 * LANES)
    keep, send = call(pack_kernel, (shape((groups, ROWS, LANES), bf16),) * 2, (total,), moved=10**5)
    partner_rows = lax.ppermute(send, "mp", swap)
    scale = 1.0 / math.sqrt(tokens.shape[0] * n_dp)
    gate_grad, up_grad = call(
        functools.partial(layout_kernel, scale, fb),
        (shape((fb * db, block), f32),) * 2,
        (total,),
        [pltpu.VMEM((fb * db, LANES), f32)],
        moved=10**6,
    )
    down_grad = call(
        functools.partial(down_layout_kernel, scale, fb),
        shape((2 * fb, per, block), f32),
        (keep, partner_rows),
        moved=10**6,
    ).transpose(1, 0, 2)
    return (grad_tokens, gate_grad.reshape(fb, db, block), up_grad.reshape(fb, db, block), down_grad)


def solution(mesh):
    in_specs = (
        P(("groups", "dp"), "mp"),
        P(("groups", "dp"), "mp"),
        P("mp", None, None),
        P("mp", None, None),
        P("mp", None, None),
    )
    out_specs = (
        P(("groups", "dp"), "mp"),
        P(("groups", "mp"), None, None),
        P(("groups", "mp"), None, None),
        P(("groups", "mp"), None, None),
    )
    return jax.shard_map(shards, mesh=mesh, in_specs=in_specs, out_specs=out_specs, check_vma=False)
```

```python
import functools
import math

import jax
import jax.numpy as jnp
import numpy as np
from jax import lax
from jax.experimental import pallas as pl
from jax.experimental.pallas import tpu as pltpu
from jax.sharding import PartitionSpec as P

F = 16
LANES = 128
ROWS = 16


def transform_tables(block):
    half = block // 2
    n = np.arange(block)
    k = np.arange(half)
    angles = ((n[:, None] * k[None, :]) % block).astype(np.float32) * np.float32(2.0 * math.pi / block)
    cosine = np.cos(angles.astype(np.float64)).astype(np.float32)
    sine = np.sin(angles.astype(np.float64)).astype(np.float32)
    parity = (1 - 2 * (n % 2)).astype(np.float32)
    norm = np.float32(1.0 / math.sqrt(block))
    forward = np.concatenate([cosine, parity[:, None], -sine[:, 1:]], axis=1) * norm
    doubling = np.where(k >= 1, 2.0, 1.0).astype(np.float32)
    inverse = np.concatenate([(cosine * doubling).T, parity[None, :], -2.0 * sine[:, 1:].T], axis=0) * norm
    order = np.arange(block).reshape(2, half // F, F).transpose(1, 0, 2).reshape(-1)
    return (
        jnp.asarray(forward.T[order], jnp.bfloat16),
        jnp.asarray(inverse.T[:, order], jnp.bfloat16),
    )


def nt_dot(a, b):
    return lax.dot_general(a, b, (((1,), (1,)), ((), ())), preferred_element_type=jnp.float32)


def swap_blocks(tiles):
    tiles = list(tiles)
    lane_block = lax.broadcasted_iota(jnp.int32, tiles[0].shape, 1) // F
    step = len(tiles) // 2
    while step:
        high = (lane_block & step) != 0
        for i in range(len(tiles)):
            if i & step:
                continue
            low_tile, high_tile = tiles[i], tiles[i + step]
            tiles[i] = jnp.where(high, pltpu.roll(high_tile, F * step, 1), low_tile)
            tiles[i + step] = jnp.where(high, high_tile, pltpu.roll(low_tile, LANES - F * step, 1))
        step //= 2
    return tiles


def weight_rows(read, write, conj, groups):
    half = groups * F
    for part in range(half // LANES):
        at = part * LANES
        re = swap_blocks([read(i, at) for i in range(8)])
        im = swap_blocks([read(i, half + at) for i in range(8)])
        for i in range(8):
            g = part * 8 + i
            cross, wim = re[i], im[i]
            if g == 0:
                first = lax.broadcasted_iota(jnp.int32, wim.shape, 1) % F == 0
                cross = jnp.where(first, wim, cross)
                wim = jnp.where(first, 0.0, wim)
            sign = 1.0 if conj else -1.0
            write(g, 0, 0, re[i])
            write(g, 0, 1, sign * wim)
            write(g, 1, 0, -sign * wim)
            write(g, 1, 1, cross)


def diagonal():
    row = lax.broadcasted_iota(jnp.int32, (F, LANES), 0)
    lane = lax.broadcasted_iota(jnp.int32, (F, LANES), 1)
    return jnp.where(lane % F == row, 1.0, 0.0).astype(jnp.bfloat16)


def spread(rows, tiles, base, count, mask):
    return jnp.concatenate(
        [
            jnp.concatenate(
                [rows[tile, pl.ds(base + r, F, stride=0), :].astype(jnp.bfloat16) * mask for tile in range(tiles)],
                axis=1,
            )
            for r in range(count)
        ],
        axis=0,
    )


def main_kernel(groups, fb, wg_in, wu_in, pt_in, x_own_in, c_own_in, wd_own_in, wd_other_in, x_other_in, c_other_in,
                qt_in, d_ref, gg_out, ug_out, wg_ref, wu_ref, pt_ref, x_own, c_own, wd_ref, x_other, c_other, qt_ref,
                sx, sc, gs, us, hs, hid, gg_ref, ug_ref, rg, ru, rd, flat, in_sem, out_sem):
    core = lax.axis_index("mp")
    db = 8
    per = db // 2
    block = pt_ref.shape[0]
    pairs = (
        (wg_in, wg_ref), (wu_in, wu_ref), (pt_in, pt_ref), (x_own_in, x_own), (c_own_in, c_own),
        (wd_own_in, wd_ref.at[pl.ds(core * per, per)]), (wd_other_in, wd_ref.at[pl.ds((1 - core) * per, per)]),
        (x_other_in, x_other), (c_other_in, c_other), (qt_in, qt_ref),
    )
    copies = [pltpu.make_async_copy(src, dst, in_sem.at[n]) for n, (src, dst) in enumerate(pairs)]
    for copy in copies:
        copy.start()

    def to_spectra(source, target, first):
        for j in range(0, per, 2):
            pair = jnp.concatenate(
                [source[:, j * block : (j + 1) * block], source[:, (j + 1) * block : (j + 2) * block]], axis=0
            )
            result = nt_dot(pt_ref[...], pair).astype(jnp.bfloat16)
            for u in range(2):
                target[:, :, first + j + u] = result[:, u * LANES : (u + 1) * LANES].reshape(groups, 2, F, LANES)

    for copy in copies[:5]:
        copy.wait()
    to_spectra(x_own, sx, core * per)
    to_spectra(c_own, sc, core * per)
    for n, (source, target) in enumerate(((wg_ref, rg), (wu_ref, ru))):
        for tile in range(block // LANES):
            flat[n, tile] = source[:, tile * LANES : (tile + 1) * LANES].astype(jnp.float32)

        def read(i, at, n=n):
            return flat[n, at // LANES, pl.ds(i, fb, stride=db), :]

        def write(g, ri, tile, rows, target=target):
            target[tile, g * 2 * ROWS + ri * ROWS : g * 2 * ROWS + ri * ROWS + fb, :] = rows

        weight_rows(read, write, False, groups)

    for copy in copies[5:9]:
        copy.wait()
    to_spectra(x_other, sx, (1 - core) * per)
    to_spectra(c_other, sc, (1 - core) * per)

    def read_down(o, at):
        return wd_ref[o, :, at : at + LANES].astype(jnp.float32)

    def write_down(g, ri, tile, rows):
        rd[tile, g * 2 * ROWS + ri * ROWS : g * 2 * ROWS + ri * ROWS + fb, :] = rows

    weight_rows(read_down, write_down, True, groups)
    for target in (gg_ref, ug_ref):
        target[:, :, fb:] = jnp.zeros((groups, 2, ROWS - fb, F, LANES), jnp.bfloat16)

    mask = diagonal()
    span = fb * F

    @pl.loop(0, groups)
    def _(g):
        for rows, source, target in ((rg, sx, gs), (ru, sx, us), (rd, sc, hs)):
            spectrum = source[g].reshape(2 * LANES, LANES)
            for ri in range(2):
                result = jnp.dot(
                    spread(rows, 2, g * 2 * ROWS + ri * ROWS, fb, mask), spectrum, preferred_element_type=jnp.float32
                )
                target[:, g, ri] = result.astype(jnp.bfloat16).reshape(fb, F, LANES)

    copies[9].wait()

    @pl.loop(0, fb // 2)
    def _(pair):
        spectra = jnp.concatenate(
            [ref[2 * pair + u].reshape(block, LANES) for u in range(2) for ref in (gs, us, hs)], axis=1
        )
        values = jnp.dot(qt_ref[...], spectra, preferred_element_type=jnp.float32)
        sides = []
        for u in range(2):
            gate, up, grad = (values[:, (3 * u + v) * LANES : (3 * u + v + 1) * LANES] for v in range(3))
            sig = 1.0 / (1.0 + jnp.exp(-gate))
            gated = gate * sig
            sides.append((gated * up).astype(jnp.bfloat16))
            sides.append((grad * up * sig * (1.0 + gate * (1.0 - sig))).astype(jnp.bfloat16))
            sides.append((grad * gated).astype(jnp.bfloat16))
        result = jnp.dot(pt_ref[...], jnp.concatenate(sides, axis=1), preferred_element_type=jnp.float32)
        result = result.astype(jnp.bfloat16)
        for u in range(2):
            for v, target in enumerate((hid, gg_ref, ug_ref)):
                at = (3 * u + v) * LANES
                target[:, :, 2 * pair + u] = result[:, at : at + LANES].reshape(groups, 2, F, LANES)

    stores = [
        pltpu.make_async_copy(src, dst, out_sem.at[n]) for n, (src, dst) in enumerate(((gg_ref, gg_out), (ug_ref, ug_out)))
    ]
    for copy in stores:
        copy.start()
    lane = lax.broadcasted_iota(jnp.int32, (8, LANES), 1)
    row = lax.broadcasted_iota(jnp.int32, (8, LANES), 0)
    low = lane % F < 8

    @pl.loop(0, groups)
    def _(g):
        first = (lane % F == 0) & (g == 0)
        for w, (rows, cols, sign) in enumerate(((gg_ref, sx, 1), (ug_ref, sx, 1), (hid, sc, -1))):
            m = nt_dot(rows[g, :, :fb].reshape(2 * span, LANES), cols[g].reshape(2 * LANES, LANES))
            re, im = [], []
            for upper in range(0, fb, 8):
                re_tile = jnp.zeros((8, LANES), jnp.float32)
                im_tile = jnp.zeros((8, LANES), jnp.float32)
                for o in range(upper, min(upper + 8, fb)):
                    def part(a, b, o=o, m=m):
                        at = a * span + o * F
                        lanes = slice(b * LANES, (b + 1) * LANES)
                        return jnp.where(low, m[at : at + 8, lanes], m[at + 8 : at + F, lanes])

                    rr, ri, ir, ii = part(0, 0), part(0, 1), part(1, 0), part(1, 1)
                    cross = ir - ri if sign > 0 else ri - ir
                    turn = o - upper
                    here = (row - lane) % 8 == turn
                    both = rr + jnp.where(first, 0.0, ii)
                    cross = jnp.where(first, ii, cross)
                    if turn:
                        both, cross = pltpu.roll(both, turn, 0), pltpu.roll(cross, turn, 0)
                    re_tile = jnp.where(here, both, re_tile)
                    im_tile = jnp.where(here, cross, im_tile)
                re.append(re_tile)
                im.append(im_tile)
            d_ref[g, w * ROWS : (w + 1) * ROWS, :LANES] = jnp.concatenate(re, axis=0).astype(jnp.bfloat16)
            d_ref[g, w * ROWS : (w + 1) * ROWS, LANES:] = jnp.concatenate(im, axis=0).astype(jnp.bfloat16)

    for copy in stores:
        copy.wait()


def straight(tile):
    halves = []
    lane = lax.broadcasted_iota(jnp.int32, (8, LANES), 1)
    for at in range(0, tile.shape[0], 8):
        half = tile[at : at + 8]
        for bit in (1, 2, 4):
            half = jnp.where((lane & bit) != 0, pltpu.roll(half, 8 - bit, 0), half)
        halves.append(half)
    return jnp.concatenate(halves, axis=0)


def factor(scale, part):
    lane = lax.broadcasted_iota(jnp.int32, (1, LANES), 1)
    return jnp.where((lane == 0) & (part == 0), scale, 2.0 * scale)


def adjoint_kernel(groups, fb, wg_in, wu_in, gg_in, ug_in, own_ref, other_ref, wg_ref, wu_ref, gg_ref, ug_ref,
                   ra, rb, part, in_sem, g_sem):
    core = lax.axis_index("mp")
    db = 8
    per = db // 2
    weights = [
        pltpu.make_async_copy(src, dst, in_sem.at[n]) for n, (src, dst) in enumerate(((wg_in, wg_ref), (wu_in, wu_ref)))
    ]

    def group_copies(g):
        return [
            pltpu.make_async_copy(src.at[g], dst.at[g], g_sem.at[n, g])
            for n, (src, dst) in enumerate(((gg_in, gg_ref), (ug_in, ug_ref)))
        ]

    for copy in weights:
        copy.start()
    for g in range(groups):
        for copy in group_copies(g):
            copy.start()
    for copy in weights:
        copy.wait()
    for source, target in ((wg_ref, ra), (wu_ref, rb)):
        for upper in range(2):
            def read(o, at, source=source, upper=upper):
                o = upper * 8 + o
                if o >= fb:
                    return jnp.zeros((db, LANES), jnp.float32)
                return source[o, :, at : at + LANES].astype(jnp.float32)

            def write(g, ri, tile, rows, target=target, upper=upper):
                target[tile * 2 + upper, g * 2 * db + ri * db : g * 2 * db + (ri + 1) * db, :] = rows

            weight_rows(read, write, True, groups)
    mask = diagonal()
    span = 4 * LANES

    @pl.loop(0, groups)
    def _(g):
        for copy in group_copies(g):
            copy.wait()
        rows = jnp.concatenate([spread(ref, 4, g * 2 * db, 2 * db, mask) for ref in (ra, rb)], axis=1)
        grads = jnp.concatenate([gg_ref[g].reshape(span, LANES), ug_ref[g].reshape(span, LANES)], axis=0)
        part[...] = jnp.dot(rows, grads, preferred_element_type=jnp.float32).reshape(2, db, F, LANES)
        for ri in range(2):
            own_ref[g, ri] = part[ri, pl.ds(core * per, per)]
            other_ref[g, ri] = part[ri, pl.ds((1 - core) * per, per)].astype(jnp.bfloat16)


def input_kernel(own_ref, got_ref, qt_ref, out_ref):
    block = qt_ref.shape[0]
    for j in range(own_ref.shape[2]):
        spectrum = (own_ref[:, :, j] + got_ref[:, :, j].astype(jnp.float32)).astype(jnp.bfloat16)
        values = jnp.dot(qt_ref[...], spectrum.reshape(block, LANES), preferred_element_type=jnp.float32)
        out_ref[:, j * block : (j + 1) * block] = values.T.astype(jnp.bfloat16)


def reduce_kernel(r_ref, out_ref):
    total = r_ref[0].astype(jnp.float32)
    for d in range(1, r_ref.shape[0]):
        total = total + r_ref[d].astype(jnp.float32)
    total = total.astype(jnp.bfloat16)
    for d in range(out_ref.shape[0]):
        out_ref[d] = total


def pack_kernel(s_ref, keep_ref, send_ref):
    core = lax.axis_index("mp")
    low = lax.broadcasted_iota(jnp.int32, (ROWS, LANES), 1) < LANES // 2
    for g in range(s_ref.shape[0]):
        re = s_ref[g, 2 * ROWS :, :LANES].astype(jnp.float32)
        im = s_ref[g, 2 * ROWS :, LANES:].astype(jnp.float32)
        lower = jnp.where(low, re, pltpu.roll(im, LANES // 2, 1))
        upper = jnp.where(low, pltpu.roll(re, LANES // 2, 1), im)
        keep_ref[g] = jnp.where(core == 0, lower, upper).astype(jnp.bfloat16)
        send_ref[g] = jnp.where(core == 0, upper, lower).astype(jnp.bfloat16)


def layout_kernel(scale, fb, s_ref, gate_ref, up_ref, flat):
    half = s_ref.shape[0] * F
    for w, target in enumerate((gate_ref, up_ref)):
        for ri in range(2):
            for part in range(half // LANES):
                tiles = swap_blocks(
                    [
                        straight(
                            s_ref[part * 8 + i, w * ROWS : (w + 1) * ROWS, ri * LANES : (ri + 1) * LANES].astype(
                                jnp.float32
                            )
                        )
                        for i in range(8)
                    ]
                )
                at = ri * half + part * LANES
                for i in range(8):
                    flat[pl.ds(i, fb, stride=8), :] = tiles[i][:fb] * factor(scale, part)
                target[:, at : at + LANES] = flat[...]


def down_layout_kernel(scale, fb, keep_ref, got_ref, down_ref):
    core = lax.axis_index("mp")
    half = keep_ref.shape[0] * F
    outputs = down_ref.shape[1]
    for source, h in ((keep_ref, core), (got_ref, 1 - core)):
        for part in range(half // LANES):
            tiles = swap_blocks([straight(source[part * 8 + i].astype(jnp.float32)) for i in range(8)])
            for ri in range(2):
                at = ri * half + part * LANES
                for o in range(outputs):
                    down_ref[pl.ds(h * fb, fb), o, at : at + LANES] = tiles[ri * outputs + o][:fb] * factor(
                        scale, part
                    )


def params(mib):
    return pltpu.CompilerParams(vmem_limit_bytes=mib << 20)


VMEM = pl.BlockSpec(memory_space=pltpu.VMEM)
HBM = pl.BlockSpec(memory_space=pltpu.HBM)


def call(kernel, out_shape, args, scratch=(), mib=16, flops=0, moved=0, in_specs=None, out_specs=None):
    return pl.pallas_call(
        kernel,
        out_shape=out_shape,
        in_specs=in_specs or [VMEM] * len(args),
        out_specs=out_specs or jax.tree.map(lambda _: VMEM, out_shape),
        scratch_shapes=list(scratch),
        compiler_params=params(mib),
        cost_estimate=pl.CostEstimate(flops=flops, bytes_accessed=moved, transcendentals=0),
    )(*args)


def shards(tokens, cotangent, gate_spectra, up_spectra, down_spectra):
    n_dp = lax.axis_size("dp")
    core = lax.axis_index("mp")
    swap = [(0, 1), (1, 0)]
    fb, db, block = gate_spectra.shape
    assert db == 8 and fb <= ROWS and fb % 2 == 0 and tokens.shape[0] == LANES and lax.axis_size("mp") == 2
    groups = block // 2 // F
    per = db // 2
    bf16, f32 = jnp.bfloat16, jnp.float32
    shape = jax.ShapeDtypeStruct
    pt, qt = transform_tables(block)

    tokens_other = lax.ppermute(tokens, "mp", swap)
    cotangent_other = lax.ppermute(cotangent, "mp", swap)
    down = down_spectra.reshape(per, 2, fb, block)
    down_own = jnp.where(core == 0, down[:, 0], down[:, 1])
    down_got = lax.ppermute(jnp.where(core == 0, down[:, 1], down[:, 0]), "mp", swap)
    wg = gate_spectra.reshape(fb * db, block)
    wu = up_spectra.reshape(fb * db, block)

    spec = shape((groups, 2, ROWS, F, LANES), bf16)
    inputs = (wg, wu, pt, tokens, cotangent, down_own, down_got, tokens_other, cotangent_other, qt)
    buffers = [shape(a.shape, bf16) for a in (wg, wu, pt, tokens, cotangent)]
    buffers += [shape((db, fb, block), bf16)] + [shape(a.shape, bf16) for a in (tokens_other, cotangent_other, qt)]
    d_all, gg, ug = call(
        functools.partial(main_kernel, groups, fb),
        (shape((groups, 3 * ROWS, 2 * LANES), bf16), spec, spec),
        inputs,
        [pltpu.VMEM(a.shape, a.dtype) for a in buffers]
        + [pltpu.VMEM((groups, 2, db, F, LANES), bf16)] * 2
        + [pltpu.VMEM((fb, groups, 2, F, LANES), bf16)] * 3
        + [pltpu.VMEM(spec.shape, bf16)] * 3
        + [pltpu.VMEM((2, groups * 2 * ROWS, LANES), f32)] * 3
        + [pltpu.VMEM((2, block // LANES, fb * db, LANES), f32)]
        + [pltpu.SemaphoreType.DMA((len(inputs),)), pltpu.SemaphoreType.DMA((2,))],
        mib=63,
        flops=10**10,
        moved=10**7,
        in_specs=[HBM] * len(inputs),
        out_specs=(VMEM, HBM, HBM),
    )

    direct = groups % n_dp == 0
    if direct:
        share = groups // n_dp
        got = lax.all_to_all(d_all.reshape(n_dp, share, 3 * ROWS, 2 * LANES), "dp", 0, 0, tiled=True)
    else:
        share = groups
        got = lax.psum(d_all.astype(f32), "dp")[None]

    own, other = call(
        functools.partial(adjoint_kernel, groups, fb),
        (shape((groups, 2, per, F, LANES), f32), shape((groups, 2, per, F, LANES), bf16)),
        (gate_spectra, up_spectra, gg, ug),
        [pltpu.VMEM(gate_spectra.shape, bf16)] * 2
        + [pltpu.VMEM(spec.shape, bf16)] * 2
        + [pltpu.VMEM((4, groups * 2 * db, LANES), f32)] * 2
        + [pltpu.VMEM((2, db, F, LANES), f32)]
        + [pltpu.SemaphoreType.DMA((2,)), pltpu.SemaphoreType.DMA((2, groups))],
        mib=63,
        flops=2 * 10**9,
        moved=10**7,
        in_specs=[HBM] * 4,
    )
    total = call(reduce_kernel, shape((n_dp if direct else 1, share, 3 * ROWS, 2 * LANES), bf16), (got,), moved=10**6)
    partner = lax.ppermute(other, "mp", swap)
    grad_tokens = call(
        input_kernel, shape(tokens.shape, bf16), (own, partner, qt), flops=5 * 10**8, moved=4 * 10**6
    )
    total, grad_tokens = lax.optimization_barrier((total, grad_tokens))
    if direct:
        total = lax.all_to_all(total, "dp", 0, 0, tiled=True)
    total = total.reshape(groups, 3 * ROWS, 2 * LANES)
    keep, send = call(pack_kernel, (shape((groups, ROWS, LANES), bf16),) * 2, (total,), moved=10**5)
    partner_rows = lax.ppermute(send, "mp", swap)
    scale = 1.0 / math.sqrt(tokens.shape[0] * n_dp)
    gate_grad, up_grad = call(
        functools.partial(layout_kernel, scale, fb),
        (shape((fb * db, block), f32),) * 2,
        (total,),
        [pltpu.VMEM((fb * db, LANES), f32)],
        moved=10**6,
    )
    down_grad = call(
        functools.partial(down_layout_kernel, scale, fb),
        shape((2 * fb, per, block), f32),
        (keep, partner_rows),
        moved=10**6,
    ).transpose(1, 0, 2)
    return (grad_tokens, gate_grad.reshape(fb, db, block), up_grad.reshape(fb, db, block), down_grad)


def solution(mesh):
    in_specs = (
        P(("groups", "dp"), "mp"),
        P(("groups", "dp"), "mp"),
        P("mp", None, None),
        P("mp", None, None),
        P("mp", None, None),
    )
    out_specs = (
        P(("groups", "dp"), "mp"),
        P(("groups", "mp"), None, None),
        P(("groups", "mp"), None, None),
        P(("groups", "mp"), None, None),
    )
    return jax.shard_map(shards, mesh=mesh, in_specs=in_specs, out_specs=out_specs, check_vma=False)
```

```python
import functools
import math

import jax
import jax.numpy as jnp
import numpy as np
from jax import lax
from jax.experimental import pallas as pl
from jax.experimental.pallas import tpu as pltpu
from jax.sharding import PartitionSpec as P

F = 8
PAIR = 2 * F
LANES = 128
ROWS = 16


def transform_tables(block):
    half = block // 2
    n = np.arange(block)
    k = np.arange(half)
    angles = ((n[:, None] * k[None, :]) % block).astype(np.float32) * np.float32(2.0 * math.pi / block)
    cosine = np.cos(angles.astype(np.float64)).astype(np.float32)
    sine = np.sin(angles.astype(np.float64)).astype(np.float32)
    parity = (1 - 2 * (n % 2)).astype(np.float32)
    norm = np.float32(1.0 / math.sqrt(block))
    forward = np.concatenate([cosine, parity[:, None], -sine[:, 1:]], axis=1) * norm
    doubling = np.where(k >= 1, 2.0, 1.0).astype(np.float32)
    inverse = np.concatenate([(cosine * doubling).T, parity[None, :], -2.0 * sine[:, 1:].T], axis=0) * norm
    order = np.arange(block).reshape(2, half // PAIR, PAIR).transpose(1, 0, 2).reshape(-1)
    extra = np.zeros((16, half), np.float32)
    inverse_cos = np.concatenate([inverse[:half, :half].T, extra], axis=0)
    inverse_cos[half] = inverse[:half, half]
    inverse_sin = inverse[half:, :half].T.copy()
    inverse_sin[:, 0] = 0.0
    forward_cos = np.concatenate([forward[:half, :half].T, extra], axis=0)
    forward_cos[half] = forward[:half, half]
    forward_sin = forward[:half, half:].T.copy()
    forward_sin[0] = 0.0
    tables = (forward.T[order], inverse.T[:, order], inverse_cos, inverse_sin, forward_cos, forward_sin)
    return [jnp.asarray(table, jnp.bfloat16) for table in tables]


def nt_dot(a, b):
    return lax.dot_general(a, b, (((1,), (1,)), ((), ())), preferred_element_type=jnp.float32)


def dot(a, b):
    return jnp.dot(a, b, preferred_element_type=jnp.float32)


def swap_blocks(tiles):
    tiles = list(tiles)
    lane_block = lax.broadcasted_iota(jnp.int32, tiles[0].shape, 1) // F
    step = len(tiles) // 2
    while step:
        high = (lane_block & step) != 0
        for i in range(len(tiles)):
            if i & step:
                continue
            low_tile, high_tile = tiles[i], tiles[i + step]
            tiles[i] = jnp.where(high, pltpu.roll(high_tile, F * step, 1), low_tile)
            tiles[i + step] = jnp.where(high, high_tile, pltpu.roll(low_tile, LANES - F * step, 1))
        step //= 2
    return tiles


def weight_rows(read, write, conj, half):
    for part in range(half // LANES):
        at = part * LANES
        tiles = swap_blocks([read(i, at) for i in range(8)] + [read(i, half + at) for i in range(8)])
        for i, tile in enumerate(tiles):
            lane = lax.broadcasted_iota(jnp.int32, tile.shape, 1)
            left = lane < LANES // 2
            turned = pltpu.roll(tile, LANES // 2, 1)
            if conj:
                real, imag = tile, jnp.where(left, -turned, turned)
            else:
                real, imag = jnp.where(left, tile, -tile), turned
            if part == 0 and i == 0:
                first = lane % F == 0
                real = jnp.where(first & ~left, 0.0, real)
                imag = jnp.where(first, jnp.where(left, 0.0, tile), imag)
            write(part * 16 + i, 0, real)
            write(part * 16 + i, 1, imag)


def adjoint_rows(read, write, half):
    for part in range(half // LANES):
        at = part * LANES
        re = swap_blocks([read(o, at) for o in range(16)])
        im = swap_blocks([read(o, half + at) for o in range(16)])
        for i in range(16):
            cross, wim = re[i], im[i]
            if part == 0 and i == 0:
                first = lax.broadcasted_iota(jnp.int32, wim.shape, 1) % F == 0
                cross = jnp.where(first, wim, cross)
                wim = jnp.where(first, 0.0, wim)
            write(part * 16 + i, 0, 0, re[i])
            write(part * 16 + i, 0, 1, wim)
            write(part * 16 + i, 1, 0, -wim)
            write(part * 16 + i, 1, 1, cross)


def diagonal():
    row = lax.broadcasted_iota(jnp.int32, (PAIR, LANES), 0)
    lane = lax.broadcasted_iota(jnp.int32, (PAIR, LANES), 1)
    return jnp.where(lane % F == row % F, 1.0, 0.0).astype(jnp.bfloat16)


def spread(read, count, mask):
    return jnp.concatenate(
        [jnp.concatenate([read(r), read(r + 1)], axis=0).astype(jnp.bfloat16) * mask for r in range(0, count, 2)], axis=0
    )


def blocks(first, second):
    zero = jnp.zeros_like(first)
    return jnp.concatenate(
        [jnp.concatenate([first, zero], axis=1), jnp.concatenate([zero, second], axis=1)], axis=0
    )


def side_by_side(values):
    return jnp.concatenate([values[..., :LANES], values[..., LANES:]], axis=-2)


def swiglu_back(gate, up, grad):
    sig = 1.0 / (1.0 + jnp.exp(-gate))
    gated = gate * sig
    return (
        (gated * up).astype(jnp.bfloat16),
        (grad * up * sig * (1.0 + gate * (1.0 - sig))).astype(jnp.bfloat16),
        (grad * gated).astype(jnp.bfloat16),
    )


def main_kernel(fb, norm, wg_in, wu_in, pt_in, x_own_in, c_own_in, wd_own_in, wd_other_in, x_other_in, c_other_in,
                qc_in, qs_in, pc_in, ps_in, d_ref, own_ref, other_ref, wg_ref, wu_ref, pt_ref, x_own, c_own, wd_ref,
                x_other, c_other, qc_ref, qs_ref, pc_ref, ps_ref, sx, sc, gs, us, hs, hid, gg, ug, rg, ru, rd, ra, rb,
                flat, part, in_sem):
    core = lax.axis_index("mp")
    db = 8
    per = db // 2
    block = pt_ref.shape[0]
    half = block // 2
    pairs = half // PAIR
    arrays = (
        (wg_in, wg_ref), (wu_in, wu_ref), (pt_in, pt_ref), (x_own_in, x_own), (c_own_in, c_own),
        (wd_own_in, wd_ref.at[pl.ds(core * per, per)]), (wd_other_in, wd_ref.at[pl.ds((1 - core) * per, per)]),
        (x_other_in, x_other), (c_other_in, c_other),
        (qc_in, qc_ref), (qs_in, qs_ref), (pc_in, pc_ref), (ps_in, ps_ref),
    )
    copies = [pltpu.make_async_copy(src, dst, in_sem.at[n]) for n, (src, dst) in enumerate(arrays)]
    for copy in copies:
        copy.start()

    def to_spectra(source, target, first):
        for j in range(0, per, 2):
            pair = jnp.concatenate(
                [source[:, j * block : (j + 1) * block], source[:, (j + 1) * block : (j + 2) * block]], axis=0
            )
            result = nt_dot(pt_ref[...], pair).reshape(pairs, 2, 2, F, 2 * LANES)
            target[:, :, :, first // 2 + j // 2] = side_by_side(result).astype(jnp.bfloat16)

    for copy in copies[:5]:
        copy.wait()
    to_spectra(x_own, sx, core * per)
    to_spectra(c_own, sc, core * per)
    for n, (source, target, adjoint) in enumerate(((wg_ref, rg, ra), (wu_ref, ru, rb))):
        for tile in range(block // LANES):
            for o in range(fb):
                flat[n, tile, o * db : (o + 1) * db] = source[o, :, tile * LANES : (tile + 1) * LANES].astype(jnp.float32)

        def read(i, at, n=n):
            return flat[n, at // LANES, pl.ds(i, fb, stride=db), :]

        def write(group, ri, rows, target=target):
            at = (group * 2 + ri) * ROWS
            target[at : at + fb, :] = rows

        weight_rows(read, write, False, half)

        def read_adjoint(o, at, n=n):
            if o >= fb:
                return jnp.zeros((db, LANES), jnp.float32)
            return flat[n, at // LANES, o * db : (o + 1) * db, :]

        def write_adjoint(group, ri, tile, rows, adjoint=adjoint):
            at = (group * 2 + ri) * db
            adjoint[tile, at : at + db, :] = rows

        adjoint_rows(read_adjoint, write_adjoint, half)

    for copy in copies[5:9]:
        copy.wait()
    to_spectra(x_other, sx, (1 - core) * per)
    to_spectra(c_other, sc, (1 - core) * per)

    def read_down(o, at):
        return wd_ref[o, :, at : at + LANES].astype(jnp.float32)

    def write_down(group, ri, rows):
        at = (group * 2 + ri) * ROWS
        rd[at : at + fb, :] = rows

    weight_rows(read_down, write_down, True, half)
    if fb < ROWS:
        for target in (gg, ug):
            target[:, :, :, fb // 2 :] = jnp.zeros((pairs, 2, 2, (ROWS - fb) // 2, PAIR, LANES), jnp.bfloat16)

    mask = diagonal()

    def both_groups(ref, g):
        return blocks(*(ref[g, :, h].reshape(LANES, LANES) for h in range(2)))

    @pl.loop(0, pairs)
    def _(g):
        for source, weights in ((sx, ((rg, gs), (ru, us))), (sc, ((rd, hs),))):
            spectrum = both_groups(source, g)
            for rows, target in weights:
                left = jnp.concatenate(
                    [
                        jnp.concatenate(
                            [
                                spread(
                                    lambda o, h=h, ri=ri, rows=rows: rows[
                                        pl.ds(((2 * g + h) * 2 + ri) * ROWS + o, F, stride=0), :
                                    ],
                                    fb,
                                    mask,
                                )
                                for h in range(2)
                            ],
                            axis=1,
                        )
                        for ri in range(2)
                    ],
                    axis=0,
                )
                result = side_by_side(dot(left, spectrum).reshape(2, fb, F, 2 * LANES)).astype(jnp.bfloat16)
                for ri in range(2):
                    target[:, g, ri] = result[ri]

    for copy in copies[9:]:
        copy.wait()
    top = lax.broadcasted_iota(jnp.int32, (F, LANES), 0)
    signed = jnp.where(top % 2 == 0, norm, -norm)

    def set_row(values, row):
        return jnp.concatenate([jnp.where(top == 0, row, values[:F]), values[F:]], axis=0)

    def add_tile(values, tile):
        return (values.reshape(-1, F, LANES) + tile[None]).reshape(values.shape)

    @pl.loop(0, fb // 2)
    def _(pair):
        sources = [(ref, 2 * pair + u) for u in range(2) for ref in (gs, us, hs)]
        re = jnp.concatenate([ref[o, :, 0].reshape(half, LANES) for ref, o in sources], axis=1)
        im = jnp.concatenate([ref[o, :, 1].reshape(half, LANES) for ref, o in sources], axis=1)
        even = dot(qc_ref[...], re)
        odd = dot(qs_ref[...], im)
        near, far = [], []
        for v in range(len(sources)):
            lanes = slice(v * LANES, (v + 1) * LANES)
            last = im[:PAIR, lanes].astype(jnp.float32)[:1]
            shared = add_tile(even[:half, lanes], last * signed)
            near.append(shared + odd[:, lanes])
            far.append(set_row(shared - odd[:, lanes], even[half : half + 1, lanes] + last * norm))
        sums, differences, middles = [], [], []
        for u in range(2):
            for a, b in zip(swiglu_back(*near[3 * u : 3 * u + 3]), swiglu_back(*far[3 * u : 3 * u + 3])):
                a, b = a.astype(jnp.float32), b.astype(jnp.float32)
                middles.append(b[:1])
                sums.append(set_row(a + b, a[:1]).astype(jnp.bfloat16))
                differences.append((a - b).astype(jnp.bfloat16))
        re = dot(pc_ref[...], jnp.concatenate(sums, axis=1))
        im = dot(ps_ref[...], jnp.concatenate(differences, axis=1))
        for v, target in enumerate((hid, gg, ug)):
            real, imag = [], []
            for u in range(2):
                at = (3 * u + v) * LANES
                middle = middles[3 * u + v]
                real.append(add_tile(re[:half, at : at + LANES], middle * signed))
                imag.append(set_row(im[:, at : at + LANES], re[half : half + 1, at : at + LANES] + middle * norm))
            for ri, two in enumerate((real, imag)):
                two = [values.reshape(pairs, 2, F, LANES) for values in two]
                target[:, ri, :, pair] = jnp.concatenate(two, axis=2).astype(jnp.bfloat16)

    lane = lax.broadcasted_iota(jnp.int32, (F, LANES), 1)
    left = lane < LANES // 2

    @pl.loop(0, pairs)
    def _(g):
        for w, (rows, cols, sign) in enumerate(((gg, sx, 1), (ug, sx, 1), (hid, sc, -1))):
            two = jnp.concatenate([rows[g, :, h, : fb // 2].reshape(2 * fb * F, LANES) for h in range(2)], axis=1)
            m = nt_dot(two, both_groups(cols, g))
            for h in range(2):
                result = []
                for upper in range(0, fb, 8):
                    sums = [jnp.zeros((F, LANES), jnp.float32)] * 2
                    for o in range(upper, min(upper + 8, fb)):
                        turn = o - upper
                        here = (top - lane) % 8 == turn
                        for q in range(2):
                            tile = m[(q * fb + o) * F : (q * fb + o + 1) * F, h * LANES : (h + 1) * LANES]
                            sums[q] = jnp.where(here, pltpu.roll(tile, turn, 0) if turn else tile, sums[q])
                    same = jnp.where(left, sums[0], sums[1])
                    cross = jnp.where(left, sums[1], sums[0])
                    turned = pltpu.roll(cross, LANES // 2, 1)
                    both = jnp.where(
                        left, same + pltpu.roll(same, LANES // 2, 1), turned - cross if sign > 0 else cross - turned
                    )
                    if h == 0:
                        both = jnp.where((lane % F == 0) & (g == 0), same, both)
                    result.append(both)
                d_ref[g, w * ROWS : (w + 1) * ROWS, h * LANES : (h + 1) * LANES] = jnp.concatenate(
                    result, axis=0
                ).astype(jnp.bfloat16)
        spectrum = jnp.concatenate([blocks(*(ref[g, :, h].reshape(2 * LANES, LANES) for h in range(2))) for ref in (gg, ug)])
        weights = jnp.concatenate(
            [
                spread(
                    lambda r, h=h, tile=tile, ref=ref: ref[
                        tile, pl.ds((2 * g + h) * 2 * db + r, F, stride=0), :
                    ],
                    2 * db,
                    mask,
                )
                for ref in (ra, rb)
                for h in range(2)
                for tile in range(2)
            ],
            axis=1,
        )
        part[...] = side_by_side(dot(weights, spectrum).reshape(2, db, F, 2 * LANES))
        for ri in range(2):
            own_ref[g, ri] = part[ri, pl.ds(core * per, per)]
            other_ref[g, ri] = part[ri, pl.ds((1 - core) * per, per)].astype(jnp.bfloat16)


def input_kernel(own_ref, got_ref, qt_ref, out_ref):
    block = qt_ref.shape[0]
    for j in range(own_ref.shape[2]):
        spectrum = (own_ref[:, :, j] + got_ref[:, :, j].astype(jnp.float32)).astype(jnp.bfloat16)
        values = dot(qt_ref[...], spectrum.reshape(block, LANES))
        out_ref[:, j * block : (j + 1) * block] = values.T.astype(jnp.bfloat16)


def reduce_kernel(r_ref, out_ref):
    total = r_ref[0].astype(jnp.float32)
    for d in range(1, r_ref.shape[0]):
        total = total + r_ref[d].astype(jnp.float32)
    total = total.astype(jnp.bfloat16)
    for d in range(out_ref.shape[0]):
        out_ref[d] = total


def straight(tile):
    halves = []
    lane = lax.broadcasted_iota(jnp.int32, (8, LANES), 1)
    for at in range(0, tile.shape[0], 8):
        half = tile[at : at + 8]
        for bit in (1, 2, 4):
            half = jnp.where((lane & bit) != 0, pltpu.roll(half, 8 - bit, 0), half)
        halves.append(half)
    return jnp.concatenate(halves, axis=0)


def entries(source, rows, part):
    tiles = []
    for i in range(16):
        lanes = slice((i % 2) * LANES, (i % 2 + 1) * LANES)
        tiles.append(straight(source[part * 8 + i // 2, rows, lanes].astype(jnp.float32)))
    return swap_blocks(tiles)


def factor(scale, part):
    lane = lax.broadcasted_iota(jnp.int32, (1, LANES), 1)
    return jnp.where((lane == 0) & (part == 0), scale, 2.0 * scale)


def layout_kernel(scale, fb, s_ref, gate_ref, up_ref, flat):
    half = s_ref.shape[0] * PAIR
    for w, target in enumerate((gate_ref, up_ref)):
        for part in range(half // LANES):
            tiles = entries(s_ref, slice(w * ROWS, (w + 1) * ROWS), part)
            for ri in range(2):
                at = ri * half + part * LANES
                for i in range(8):
                    flat[w, ri, pl.ds(i, fb, stride=8), :] = tiles[8 * ri + i][:fb] * factor(scale, part)
                target[:, at : at + LANES] = flat[w, ri]


def down_layout_kernel(scale, fb, own_ref, got_ref, down_ref):
    core = lax.axis_index("mp")
    half = own_ref.shape[0] * PAIR
    outputs = down_ref.shape[1]
    for source, h in ((own_ref, core), (got_ref, 1 - core)):
        for part in range(half // LANES):
            tiles = entries(source, slice(0, ROWS), part)
            for ri in range(2):
                at = ri * half + part * LANES
                for o in range(outputs):
                    rows = jnp.where(core == 0, tiles[8 * ri + o], tiles[8 * ri + outputs + o])
                    down_ref[pl.ds(h * fb, fb), o, at : at + LANES] = rows[:fb] * factor(scale, part)


def params(mib):
    return pltpu.CompilerParams(vmem_limit_bytes=mib << 20)


VMEM = pl.BlockSpec(memory_space=pltpu.VMEM)
HBM = pl.BlockSpec(memory_space=pltpu.HBM)


def call(kernel, out_shape, args, scratch=(), mib=16, flops=0, moved=0, in_specs=None, out_specs=None):
    return pl.pallas_call(
        kernel,
        out_shape=out_shape,
        in_specs=in_specs or [VMEM] * len(args),
        out_specs=out_specs or jax.tree.map(lambda _: VMEM, out_shape),
        scratch_shapes=list(scratch),
        compiler_params=params(mib),
        cost_estimate=pl.CostEstimate(flops=flops, bytes_accessed=moved, transcendentals=0),
    )(*args)


def shards(tokens, cotangent, gate_spectra, up_spectra, down_spectra):
    n_dp = lax.axis_size("dp")
    core = lax.axis_index("mp")
    swap = [(0, 1), (1, 0)]
    fb, db, block = gate_spectra.shape
    assert db == 8 and fb <= ROWS and fb % 2 == 0 and tokens.shape[0] == LANES and lax.axis_size("mp") == 2
    half = block // 2
    pairs = half // PAIR
    groups = half // F
    per = db // 2
    bf16, f32 = jnp.bfloat16, jnp.float32
    shape = jax.ShapeDtypeStruct
    pt, qt, qc, qs, pc, ps = transform_tables(block)
    norm = float(np.asarray(1.0 / math.sqrt(block), jnp.bfloat16))

    tokens_other = lax.ppermute(tokens, "mp", swap)
    cotangent_other = lax.ppermute(cotangent, "mp", swap)
    down = down_spectra.reshape(per, 2, fb, block)
    down_own = jnp.where(core == 0, down[:, 0], down[:, 1])
    down_got = lax.ppermute(jnp.where(core == 0, down[:, 1], down[:, 0]), "mp", swap)

    inputs = (
        gate_spectra, up_spectra, pt, tokens, cotangent, down_own, down_got, tokens_other, cotangent_other, qc, qs, pc, ps
    )
    buffers = [shape((db, fb, block), bf16) if n == 5 else a for n, a in enumerate(inputs) if n != 6]
    d_all, own, other = call(
        functools.partial(main_kernel, fb, norm),
        (
            shape((pairs, 3 * ROWS, 2 * LANES), bf16),
            shape((pairs, 2, per, PAIR, LANES), f32),
            shape((pairs, 2, per, PAIR, LANES), bf16),
        ),
        inputs,
        [pltpu.VMEM(a.shape, bf16) for a in buffers]
        + [pltpu.VMEM((pairs, 2, 2, db // 2, PAIR, LANES), bf16)] * 2
        + [pltpu.VMEM((fb, pairs, 2, PAIR, LANES), bf16)] * 3
        + [pltpu.VMEM((pairs, 2, 2, ROWS // 2, PAIR, LANES), bf16)] * 3
        + [pltpu.VMEM((groups * 2 * ROWS, LANES), f32)] * 3
        + [pltpu.VMEM((2, groups * 2 * db, LANES), f32)] * 2
        + [pltpu.VMEM((2, block // LANES, fb * db, LANES), f32), pltpu.VMEM((2, db, PAIR, LANES), f32)]
        + [pltpu.SemaphoreType.DMA((len(inputs),))],
        mib=63,
        flops=10**10,
        moved=10**7,
        in_specs=[HBM] * len(inputs),
    )

    direct = pairs % n_dp == 0
    if direct:
        share = pairs // n_dp
        got = lax.all_to_all(d_all.reshape(n_dp, share, 3 * ROWS, 2 * LANES), "dp", 0, 0, tiled=True)
    else:
        share = pairs
        got = lax.psum(d_all.astype(f32), "dp")[None]
    partner = lax.ppermute(other, "mp", swap)
    grad_tokens = call(
        input_kernel, shape(tokens.shape, bf16), (own, partner, qt), flops=5 * 10**8, moved=4 * 10**6
    )

    total = call(reduce_kernel, shape((n_dp if direct else 1, share, 3 * ROWS, 2 * LANES), bf16), (got,), moved=10**6)
    total, grad_tokens = lax.optimization_barrier((total, grad_tokens))
    if direct:
        total = lax.all_to_all(total, "dp", 0, 0, tiled=True)
    total = total.reshape(pairs, 3 * ROWS, 2 * LANES)
    down_sums = total[:, 2 * ROWS :]
    partner_sums = lax.ppermute(down_sums, "mp", swap)
    scale = 1.0 / math.sqrt(tokens.shape[0] * n_dp)
    gate_grad, up_grad = call(
        functools.partial(layout_kernel, scale, fb),
        (shape((fb * db, block), f32),) * 2,
        (total,),
        [pltpu.VMEM((2, 2, fb * db, LANES), f32)],
        moved=10**6,
    )
    down_grad = call(
        functools.partial(down_layout_kernel, scale, fb),
        shape((2 * fb, per, block), f32),
        (down_sums, partner_sums),
        moved=10**6,
    ).transpose(1, 0, 2)
    return (grad_tokens, gate_grad.reshape(fb, db, block), up_grad.reshape(fb, db, block), down_grad)


def solution(mesh):
    in_specs = (
        P(("groups", "dp"), "mp"),
        P(("groups", "dp"), "mp"),
        P("mp", None, None),
        P("mp", None, None),
        P("mp", None, None),
    )
    out_specs = (
        P(("groups", "dp"), "mp"),
        P(("groups", "mp"), None, None),
        P(("groups", "mp"), None, None),
        P(("groups", "mp"), None, None),
    )
    return jax.shard_map(shards, mesh=mesh, in_specs=in_specs, out_specs=out_specs, check_vma=False)
```

```python
import functools
import math

import jax
import jax.numpy as jnp
import numpy as np
from jax import lax
from jax.experimental import pallas as pl
from jax.experimental.pallas import tpu as pltpu
from jax.sharding import PartitionSpec as P

F = 8
PAIR = 2 * F
LANES = 128
ROWS = 16


def transform_tables(block):
    half = block // 2
    n = np.arange(block)
    k = np.arange(half)
    angles = ((n[:, None] * k[None, :]) % block).astype(np.float32) * np.float32(2.0 * math.pi / block)
    cosine = np.cos(angles.astype(np.float64)).astype(np.float32)
    sine = np.sin(angles.astype(np.float64)).astype(np.float32)
    parity = (1 - 2 * (n % 2)).astype(np.float32)
    norm = np.float32(1.0 / math.sqrt(block))
    forward = np.concatenate([cosine, parity[:, None], -sine[:, 1:]], axis=1) * norm
    doubling = np.where(k >= 1, 2.0, 1.0).astype(np.float32)
    inverse = np.concatenate([(cosine * doubling).T, parity[None, :], -2.0 * sine[:, 1:].T], axis=0) * norm
    order = np.arange(block).reshape(2, half // PAIR, PAIR).transpose(1, 0, 2).reshape(-1)
    extra = np.zeros((16, half), np.float32)
    folded = np.concatenate([np.arange(half), [half], np.arange(block - 1, half, -1)])
    forward_cos = np.concatenate([forward[:half, :half].T, extra], axis=0)
    forward_cos[half] = forward[:half, half]
    forward_sin = forward[:half, half:].T.copy()
    forward_sin[0] = 0.0
    natural = inverse.T[:, order]
    tables = (forward.T[order], natural, natural[folded], forward_cos, forward_sin)
    return [jnp.asarray(table, jnp.bfloat16) for table in tables]


def nt_dot(a, b):
    return lax.dot_general(a, b, (((1,), (1,)), ((), ())), preferred_element_type=jnp.float32)


def dot(a, b):
    return jnp.dot(a, b, preferred_element_type=jnp.float32)


def swap_blocks(tiles):
    tiles = list(tiles)
    lane_block = lax.broadcasted_iota(jnp.int32, tiles[0].shape, 1) // F
    step = len(tiles) // 2
    while step:
        high = (lane_block & step) != 0
        for i in range(len(tiles)):
            if i & step:
                continue
            low_tile, high_tile = tiles[i], tiles[i + step]
            tiles[i] = jnp.where(high, pltpu.roll(high_tile, F * step, 1), low_tile)
            tiles[i + step] = jnp.where(high, high_tile, pltpu.roll(low_tile, LANES - F * step, 1))
        step //= 2
    return tiles


def weight_rows(read, write, conj, half):
    for part in range(half // LANES):
        at = part * LANES
        tiles = swap_blocks([read(i, at) for i in range(8)] + [read(i, half + at) for i in range(8)])
        for i, tile in enumerate(tiles):
            lane = lax.broadcasted_iota(jnp.int32, tile.shape, 1)
            left = lane < LANES // 2
            turned = pltpu.roll(tile, LANES // 2, 1)
            if conj:
                real, imag = tile, jnp.where(left, -turned, turned)
            else:
                real, imag = jnp.where(left, tile, -tile), turned
            if part == 0 and i == 0:
                first = lane % F == 0
                real = jnp.where(first & ~left, 0.0, real)
                imag = jnp.where(first, jnp.where(left, 0.0, tile), imag)
            write(part * 16 + i, 0, real)
            write(part * 16 + i, 1, imag)


def adjoint_rows(read, write, half):
    for part in range(half // LANES):
        at = part * LANES
        re = swap_blocks([read(o, at) for o in range(16)])
        im = swap_blocks([read(o, half + at) for o in range(16)])
        for i in range(16):
            cross, wim = re[i], im[i]
            if part == 0 and i == 0:
                first = lax.broadcasted_iota(jnp.int32, wim.shape, 1) % F == 0
                cross = jnp.where(first, wim, cross)
                wim = jnp.where(first, 0.0, wim)
            write(part * 16 + i, 0, 0, re[i])
            write(part * 16 + i, 0, 1, wim)
            write(part * 16 + i, 1, 0, -wim)
            write(part * 16 + i, 1, 1, cross)


def diagonal():
    row = lax.broadcasted_iota(jnp.int32, (PAIR, LANES), 0)
    lane = lax.broadcasted_iota(jnp.int32, (PAIR, LANES), 1)
    return jnp.where(lane % F == row % F, 1.0, 0.0).astype(jnp.bfloat16)


def spread(read, count, mask):
    return jnp.concatenate(
        [jnp.concatenate([read(r), read(r + 1)], axis=0).astype(jnp.bfloat16) * mask for r in range(0, count, 2)], axis=0
    )


def blocks(first, second):
    zero = jnp.zeros_like(first)
    return jnp.concatenate(
        [jnp.concatenate([first, zero], axis=1), jnp.concatenate([zero, second], axis=1)], axis=0
    )


def side_by_side(values):
    return jnp.concatenate([values[..., :LANES], values[..., LANES:]], axis=-2)


def swiglu_back(gate, up, grad):
    sig = 1.0 / (1.0 + jnp.exp(-gate))
    gated = gate * sig
    slope = sig + gated * (1.0 - sig)
    return (
        (gated * up).astype(jnp.bfloat16),
        (grad * up * slope).astype(jnp.bfloat16),
        (grad * gated).astype(jnp.bfloat16),
    )


def main_kernel(fb, norm, wg_in, wu_in, pt_in, x_own_in, c_own_in, wd_own_in, wd_other_in, x_other_in, c_other_in,
                qf_in, pc_in, ps_in, d_ref, gg_out, ug_out, wg_ref, wu_ref, pt_ref, x_own, c_own, wd_ref,
                x_other, c_other, qf_ref, pc_ref, ps_ref, sx, sc, gs, us, hs, hid, gg, ug, rg, ru, rd,
                sums_ref, diffs_ref, mids_ref, flat, in_sem, out_sem):
    core = lax.axis_index("mp")
    db = 8
    per = db // 2
    block = pt_ref.shape[0]
    half = block // 2
    pairs = half // PAIR
    arrays = (
        (wg_in, wg_ref), (wu_in, wu_ref), (pt_in, pt_ref), (x_own_in, x_own), (c_own_in, c_own),
        (wd_own_in, wd_ref.at[pl.ds(core * per, per)]), (wd_other_in, wd_ref.at[pl.ds((1 - core) * per, per)]),
        (x_other_in, x_other), (c_other_in, c_other),
        (qf_in, qf_ref), (pc_in, pc_ref), (ps_in, ps_ref),
    )
    copies = [pltpu.make_async_copy(src, dst, in_sem.at[n]) for n, (src, dst) in enumerate(arrays)]
    for copy in copies:
        copy.start()

    def to_spectra(source, target, first):
        rows = jnp.concatenate([source[:, j * block : (j + 1) * block] for j in range(per)], axis=0)
        result = nt_dot(pt_ref[...], rows).reshape(pairs, 2, 2, F, per * LANES)
        for j in range(0, per, 2):
            two = side_by_side(result[..., j * LANES : (j + 2) * LANES])
            target[:, :, :, first // 2 + j // 2] = two.astype(jnp.bfloat16)

    for copy in copies[:5]:
        copy.wait()
    to_spectra(x_own, sx, core * per)
    to_spectra(c_own, sc, core * per)
    for n, (source, target) in enumerate(((wg_ref, rg), (wu_ref, ru))):
        for tile in range(block // LANES):
            for o in range(fb):
                flat[n, tile, o * db : (o + 1) * db] = source[o, :, tile * LANES : (tile + 1) * LANES].astype(jnp.float32)

        def read(i, at, n=n):
            return flat[n, at // LANES, pl.ds(i, fb, stride=db), :]

        def write(group, ri, rows, target=target):
            at = (group * 2 + ri) * ROWS
            target[at : at + fb, :] = rows

        weight_rows(read, write, False, half)

    for copy in copies[5:9]:
        copy.wait()
    to_spectra(x_other, sx, (1 - core) * per)
    to_spectra(c_other, sc, (1 - core) * per)

    def read_down(o, at):
        return wd_ref[o, :, at : at + LANES].astype(jnp.float32)

    def write_down(group, ri, rows):
        at = (group * 2 + ri) * ROWS
        rd[at : at + fb, :] = rows

    weight_rows(read_down, write_down, True, half)
    if fb < ROWS:
        for target in (gg, ug):
            target[:, :, :, fb // 2 :] = jnp.zeros((pairs, 2, 2, (ROWS - fb) // 2, PAIR, LANES), jnp.bfloat16)

    mask = diagonal()

    def both_groups(ref, g):
        return blocks(*(ref[g, :, h].reshape(LANES, LANES) for h in range(2)))

    def mix(g):
        for source, weights in ((sx, ((rg, gs), (ru, us))), (sc, ((rd, hs),))):
            spectrum = both_groups(source, g)
            for rows, target in weights:
                wide = jnp.concatenate(
                    [
                        jnp.concatenate(
                            [
                                spread(
                                    lambda o, h=h, ri=ri, rows=rows: rows[
                                        pl.ds(((2 * g + h) * 2 + ri) * ROWS + o, F, stride=0), :
                                    ],
                                    fb,
                                    mask,
                                )
                                for h in range(2)
                            ],
                            axis=1,
                        )
                        for ri in range(2)
                    ],
                    axis=0,
                )
                result = side_by_side(dot(wide, spectrum).reshape(2, fb, F, 2 * LANES)).astype(jnp.bfloat16)
                for ri in range(2):
                    target[:, g, ri] = result[ri]

    @pl.loop(0, pairs // 4)
    def _(n):
        for u in range(4):
            mix(4 * n + u)

    for copy in copies[9:]:
        copy.wait()
    top = lax.broadcasted_iota(jnp.int32, (F, LANES), 0)
    wide_top = lax.broadcasted_iota(jnp.int32, (F, 2 * LANES), 0)
    signed = jnp.where(wide_top % 2 == 0, norm, -norm)
    inner = jnp.where(lax.broadcasted_iota(jnp.int32, (PAIR, 2 * LANES), 0) == 0, 0.0, 1.0).astype(jnp.bfloat16)

    def set_row(values, row):
        return jnp.concatenate([jnp.where(wide_top == 0, row, values[:F]), values[F:]], axis=0)

    def add_tile(values, tile):
        return (values.reshape(-1, F, 2 * LANES) + tile[None]).reshape(values.shape)

    def to_values(pair):
        spectra = jnp.concatenate(
            [ref[2 * pair + u].reshape(block, LANES) for ref in (gs, us, hs) for u in range(2)], axis=1
        )
        return dot(qf_ref[...], spectra)

    def to_grads(values, slot):
        gate, up, grad = (values[:, v * 2 * LANES : (v + 1) * 2 * LANES] for v in range(3))
        for v, side in enumerate(swiglu_back(gate, up, grad)):
            near, far = side[:half], side[half:]
            mids_ref[slot, v] = far[:PAIR].astype(jnp.float32)[:F]
            sums_ref[slot, v, :PAIR] = near[:PAIR] + far[:PAIR] * inner
            sums_ref[slot, v, PAIR:] = near[PAIR:] + far[PAIR:]
            diffs_ref[slot, v] = near - far

    def to_grad_spectra(pair, slot):
        re = dot(pc_ref[...], jnp.concatenate([sums_ref[slot, v] for v in range(3)], axis=1))
        im = dot(ps_ref[...], jnp.concatenate([diffs_ref[slot, v] for v in range(3)], axis=1))
        for v, target in enumerate((hid, gg, ug)):
            lanes = slice(v * 2 * LANES, (v + 1) * 2 * LANES)
            middle = mids_ref[slot, v][:1]
            real = add_tile(re[:half, lanes], middle * signed)
            imag = set_row(im[:, lanes], re[half : half + 1, lanes] + middle * norm)
            for ri, both in enumerate((real, imag)):
                target[:, ri, :, pair] = side_by_side(both.reshape(pairs, 2, F, 2 * LANES)).astype(jnp.bfloat16)

    steps = fb // 2
    to_grads(to_values(0), 0)

    @pl.loop(0, (steps - 1) // 2)
    def _(n):
        for u in range(2):
            values = to_values(2 * n + u + 1)
            to_grad_spectra(2 * n + u, u)
            to_grads(values, 1 - u)

    if steps % 2 == 0:
        to_grad_spectra(steps - 2, 0)
        to_grads(to_values(steps - 1), 1)
    to_grad_spectra(steps - 1, 1 - steps % 2)

    stores = [
        pltpu.make_async_copy(src, dst, out_sem.at[n]) for n, (src, dst) in enumerate(((gg, gg_out), (ug, ug_out)))
    ]
    for copy in stores:
        copy.start()
    lane = lax.broadcasted_iota(jnp.int32, (F, LANES), 1)
    left = lane < LANES // 2

    def weight_sums(g):
        for w, (rows, cols, sign) in enumerate(((gg, sx, 1), (ug, sx, 1), (hid, sc, -1))):
            two = jnp.concatenate([rows[g, :, h, : fb // 2].reshape(2 * fb * F, LANES) for h in range(2)], axis=1)
            m = nt_dot(two, both_groups(cols, g))
            for h in range(2):
                result = []
                for upper in range(0, fb, 8):
                    sums = [jnp.zeros((F, LANES), jnp.float32)] * 2
                    for o in range(upper, min(upper + 8, fb)):
                        turn = o - upper
                        here = (top - lane) % 8 == turn
                        for q in range(2):
                            tile = m[(q * fb + o) * F : (q * fb + o + 1) * F, h * LANES : (h + 1) * LANES]
                            sums[q] = jnp.where(here, pltpu.roll(tile, turn, 0) if turn else tile, sums[q])
                    same = jnp.where(left, sums[0], sums[1])
                    cross = jnp.where(left, sums[1], sums[0])
                    turned = pltpu.roll(cross, LANES // 2, 1)
                    both = jnp.where(
                        left, same + pltpu.roll(same, LANES // 2, 1), turned - cross if sign > 0 else cross - turned
                    )
                    if h == 0:
                        both = jnp.where((lane % F == 0) & (g == 0), same, both)
                    result.append(both)
                d_ref[g, w * ROWS : (w + 1) * ROWS, h * LANES : (h + 1) * LANES] = jnp.concatenate(
                    result, axis=0
                ).astype(jnp.bfloat16)

    @pl.loop(0, pairs // 4)
    def _(n):
        for u in range(4):
            weight_sums(4 * n + u)

    for copy in stores:
        copy.wait()


def adjoint_kernel(fb, wg_in, wu_in, gg_in, ug_in, own_ref, other_ref, wg_ref, wu_ref, gg, ug, ra, rb, part, in_sem,
                   g_sem):
    core = lax.axis_index("mp")
    db = 8
    per = db // 2
    pairs = gg.shape[0]
    half = pairs * PAIR
    weights = [
        pltpu.make_async_copy(src, dst, in_sem.at[n]) for n, (src, dst) in enumerate(((wg_in, wg_ref), (wu_in, wu_ref)))
    ]

    def group_copies(g):
        return [
            pltpu.make_async_copy(src.at[g], dst.at[g], g_sem.at[n, g])
            for n, (src, dst) in enumerate(((gg_in, gg), (ug_in, ug)))
        ]

    for copy in weights:
        copy.start()
    for g in range(pairs):
        for copy in group_copies(g):
            copy.start()
    for copy in weights:
        copy.wait()
    for source, adjoint in ((wg_ref, ra), (wu_ref, rb)):
        def read(o, at, source=source):
            if o >= fb:
                return jnp.zeros((db, LANES), jnp.float32)
            return source[o, :, at : at + LANES].astype(jnp.float32)

        def write(group, ri, tile, rows, adjoint=adjoint):
            at = (group * 2 + ri) * db
            adjoint[tile, at : at + db, :] = rows

        adjoint_rows(read, write, half)
    mask = diagonal()

    def mix(g, slot):
        spectrum = jnp.concatenate([blocks(*(ref[g, :, h].reshape(2 * LANES, LANES) for h in range(2))) for ref in (gg, ug)])
        wide = jnp.concatenate(
            [
                spread(
                    lambda r, h=h, tile=tile, ref=ref: ref[tile, pl.ds((2 * g + h) * 2 * db + r, F, stride=0), :],
                    2 * db,
                    mask,
                )
                for ref in (ra, rb)
                for h in range(2)
                for tile in range(2)
            ],
            axis=1,
        )
        part[slot] = side_by_side(dot(wide, spectrum).reshape(2, db, F, 2 * LANES))
        for ri in range(2):
            own_ref[g, ri] = part[slot, ri, pl.ds(core * per, per)]
            other_ref[g, ri] = part[slot, ri, pl.ds((1 - core) * per, per)].astype(jnp.bfloat16)

    @pl.loop(0, pairs // 2)
    def _(n):
        for u in range(2):
            for copy in group_copies(2 * n + u):
                copy.wait()
        for u in range(2):
            mix(2 * n + u, u)


def input_kernel(own_ref, got_ref, qt_ref, out_ref):
    block = qt_ref.shape[0]
    for j in range(own_ref.shape[2]):
        spectrum = (own_ref[:, :, j] + got_ref[:, :, j].astype(jnp.float32)).astype(jnp.bfloat16)
        values = dot(qt_ref[...], spectrum.reshape(block, LANES))
        out_ref[:, j * block : (j + 1) * block] = values.T.astype(jnp.bfloat16)


def straight(tile):
    halves = []
    lane = lax.broadcasted_iota(jnp.int32, (8, LANES), 1)
    for at in range(0, tile.shape[0], 8):
        half = tile[at : at + 8]
        for bit in (1, 2, 4):
            half = jnp.where((lane & bit) != 0, pltpu.roll(half, 8 - bit, 0), half)
        halves.append(half)
    return jnp.concatenate(halves, axis=0)


def reduce_kernel(r_ref, out_ref):
    for g in range(r_ref.shape[1]):
        for lanes in (slice(0, LANES), slice(LANES, 2 * LANES)):
            total = r_ref[0, g, :, lanes].astype(jnp.float32)
            for d in range(1, r_ref.shape[0]):
                total = total + r_ref[d, g, :, lanes].astype(jnp.float32)
            total = straight(total).astype(jnp.bfloat16)
            for d in range(out_ref.shape[0]):
                out_ref[d, g, :, lanes] = total


def entries(source, rows, part):
    tiles = []
    for i in range(16):
        lanes = slice((i % 2) * LANES, (i % 2 + 1) * LANES)
        tiles.append(source[part * 8 + i // 2, rows, lanes].astype(jnp.float32))
    return swap_blocks(tiles)


def factor(scale, part):
    lane = lax.broadcasted_iota(jnp.int32, (1, LANES), 1)
    return jnp.where((lane == 0) & (part == 0), scale, 2.0 * scale)


def layout_kernel(scale, fb, s_ref, gate_ref, up_ref, flat):
    half = s_ref.shape[0] * PAIR
    for w, target in enumerate((gate_ref, up_ref)):
        for part in range(half // LANES):
            tiles = entries(s_ref, slice(w * ROWS, (w + 1) * ROWS), part)
            for ri in range(2):
                at = ri * half + part * LANES
                for i in range(8):
                    flat[w, ri, pl.ds(i, fb, stride=8), :] = tiles[8 * ri + i][:fb] * factor(scale, part)
                target[:, at : at + LANES] = flat[w, ri]


def down_layout_kernel(scale, fb, own_ref, got_ref, down_ref):
    core = lax.axis_index("mp")
    half = own_ref.shape[0] * PAIR
    outputs = down_ref.shape[1]
    for source, h in ((own_ref, core), (got_ref, 1 - core)):
        for part in range(half // LANES):
            tiles = entries(source, slice(0, ROWS), part)
            for ri in range(2):
                at = ri * half + part * LANES
                for o in range(outputs):
                    rows = jnp.where(core == 0, tiles[8 * ri + o], tiles[8 * ri + outputs + o])
                    down_ref[pl.ds(h * fb, fb), o, at : at + LANES] = rows[:fb] * factor(scale, part)


def params(mib):
    return pltpu.CompilerParams(vmem_limit_bytes=mib << 20)


VMEM = pl.BlockSpec(memory_space=pltpu.VMEM)
HBM = pl.BlockSpec(memory_space=pltpu.HBM)


def call(kernel, out_shape, args, scratch=(), mib=16, flops=0, moved=0, in_specs=None, out_specs=None):
    return pl.pallas_call(
        kernel,
        out_shape=out_shape,
        in_specs=in_specs or [VMEM] * len(args),
        out_specs=out_specs or jax.tree.map(lambda _: VMEM, out_shape),
        scratch_shapes=list(scratch),
        compiler_params=params(mib),
        cost_estimate=pl.CostEstimate(flops=flops, bytes_accessed=moved, transcendentals=0),
    )(*args)


def shards(tokens, cotangent, gate_spectra, up_spectra, down_spectra):
    n_dp = lax.axis_size("dp")
    core = lax.axis_index("mp")
    swap = [(0, 1), (1, 0)]
    fb, db, block = gate_spectra.shape
    assert db == 8 and fb <= ROWS and fb % 2 == 0 and tokens.shape[0] == LANES and lax.axis_size("mp") == 2
    half = block // 2
    pairs = half // PAIR
    groups = half // F
    per = db // 2
    bf16, f32 = jnp.bfloat16, jnp.float32
    shape = jax.ShapeDtypeStruct
    pt, qt, qf, pc, ps = transform_tables(block)
    norm = float(np.asarray(1.0 / math.sqrt(block), jnp.bfloat16))

    tokens_other = lax.ppermute(tokens, "mp", swap)
    cotangent_other = lax.ppermute(cotangent, "mp", swap)
    down = down_spectra.reshape(per, 2, fb, block)
    down_own = jnp.where(core == 0, down[:, 0], down[:, 1])
    down_got = lax.ppermute(jnp.where(core == 0, down[:, 1], down[:, 0]), "mp", swap)

    inputs = (
        gate_spectra, up_spectra, pt, tokens, cotangent, down_own, down_got, tokens_other, cotangent_other, qf, pc, ps
    )
    buffers = [shape((db, fb, block), bf16) if n == 5 else a for n, a in enumerate(inputs) if n != 6]
    spec = shape((pairs, 2, 2, ROWS // 2, PAIR, LANES), bf16)
    d_all, gg, ug = call(
        functools.partial(main_kernel, fb, norm),
        (shape((pairs, 3 * ROWS, 2 * LANES), bf16), spec, spec),
        inputs,
        [pltpu.VMEM(a.shape, bf16) for a in buffers]
        + [pltpu.VMEM((pairs, 2, 2, db // 2, PAIR, LANES), bf16)] * 2
        + [pltpu.VMEM((fb, pairs, 2, PAIR, LANES), bf16)] * 3
        + [pltpu.VMEM(spec.shape, bf16)] * 3
        + [pltpu.VMEM((groups * 2 * ROWS, LANES), f32)] * 3
        + [pltpu.VMEM((2, 3, half, 2 * LANES), bf16)] * 2
        + [pltpu.VMEM((2, 3, F, 2 * LANES), f32), pltpu.VMEM((2, block // LANES, fb * db, LANES), f32)]
        + [pltpu.SemaphoreType.DMA((len(inputs),)), pltpu.SemaphoreType.DMA((2,))],
        mib=63,
        flops=10**10,
        moved=10**7,
        in_specs=[HBM] * len(inputs),
        out_specs=(VMEM, HBM, HBM),
    )

    direct = pairs % n_dp == 0
    if direct:
        share = pairs // n_dp
        got = lax.all_to_all(d_all.reshape(n_dp, share, 3 * ROWS, 2 * LANES), "dp", 0, 0, tiled=True)
    else:
        share = pairs
        got = lax.psum(d_all.astype(f32), "dp")[None]
    own, other = call(
        functools.partial(adjoint_kernel, fb),
        (shape((pairs, 2, per, PAIR, LANES), f32), shape((pairs, 2, per, PAIR, LANES), bf16)),
        (gate_spectra, up_spectra, gg, ug),
        [pltpu.VMEM(gate_spectra.shape, bf16)] * 2
        + [pltpu.VMEM(spec.shape, bf16)] * 2
        + [pltpu.VMEM((2, groups * 2 * db, LANES), f32)] * 2
        + [pltpu.VMEM((2, 2, db, PAIR, LANES), f32)]
        + [pltpu.SemaphoreType.DMA((2,)), pltpu.SemaphoreType.DMA((2, pairs))],
        mib=63,
        flops=2 * 10**9,
        moved=10**7,
        in_specs=[HBM] * 4,
    )
    total = call(reduce_kernel, shape((n_dp if direct else 1, share, 3 * ROWS, 2 * LANES), bf16), (got,), moved=10**6)
    total, own, other = lax.optimization_barrier((total, own, other))
    partner = lax.ppermute(other, "mp", swap)
    grad_tokens = call(
        input_kernel, shape(tokens.shape, bf16), (own, partner, qt), flops=5 * 10**8, moved=4 * 10**6
    )
    if direct:
        total = lax.all_to_all(total, "dp", 0, 0, tiled=True)
    total = total.reshape(pairs, 3 * ROWS, 2 * LANES)
    down_sums = total[:, 2 * ROWS :]
    partner_sums = lax.ppermute(down_sums, "mp", swap)
    scale = 1.0 / math.sqrt(tokens.shape[0] * n_dp)
    gate_grad, up_grad = call(
        functools.partial(layout_kernel, scale, fb),
        (shape((fb * db, block), f32),) * 2,
        (total,),
        [pltpu.VMEM((2, 2, fb * db, LANES), f32)],
        moved=10**6,
    )
    down_grad = call(
        functools.partial(down_layout_kernel, scale, fb),
        shape((2 * fb, per, block), f32),
        (down_sums, partner_sums),
        moved=10**6,
    ).transpose(1, 0, 2)
    return (grad_tokens, gate_grad.reshape(fb, db, block), up_grad.reshape(fb, db, block), down_grad)


def solution(mesh):
    in_specs = (
        P(("groups", "dp"), "mp"),
        P(("groups", "dp"), "mp"),
        P("mp", None, None),
        P("mp", None, None),
        P("mp", None, None),
    )
    out_specs = (
        P(("groups", "dp"), "mp"),
        P(("groups", "mp"), None, None),
        P(("groups", "mp"), None, None),
        P(("groups", "mp"), None, None),
    )
    return jax.shard_map(shards, mesh=mesh, in_specs=in_specs, out_specs=out_specs, check_vma=False)
```

```python
import functools
import math

import jax
import jax.numpy as jnp
import numpy as np
from jax import lax
from jax.experimental import pallas as pl
from jax.experimental.pallas import tpu as pltpu
from jax.sharding import PartitionSpec as P


F = 8
PAIR = 2 * F
LANES = 128
ROWS = 16


def transform_tables(block):
    half = block // 2
    n = np.arange(block)
    k = np.arange(half)
    angles = ((n[:, None] * k[None, :]) % block).astype(np.float32) * np.float32(2.0 * math.pi / block)
    cosine = np.cos(angles.astype(np.float64)).astype(np.float32)
    sine = np.sin(angles.astype(np.float64)).astype(np.float32)
    parity = (1 - 2 * (n % 2)).astype(np.float32)
    norm = np.float32(1.0 / math.sqrt(block))
    forward = np.concatenate([cosine, parity[:, None], -sine[:, 1:]], axis=1) * norm
    doubling = np.where(k >= 1, 2.0, 1.0).astype(np.float32)
    inverse = np.concatenate([(cosine * doubling).T, parity[None, :], -2.0 * sine[:, 1:].T], axis=0) * norm
    order = np.arange(block).reshape(2, half // PAIR, PAIR).transpose(1, 0, 2).reshape(-1)
    extra = np.zeros((16, half), np.float32)
    folded = np.concatenate([np.arange(half), [half], np.arange(block - 1, half, -1)])
    forward_cos = np.concatenate([forward[:half, :half].T, extra], axis=0)
    forward_cos[half] = forward[:half, half]
    forward_sin = forward[:half, half:].T.copy()
    forward_sin[0] = 0.0
    natural = inverse.T[:, order]
    tables = (forward.T[order], natural, natural[folded], forward_cos, forward_sin)
    return [jnp.asarray(table, jnp.bfloat16) for table in tables]


def nt_dot(a, b):
    return lax.dot_general(a, b, (((1,), (1,)), ((), ())), preferred_element_type=jnp.float32)


def dot(a, b):
    return jnp.dot(a, b, preferred_element_type=jnp.float32)


def swap_blocks(tiles):
    tiles = list(tiles)
    lane_block = lax.broadcasted_iota(jnp.int32, tiles[0].shape, 1) // F
    step = len(tiles) // 2
    while step:
        high = (lane_block & step) != 0
        for i in range(len(tiles)):
            if i & step:
                continue
            low_tile, high_tile = tiles[i], tiles[i + step]
            tiles[i] = jnp.where(high, pltpu.roll(high_tile, F * step, 1), low_tile)
            tiles[i + step] = jnp.where(high, high_tile, pltpu.roll(low_tile, LANES - F * step, 1))
        step //= 2
    return tiles


def weight_rows(read, write, conj, half):
    for part in range(half // LANES):
        at = part * LANES
        tiles = swap_blocks([read(i, at) for i in range(8)] + [read(i, half + at) for i in range(8)])
        for i, tile in enumerate(tiles):
            lane = lax.broadcasted_iota(jnp.int32, tile.shape, 1)
            left = lane < LANES // 2
            turned = pltpu.roll(tile, LANES // 2, 1)
            if conj:
                real, imag = tile, jnp.where(left, -turned, turned)
            else:
                real, imag = jnp.where(left, tile, -tile), turned
            if part == 0 and i == 0:
                first = lane % F == 0
                real = jnp.where(first & ~left, 0.0, real)
                imag = jnp.where(first, jnp.where(left, 0.0, tile), imag)
            write(part * 16 + i, 0, real)
            write(part * 16 + i, 1, imag)


def adjoint_rows(read, write, half):
    for part in range(half // LANES):
        at = part * LANES
        re = swap_blocks([read(o, at) for o in range(16)])
        im = swap_blocks([read(o, half + at) for o in range(16)])
        for i in range(16):
            cross, wim = re[i], im[i]
            if part == 0 and i == 0:
                first = lax.broadcasted_iota(jnp.int32, wim.shape, 1) % F == 0
                cross = jnp.where(first, wim, cross)
                wim = jnp.where(first, 0.0, wim)
            write(part * 16 + i, 0, 0, re[i])
            write(part * 16 + i, 0, 1, wim)
            write(part * 16 + i, 1, 0, -wim)
            write(part * 16 + i, 1, 1, cross)


def diagonal():
    row = lax.broadcasted_iota(jnp.int32, (PAIR, LANES), 0)
    lane = lax.broadcasted_iota(jnp.int32, (PAIR, LANES), 1)
    return jnp.where(lane % F == row % F, 1.0, 0.0).astype(jnp.bfloat16)


def spread(read, count, mask):
    return jnp.concatenate(
        [jnp.concatenate([read(r), read(r + 1)], axis=0).astype(jnp.bfloat16) * mask for r in range(0, count, 2)], axis=0
    )


def blocks(first, second):
    zero = jnp.zeros_like(first)
    return jnp.concatenate(
        [jnp.concatenate([first, zero], axis=1), jnp.concatenate([zero, second], axis=1)], axis=0
    )


def side_by_side(values):
    return jnp.concatenate([values[..., :LANES], values[..., LANES:]], axis=-2)


def swiglu_back(gate, up, grad):
    sig = 1.0 / (1.0 + jnp.exp(-gate))
    gated = gate * sig
    slope = sig + gated * (1.0 - sig)
    return (
        (gated * up).astype(jnp.bfloat16),
        (grad * up * slope).astype(jnp.bfloat16),
        (grad * gated).astype(jnp.bfloat16),
    )


def main_kernel(fb, norm, wg_in, wu_in, pt_in, x_own_in, c_own_in, wd_own_in, wd_other_in, x_other_in, c_other_in,
                qf_in, pc_in, ps_in, d_out, gg_out, ug_out, wg_ref, wu_ref, pt_ref, x_own, c_own, wd_ref,
                x_other, c_other, qf_ref, pc_ref, ps_ref, sx, sc, gs, us, hs, hid, gg, ug, rg, ru, rd,
                sums_ref, diffs_ref, mids_ref, flat, flat_down, d_ref, in_sem, out_sem, d_sem):
    core = lax.axis_index("mp")
    db = 8
    per = db // 2
    block = pt_ref.shape[0]
    half = block // 2
    pairs = half // PAIR
    arrays = (
        (wg_in, wg_ref), (wu_in, wu_ref), (pt_in, pt_ref), (x_own_in, x_own), (c_own_in, c_own),
        (wd_own_in, wd_ref.at[core]), (wd_other_in, wd_ref.at[1 - core]),
        (x_other_in, x_other), (c_other_in, c_other),
        (qf_in, qf_ref), (pc_in, pc_ref), (ps_in, ps_ref),
    )
    copies = [pltpu.make_async_copy(src, dst, in_sem.at[n]) for n, (src, dst) in enumerate(arrays)]
    for copy in copies:
        copy.start()

    def to_spectra(source, target, first):
        rows = jnp.concatenate([source[:, j * block : (j + 1) * block] for j in range(per)], axis=0)
        result = nt_dot(pt_ref[...], rows).reshape(pairs, 2, 2, F, per * LANES)
        for j in range(0, per, 2):
            two = side_by_side(result[..., j * LANES : (j + 2) * LANES])
            target[:, :, :, first // 2 + j // 2] = two.astype(jnp.bfloat16)

    for copy in copies[:5]:
        copy.wait()
    to_spectra(x_own, sx, core * per)
    to_spectra(c_own, sc, core * per)
    for n, (source, target) in enumerate(((wg_ref, rg), (wu_ref, ru))):
        for tile in range(block // LANES):
            for o in range(fb):
                flat[n, tile, o * db : (o + 1) * db] = source[o, :, tile * LANES : (tile + 1) * LANES].astype(jnp.float32)

        def read(i, at, n=n):
            return flat[n, at // LANES, pl.ds(i, fb, stride=db), :]

        def write(group, ri, rows, target=target):
            at = (group * 2 + ri) * ROWS
            target[at : at + fb, :] = rows

        weight_rows(read, write, False, half)

    for copy in copies[5:9]:
        copy.wait()
    to_spectra(x_other, sx, (1 - core) * per)
    to_spectra(c_other, sc, (1 - core) * per)

    for o in range(db):
        for tile in range(block // LANES):
            flat_down[tile, o] = wd_ref[o // per, :, o % per, tile * LANES : (tile + 1) * LANES].astype(jnp.float32)

    def read_down(o, at):
        return flat_down[at // LANES, o, pl.ds(core * fb, fb), :]

    def write_down(group, ri, rows):
        at = (group * 2 + ri) * ROWS
        rd[at : at + fb, :] = rows

    weight_rows(read_down, write_down, True, half)
    if fb < ROWS:
        for target in (gg, ug):
            target[:, :, :, fb // 2 :] = jnp.zeros((pairs, 2, 2, (ROWS - fb) // 2, PAIR, LANES), jnp.bfloat16)

    mask = diagonal()

    def both_groups(ref, g):
        return blocks(*(ref[g, :, h].reshape(LANES, LANES) for h in range(2)))

    def mix(g):
        for source, weights in ((sx, ((rg, gs), (ru, us))), (sc, ((rd, hs),))):
            spectrum = both_groups(source, g)
            for rows, target in weights:
                wide = jnp.concatenate(
                    [
                        jnp.concatenate(
                            [
                                spread(
                                    lambda o, h=h, ri=ri, rows=rows: rows[
                                        pl.ds(((2 * g + h) * 2 + ri) * ROWS + o, F, stride=0), :
                                    ],
                                    fb,
                                    mask,
                                )
                                for h in range(2)
                            ],
                            axis=1,
                        )
                        for ri in range(2)
                    ],
                    axis=0,
                )
                result = side_by_side(dot(wide, spectrum).reshape(2, fb, F, 2 * LANES)).astype(jnp.bfloat16)
                for ri in range(2):
                    target[:, g, ri] = result[ri]

    @pl.loop(0, pairs // 4)
    def _(n):
        for u in range(4):
            mix(4 * n + u)

    for copy in copies[9:]:
        copy.wait()
    top = lax.broadcasted_iota(jnp.int32, (F, LANES), 0)
    wide_top = lax.broadcasted_iota(jnp.int32, (F, 2 * LANES), 0)
    signed = jnp.where(wide_top % 2 == 0, norm, -norm)
    inner = jnp.where(lax.broadcasted_iota(jnp.int32, (PAIR, 2 * LANES), 0) == 0, 0.0, 1.0).astype(jnp.bfloat16)

    def set_row(values, row):
        return jnp.concatenate([jnp.where(wide_top == 0, row, values[:F]), values[F:]], axis=0)

    def add_tile(values, tile):
        return (values.reshape(-1, F, 2 * LANES) + tile[None]).reshape(values.shape)

    def to_values(pair):
        spectra = jnp.concatenate(
            [ref[2 * pair + u].reshape(block, LANES) for ref in (gs, us, hs) for u in range(2)], axis=1
        )
        return dot(qf_ref[...], spectra)

    def to_grads(values, slot):
        gate, up, grad = (values[:, v * 2 * LANES : (v + 1) * 2 * LANES] for v in range(3))
        for v, side in enumerate(swiglu_back(gate, up, grad)):
            near, far = side[:half], side[half:]
            mids_ref[slot, v] = far[:PAIR].astype(jnp.float32)[:F]
            sums_ref[slot, v, :PAIR] = near[:PAIR] + far[:PAIR] * inner
            sums_ref[slot, v, PAIR:] = near[PAIR:] + far[PAIR:]
            diffs_ref[slot, v] = near - far

    def to_grad_spectra(pair, slot):
        re = dot(pc_ref[...], jnp.concatenate([sums_ref[slot, v] for v in range(3)], axis=1))
        im = dot(ps_ref[...], jnp.concatenate([diffs_ref[slot, v] for v in range(3)], axis=1))
        for v, target in enumerate((hid, gg, ug)):
            lanes = slice(v * 2 * LANES, (v + 1) * 2 * LANES)
            middle = mids_ref[slot, v][:1]
            real = add_tile(re[:half, lanes], middle * signed)
            imag = set_row(im[:, lanes], re[half : half + 1, lanes] + middle * norm)
            for ri, both in enumerate((real, imag)):
                target[:, ri, :, pair] = side_by_side(both.reshape(pairs, 2, F, 2 * LANES)).astype(jnp.bfloat16)

    steps = fb // 2
    to_grads(to_values(0), 0)

    @pl.loop(0, (steps - 1) // 2)
    def _(n):
        for u in range(2):
            values = to_values(2 * n + u + 1)
            to_grad_spectra(2 * n + u, u)
            to_grads(values, 1 - u)

    if steps % 2 == 0:
        to_grad_spectra(steps - 2, 0)
        to_grads(to_values(steps - 1), 1)
    to_grad_spectra(steps - 1, 1 - steps % 2)

    stores = [
        pltpu.make_async_copy(src, dst, out_sem.at[n]) for n, (src, dst) in enumerate(((gg, gg_out), (ug, ug_out)))
    ]
    for copy in stores:
        copy.start()
    lane = lax.broadcasted_iota(jnp.int32, (F, LANES), 1)
    left = lane < LANES // 2

    def weight_sums(g):
        for w, (rows, cols, sign) in enumerate(((gg, sx, 1), (ug, sx, 1), (hid, sc, -1))):
            two = jnp.concatenate([rows[g, :, h, : fb // 2].reshape(2 * fb * F, LANES) for h in range(2)], axis=1)
            m = nt_dot(two, both_groups(cols, g))
            for h in range(2):
                result = []
                for upper in range(0, fb, 8):
                    sums = [jnp.zeros((F, LANES), jnp.float32)] * 2
                    for o in range(upper, min(upper + 8, fb)):
                        turn = o - upper
                        here = (top - lane) % 8 == turn
                        for q in range(2):
                            tile = m[(q * fb + o) * F : (q * fb + o + 1) * F, h * LANES : (h + 1) * LANES]
                            sums[q] = jnp.where(here, pltpu.roll(tile, turn, 0) if turn else tile, sums[q])
                    same = jnp.where(left, sums[0], sums[1])
                    cross = jnp.where(left, sums[1], sums[0])
                    turned = pltpu.roll(cross, LANES // 2, 1)
                    both = jnp.where(
                        left, same + pltpu.roll(same, LANES // 2, 1), turned - cross if sign > 0 else cross - turned
                    )
                    if h == 0:
                        both = jnp.where((lane % F == 0) & (g == 0), same, both)
                    result.append(both)
                d_ref[g, w * ROWS : (w + 1) * ROWS, h * LANES : (h + 1) * LANES] = jnp.concatenate(
                    result, axis=0
                ).astype(jnp.bfloat16)

    def sums_copy(n):
        rows = pl.ds(4 * n, 4)
        return pltpu.make_async_copy(d_ref.at[rows], d_out.at[rows], d_sem.at[n])

    @pl.loop(0, pairs // 4)
    def _(n):
        for u in range(4):
            weight_sums(4 * n + u)
        sums_copy(n).start()

    for n in range(pairs // 4):
        sums_copy(n).wait()
    for copy in stores:
        copy.wait()


def adjoint_kernel(fb, wg_in, wu_in, gg_in, ug_in, own_out, other_out, wg_ref, wu_ref, gg, ug, ra, rb, part, own_ref,
                   other_ref, in_sem, g_sem, out_sem):
    core = lax.axis_index("mp")
    db = 8
    per = db // 2
    pairs = gg.shape[0]
    half = pairs * PAIR
    weights = [
        pltpu.make_async_copy(src, dst, in_sem.at[n]) for n, (src, dst) in enumerate(((wg_in, wg_ref), (wu_in, wu_ref)))
    ]

    def group_copies(g):
        return [
            pltpu.make_async_copy(src.at[g], dst.at[g], g_sem.at[n, g])
            for n, (src, dst) in enumerate(((gg_in, gg), (ug_in, ug)))
        ]

    def results(n):
        rows = pl.ds(2 * n, 2)
        return [
            pltpu.make_async_copy(src.at[rows], dst.at[rows], out_sem.at[k, n])
            for k, (src, dst) in enumerate(((own_ref, own_out), (other_ref, other_out)))
        ]

    for copy in weights:
        copy.start()
    for g in range(pairs):
        for copy in group_copies(g):
            copy.start()
    for copy in weights:
        copy.wait()
    for source, adjoint in ((wg_ref, ra), (wu_ref, rb)):
        def read(o, at, source=source):
            if o >= fb:
                return jnp.zeros((db, LANES), jnp.float32)
            return source[o, :, at : at + LANES].astype(jnp.float32)

        def write(group, ri, tile, rows, adjoint=adjoint):
            at = (group * 2 + ri) * db
            adjoint[tile, at : at + db, :] = rows

        adjoint_rows(read, write, half)
    mask = diagonal()

    def mix(g, slot):
        spectrum = jnp.concatenate([blocks(*(ref[g, :, h].reshape(2 * LANES, LANES) for h in range(2))) for ref in (gg, ug)])
        wide = jnp.concatenate(
            [
                spread(
                    lambda r, h=h, tile=tile, ref=ref: ref[tile, pl.ds((2 * g + h) * 2 * db + r, F, stride=0), :],
                    2 * db,
                    mask,
                )
                for ref in (ra, rb)
                for h in range(2)
                for tile in range(2)
            ],
            axis=1,
        )
        part[slot] = side_by_side(dot(wide, spectrum).reshape(2, db, F, 2 * LANES))
        for ri in range(2):
            own_ref[g, ri] = part[slot, ri, pl.ds(core * per, per)]
            other_ref[g, ri] = part[slot, ri, pl.ds((1 - core) * per, per)].astype(jnp.bfloat16)

    @pl.loop(0, pairs // 2)
    def _(n):
        for u in range(2):
            for copy in group_copies(2 * n + u):
                copy.wait()
        for u in range(2):
            mix(2 * n + u, u)
        for copy in results(n):
            copy.start()

    for n in range(pairs // 2):
        for copy in results(n):
            copy.wait()


def input_kernel(qt_in, own_in, got_in, out_ref, qt_ref, own_ref, got_ref, in_sem):
    block = qt_ref.shape[0]
    copies = [
        pltpu.make_async_copy(src, dst, in_sem.at[n])
        for n, (src, dst) in enumerate(((qt_in, qt_ref), (own_in, own_ref), (got_in, got_ref)))
    ]
    for copy in copies:
        copy.start()
    for copy in copies:
        copy.wait()
    spectra = (own_ref[...] + got_ref[...].astype(jnp.float32)).astype(jnp.bfloat16)
    for j in range(0, own_ref.shape[2], 2):
        two = jnp.concatenate([spectra[:, :, j + u].reshape(block, LANES) for u in range(2)], axis=1)
        values = dot(qt_ref[...], two)
        for u in range(2):
            out_ref[:, (j + u) * block : (j + u + 1) * block] = values[:, u * LANES : (u + 1) * LANES].T.astype(jnp.bfloat16)


def straight(tile):
    halves = []
    lane = lax.broadcasted_iota(jnp.int32, (8, LANES), 1)
    for at in range(0, tile.shape[0], 8):
        half = tile[at : at + 8]
        for bit in (1, 2, 4):
            half = jnp.where((lane & bit) != 0, pltpu.roll(half, 8 - bit, 0), half)
        halves.append(half)
    return jnp.concatenate(halves, axis=0)


def reduce_kernel(r_ref, out_ref):
    for g in range(r_ref.shape[1]):
        for lanes in (slice(0, LANES), slice(LANES, 2 * LANES)):
            total = r_ref[0, g, :, lanes].astype(jnp.float32)
            for d in range(1, r_ref.shape[0]):
                total = total + r_ref[d, g, :, lanes].astype(jnp.float32)
            total = straight(total).astype(jnp.bfloat16)
            for d in range(out_ref.shape[0]):
                out_ref[d, g, :, lanes] = total


def entries(source, rows, part):
    tiles = []
    for i in range(16):
        lanes = slice((i % 2) * LANES, (i % 2 + 1) * LANES)
        tiles.append(source[part * 8 + i // 2, rows, lanes].astype(jnp.float32))
    return swap_blocks(tiles)


def factor(scale, part):
    lane = lax.broadcasted_iota(jnp.int32, (1, LANES), 1)
    return jnp.where((lane == 0) & (part == 0), scale, 2.0 * scale)


def layout_kernel(scale, fb, s_ref, gate_ref, up_ref, flat):
    half = s_ref.shape[0] * PAIR
    for w, target in enumerate((gate_ref, up_ref)):
        for part in range(half // LANES):
            tiles = entries(s_ref, slice(w * ROWS, (w + 1) * ROWS), part)
            for ri in range(2):
                at = ri * half + part * LANES
                for i in range(8):
                    flat[w, ri, pl.ds(i, fb, stride=8), :] = tiles[8 * ri + i][:fb] * factor(scale, part)
                target[:, at : at + LANES] = flat[w, ri]


def down_layout_kernel(scale, fb, own_ref, got_ref, down_ref):
    core = lax.axis_index("mp")
    half = own_ref.shape[0] * PAIR
    outputs = down_ref.shape[1]
    for source, h in ((own_ref, core), (got_ref, 1 - core)):
        for part in range(half // LANES):
            tiles = entries(source, slice(0, ROWS), part)
            for ri in range(2):
                at = ri * half + part * LANES
                for o in range(outputs):
                    rows = jnp.where(core == 0, tiles[8 * ri + o], tiles[8 * ri + outputs + o])
                    down_ref[pl.ds(h * fb, fb), o, at : at + LANES] = rows[:fb] * factor(scale, part)


ALL_VMEM = 67043328


VMEM = pl.BlockSpec(memory_space=pltpu.VMEM)
HBM = pl.BlockSpec(memory_space=pltpu.HBM)


def call(kernel, out_shape, args, scratch=(), limit=16 << 20, flops=0, moved=0, in_specs=None, out_specs=None):
    return pl.pallas_call(
        kernel,
        out_shape=out_shape,
        in_specs=in_specs or [VMEM] * len(args),
        out_specs=out_specs or jax.tree.map(lambda _: VMEM, out_shape),
        scratch_shapes=list(scratch),
        compiler_params=pltpu.CompilerParams(vmem_limit_bytes=limit),
        cost_estimate=pl.CostEstimate(flops=flops, bytes_accessed=moved, transcendentals=0),
    )(*args)


def shards(tokens, cotangent, gate_spectra, up_spectra, down_spectra):
    n_dp = lax.axis_size("dp")
    swap = [(0, 1), (1, 0)]
    fb, db, block = gate_spectra.shape
    assert db == 8 and fb <= ROWS and fb % 2 == 0 and tokens.shape[0] == LANES and lax.axis_size("mp") == 2
    half = block // 2
    pairs = half // PAIR
    groups = half // F
    per = db // 2
    bf16, f32 = jnp.bfloat16, jnp.float32
    shape = jax.ShapeDtypeStruct
    pt, qt, qf, pc, ps = transform_tables(block)
    norm = float(np.asarray(1.0 / math.sqrt(block), jnp.bfloat16))

    tokens_other = lax.ppermute(tokens, "mp", swap)
    cotangent_other = lax.ppermute(cotangent, "mp", swap)
    down_own = down_spectra.transpose(1, 0, 2)
    down_got = lax.ppermute(down_own, "mp", swap)

    inputs = (
        gate_spectra, up_spectra, pt, tokens, cotangent, down_own, down_got, tokens_other, cotangent_other, qf, pc, ps
    )
    buffers = [shape((2,) + down_own.shape, bf16) if n == 5 else a for n, a in enumerate(inputs) if n != 6]
    spec = shape((pairs, 2, 2, ROWS // 2, PAIR, LANES), bf16)
    d_all, gg, ug = call(
        functools.partial(main_kernel, fb, norm),
        (shape((pairs, 3 * ROWS, 2 * LANES), bf16), spec, spec),
        inputs,
        [pltpu.VMEM(a.shape, bf16) for a in buffers]
        + [pltpu.VMEM((pairs, 2, 2, db // 2, PAIR, LANES), bf16)] * 2
        + [pltpu.VMEM((fb, pairs, 2, PAIR, LANES), bf16)] * 3
        + [pltpu.VMEM(spec.shape, bf16)] * 3
        + [pltpu.VMEM((groups * 2 * ROWS, LANES), f32)] * 3
        + [pltpu.VMEM((2, 3, half, 2 * LANES), bf16)] * 2
        + [pltpu.VMEM((2, 3, F, 2 * LANES), f32), pltpu.VMEM((2, block // LANES, fb * db, LANES), f32)]
        + [pltpu.VMEM((block // LANES, db, 2 * fb, LANES), f32), pltpu.VMEM((pairs, 3 * ROWS, 2 * LANES), bf16)]
        + [pltpu.SemaphoreType.DMA((n,)) for n in (len(inputs), 2, pairs // 4)],
        limit=ALL_VMEM,
        flops=10**10,
        moved=10**7,
        in_specs=[HBM] * len(inputs),
        out_specs=(HBM, HBM, HBM),
    )

    direct = pairs % n_dp == 0
    if direct:
        share = pairs // n_dp
        got = lax.all_to_all(d_all.reshape(n_dp, share, 3 * ROWS, 2 * LANES), "dp", 0, 0, tiled=True)
    else:
        share = pairs
        got = lax.psum(d_all.astype(f32), "dp")[None]
    own, other = call(
        functools.partial(adjoint_kernel, fb),
        (shape((pairs, 2, per, PAIR, LANES), f32), shape((pairs, 2, per, PAIR, LANES), bf16)),
        (gate_spectra, up_spectra, gg, ug),
        [pltpu.VMEM(gate_spectra.shape, bf16)] * 2
        + [pltpu.VMEM(spec.shape, bf16)] * 2
        + [pltpu.VMEM((2, groups * 2 * db, LANES), f32)] * 2
        + [pltpu.VMEM((2, 2, db, PAIR, LANES), f32)]
        + [pltpu.VMEM((pairs, 2, per, PAIR, LANES), t) for t in (f32, bf16)]
        + [pltpu.SemaphoreType.DMA(n) for n in ((2,), (2, pairs), (2, pairs // 2))],
        limit=63 << 20,
        flops=2 * 10**9,
        moved=10**7,
        in_specs=[HBM] * 4,
        out_specs=(HBM, HBM),
    )
    total = call(reduce_kernel, shape((n_dp if direct else 1, share, 3 * ROWS, 2 * LANES), bf16), (got,), moved=10**6)
    total, own, other = lax.optimization_barrier((total, own, other))
    if direct:
        total = lax.all_to_all(total, "dp", 0, 0, tiled=True)
    partner = lax.ppermute(other, "mp", swap)
    grad_tokens = call(
        input_kernel,
        shape(tokens.shape, bf16),
        (qt, own, partner),
        [pltpu.VMEM(a.shape, a.dtype) for a in (qt, own, partner)] + [pltpu.SemaphoreType.DMA((3,))],
        limit=12 << 20,
        flops=5 * 10**8,
        moved=4 * 10**6,
        in_specs=[HBM] * 3,
    )
    total = total.reshape(pairs, 3 * ROWS, 2 * LANES)
    down_sums = total[:, 2 * ROWS :]
    partner_sums = lax.ppermute(down_sums, "mp", swap)
    scale = 1.0 / math.sqrt(tokens.shape[0] * n_dp)
    gate_grad, up_grad = call(
        functools.partial(layout_kernel, scale, fb),
        (shape((fb * db, block), f32),) * 2,
        (total,),
        [pltpu.VMEM((2, 2, fb * db, LANES), f32)],
        moved=10**6,
    )
    down_grad = call(
        functools.partial(down_layout_kernel, scale, fb),
        shape((2 * fb, per, block), f32),
        (down_sums, partner_sums),
        moved=10**6,
    ).transpose(1, 0, 2)
    return (grad_tokens, gate_grad.reshape(fb, db, block), up_grad.reshape(fb, db, block), down_grad)


def solution(mesh):
    in_specs = (
        P(("groups", "dp"), "mp"),
        P(("groups", "dp"), "mp"),
        P("mp", None, None),
        P("mp", None, None),
        P("mp", None, None),
    )
    out_specs = (
        P(("groups", "dp"), "mp"),
        P(("groups", "mp"), None, None),
        P(("groups", "mp"), None, None),
        P(("groups", "mp"), None, None),
    )
    return jax.shard_map(shards, mesh=mesh, in_specs=in_specs, out_specs=out_specs, check_vma=False)
```

```python
import functools
import math

import jax
import jax.numpy as jnp
import numpy as np
from jax import lax
from jax.experimental import pallas as pl
from jax.experimental.pallas import tpu as pltpu
from jax.sharding import PartitionSpec as P


F = 8
PAIR = 2 * F
LANES = 128
ROWS = 16


def transform_tables(block):
    half = block // 2
    n = np.arange(block)
    k = np.arange(half)
    angles = ((n[:, None] * k[None, :]) % block).astype(np.float32) * np.float32(2.0 * math.pi / block)
    cosine = np.cos(angles.astype(np.float64)).astype(np.float32)
    sine = np.sin(angles.astype(np.float64)).astype(np.float32)
    parity = (1 - 2 * (n % 2)).astype(np.float32)
    norm = np.float32(1.0 / math.sqrt(block))
    forward = np.concatenate([cosine, parity[:, None], -sine[:, 1:]], axis=1) * norm
    doubling = np.where(k >= 1, 2.0, 1.0).astype(np.float32)
    inverse = np.concatenate([(cosine * doubling).T, parity[None, :], -2.0 * sine[:, 1:].T], axis=0) * norm
    order = np.arange(block).reshape(2, half // PAIR, PAIR).transpose(1, 0, 2).reshape(-1)
    extra = np.zeros((16, half), np.float32)
    folded = np.concatenate([np.arange(half), [half], np.arange(block - 1, half, -1)])
    forward_cos = np.concatenate([forward[:half, :half].T, extra], axis=0)
    forward_cos[half] = forward[:half, half]
    forward_sin = forward[:half, half:].T.copy()
    forward_sin[0] = 0.0
    natural = inverse.T[:, order]
    tables = (forward.T[order], natural, natural[folded], forward_cos, forward_sin)
    return [jnp.asarray(table, jnp.bfloat16) for table in tables]


def nt_dot(a, b):
    return lax.dot_general(a, b, (((1,), (1,)), ((), ())), preferred_element_type=jnp.float32)


def dot(a, b):
    return jnp.dot(a, b, preferred_element_type=jnp.float32)


def swap_blocks(tiles):
    tiles = list(tiles)
    lane_block = lax.broadcasted_iota(jnp.int32, tiles[0].shape, 1) // F
    step = len(tiles) // 2
    while step:
        high = (lane_block & step) != 0
        for i in range(len(tiles)):
            if i & step:
                continue
            low_tile, high_tile = tiles[i], tiles[i + step]
            tiles[i] = jnp.where(high, pltpu.roll(high_tile, F * step, 1), low_tile)
            tiles[i + step] = jnp.where(high, high_tile, pltpu.roll(low_tile, LANES - F * step, 1))
        step //= 2
    return tiles


def weight_rows(read, write, conj, half):
    for part in range(half // LANES):
        at = part * LANES
        tiles = swap_blocks([read(i, at) for i in range(8)] + [read(i, half + at) for i in range(8)])
        for i, tile in enumerate(tiles):
            lane = lax.broadcasted_iota(jnp.int32, tile.shape, 1)
            left = lane < LANES // 2
            turned = pltpu.roll(tile, LANES // 2, 1)
            if conj:
                real, imag = tile, jnp.where(left, -turned, turned)
            else:
                real, imag = jnp.where(left, tile, -tile), turned
            if part == 0 and i == 0:
                first = lane % F == 0
                real = jnp.where(first & ~left, 0.0, real)
                imag = jnp.where(first, jnp.where(left, 0.0, tile), imag)
            write(part * 16 + i, 0, real)
            write(part * 16 + i, 1, imag)


def adjoint_rows(read, write, half):
    for part in range(half // LANES):
        at = part * LANES
        re = swap_blocks([read(o, at) for o in range(16)])
        im = swap_blocks([read(o, half + at) for o in range(16)])
        for i in range(16):
            cross, wim = re[i], im[i]
            if part == 0 and i == 0:
                first = lax.broadcasted_iota(jnp.int32, wim.shape, 1) % F == 0
                cross = jnp.where(first, wim, cross)
                wim = jnp.where(first, 0.0, wim)
            write(part * 16 + i, 0, 0, re[i])
            write(part * 16 + i, 0, 1, wim)
            write(part * 16 + i, 1, 0, -wim)
            write(part * 16 + i, 1, 1, cross)


def diagonal():
    row = lax.broadcasted_iota(jnp.int32, (PAIR, LANES), 0)
    lane = lax.broadcasted_iota(jnp.int32, (PAIR, LANES), 1)
    return jnp.where(lane % F == row % F, 1.0, 0.0).astype(jnp.bfloat16)


def spread(read, count, mask):
    return jnp.concatenate(
        [jnp.concatenate([read(r), read(r + 1)], axis=0).astype(jnp.bfloat16) * mask for r in range(0, count, 2)], axis=0
    )


def blocks(first, second):
    zero = jnp.zeros_like(first)
    return jnp.concatenate(
        [jnp.concatenate([first, zero], axis=1), jnp.concatenate([zero, second], axis=1)], axis=0
    )


def side_by_side(values):
    return jnp.concatenate([values[..., :LANES], values[..., LANES:]], axis=-2)


def swiglu_back(gate, up, grad):
    sig = 1.0 / (1.0 + jnp.exp(-gate))
    gated = gate * sig
    slope = sig + gated * (1.0 - sig)
    return (
        (gated * up).astype(jnp.bfloat16),
        (grad * up * slope).astype(jnp.bfloat16),
        (grad * gated).astype(jnp.bfloat16),
    )


def main_kernel(fb, norm, wg_in, wu_in, pt_in, x_own_in, c_own_in, wd_own_in, wd_other_in, x_other_in, c_other_in,
                qf_in, pc_in, ps_in, d_out, gg_out, ug_out, wg_ref, wu_ref, pt_ref, x_own, c_own, wd_ref,
                x_other, c_other, qf_ref, pc_ref, ps_ref, sx, sc, gs, us, hs, hid, gg, ug, rg, ru, rd,
                sums_ref, diffs_ref, mids_ref, flat, flat_down, d_ref, in_sem, out_sem, d_sem):
    core = lax.axis_index("mp")
    db = 8
    per = db // 2
    block = pt_ref.shape[0]
    half = block // 2
    pairs = half // PAIR
    arrays = (
        (wg_in, wg_ref), (wu_in, wu_ref), (pt_in, pt_ref), (x_own_in, x_own), (c_own_in, c_own),
        (wd_own_in, wd_ref.at[core]), (wd_other_in, wd_ref.at[1 - core]),
        (x_other_in, x_other), (c_other_in, c_other),
        (qf_in, qf_ref), (pc_in, pc_ref), (ps_in, ps_ref),
    )
    copies = [pltpu.make_async_copy(src, dst, in_sem.at[n]) for n, (src, dst) in enumerate(arrays)]
    for copy in copies:
        copy.start()

    def to_spectra(source, target, first):
        rows = jnp.concatenate([source[:, j * block : (j + 1) * block] for j in range(per)], axis=0)
        result = nt_dot(pt_ref[...], rows).reshape(pairs, 2, 2, F, per * LANES)
        for j in range(0, per, 2):
            two = side_by_side(result[..., j * LANES : (j + 2) * LANES])
            target[:, :, :, first // 2 + j // 2] = two.astype(jnp.bfloat16)

    for copy in copies[:5]:
        copy.wait()
    to_spectra(x_own, sx, core * per)
    to_spectra(c_own, sc, core * per)
    for n, (source, target) in enumerate(((wg_ref, rg), (wu_ref, ru))):
        for tile in range(block // LANES):
            for o in range(fb):
                flat[n, tile, o * db : (o + 1) * db] = source[o, :, tile * LANES : (tile + 1) * LANES].astype(jnp.float32)

        def read(i, at, n=n):
            return flat[n, at // LANES, pl.ds(i, fb, stride=db), :]

        def write(group, ri, rows, target=target):
            at = (group * 2 + ri) * ROWS
            target[at : at + fb, :] = rows

        weight_rows(read, write, False, half)

    for copy in copies[5:9]:
        copy.wait()
    to_spectra(x_other, sx, (1 - core) * per)
    to_spectra(c_other, sc, (1 - core) * per)

    for side in range(2):
        for tile in range(block // LANES):
            rows = wd_ref[side, :, :, tile * LANES : (tile + 1) * LANES].astype(jnp.float32)
            flat_down[side, tile] = rows.reshape(2 * fb * per, LANES)

    def read_down(o, at):
        return flat_down[o // per, at // LANES, pl.ds(core * fb * per + o % per, fb, stride=per), :]

    def write_down(group, ri, rows):
        at = (group * 2 + ri) * ROWS
        rd[at : at + fb, :] = rows

    weight_rows(read_down, write_down, True, half)
    if fb < ROWS:
        for target in (gg, ug):
            target[:, :, :, fb // 2 :] = jnp.zeros((pairs, 2, 2, (ROWS - fb) // 2, PAIR, LANES), jnp.bfloat16)

    mask = diagonal()

    def both_groups(ref, g):
        return blocks(*(ref[g, :, h].reshape(LANES, LANES) for h in range(2)))

    def mix(g):
        for source, weights in ((sx, ((rg, gs), (ru, us))), (sc, ((rd, hs),))):
            spectrum = both_groups(source, g)
            for rows, target in weights:
                wide = jnp.concatenate(
                    [
                        jnp.concatenate(
                            [
                                spread(
                                    lambda o, h=h, ri=ri, rows=rows: rows[
                                        pl.ds(((2 * g + h) * 2 + ri) * ROWS + o, F, stride=0), :
                                    ],
                                    fb,
                                    mask,
                                )
                                for h in range(2)
                            ],
                            axis=1,
                        )
                        for ri in range(2)
                    ],
                    axis=0,
                )
                result = side_by_side(dot(wide, spectrum).reshape(2, fb, F, 2 * LANES)).astype(jnp.bfloat16)
                for ri in range(2):
                    target[:, g, ri] = result[ri]

    @pl.loop(0, pairs // 8)
    def _(n):
        for u in range(8):
            mix(8 * n + u)

    for copy in copies[9:]:
        copy.wait()
    top = lax.broadcasted_iota(jnp.int32, (F, LANES), 0)
    wide_top = lax.broadcasted_iota(jnp.int32, (F, 2 * LANES), 0)
    signed = jnp.where(wide_top % 2 == 0, norm, -norm)
    inner = jnp.where(lax.broadcasted_iota(jnp.int32, (PAIR, 2 * LANES), 0) == 0, 0.0, 1.0).astype(jnp.bfloat16)

    def set_row(values, row):
        return jnp.concatenate([jnp.where(wide_top == 0, row, values[:F]), values[F:]], axis=0)

    def add_tile(values, tile):
        return (values.reshape(-1, F, 2 * LANES) + tile[None]).reshape(values.shape)

    def to_values(pair):
        spectra = jnp.concatenate(
            [ref[2 * pair + u].reshape(block, LANES) for ref in (gs, us, hs) for u in range(2)], axis=1
        )
        return dot(qf_ref[...], spectra)

    def to_grads(values, slot):
        gate, up, grad = (values[:, v * 2 * LANES : (v + 1) * 2 * LANES] for v in range(3))
        for v, side in enumerate(swiglu_back(gate, up, grad)):
            near, far = side[:half], side[half:]
            mids_ref[slot, v] = far[:PAIR].astype(jnp.float32)[:F]
            sums_ref[slot, v, :PAIR] = near[:PAIR] + far[:PAIR] * inner
            sums_ref[slot, v, PAIR:] = near[PAIR:] + far[PAIR:]
            diffs_ref[slot, v] = near - far

    def to_grad_spectra(pair, slot):
        re = dot(pc_ref[...], jnp.concatenate([sums_ref[slot, v] for v in range(3)], axis=1))
        im = dot(ps_ref[...], jnp.concatenate([diffs_ref[slot, v] for v in range(3)], axis=1))
        for v, target in enumerate((hid, gg, ug)):
            lanes = slice(v * 2 * LANES, (v + 1) * 2 * LANES)
            middle = mids_ref[slot, v][:1]
            real = add_tile(re[:half, lanes], middle * signed)
            imag = set_row(im[:, lanes], re[half : half + 1, lanes] + middle * norm)
            for ri, both in enumerate((real, imag)):
                target[:, ri, :, pair] = side_by_side(both.reshape(pairs, 2, F, 2 * LANES)).astype(jnp.bfloat16)

    steps = fb // 2
    to_grads(to_values(0), 0)

    @pl.loop(0, (steps - 1) // 2)
    def _(n):
        for u in range(2):
            values = to_values(2 * n + u + 1)
            to_grad_spectra(2 * n + u, u)
            to_grads(values, 1 - u)

    if steps % 2 == 0:
        to_grad_spectra(steps - 2, 0)
        to_grads(to_values(steps - 1), 1)
    to_grad_spectra(steps - 1, 1 - steps % 2)

    stores = [
        pltpu.make_async_copy(src, dst, out_sem.at[n]) for n, (src, dst) in enumerate(((gg, gg_out), (ug, ug_out)))
    ]
    for copy in stores:
        copy.start()
    lane = lax.broadcasted_iota(jnp.int32, (F, LANES), 1)
    left = lane < LANES // 2

    def weight_sums(g):
        for w, (rows, cols, sign) in enumerate(((gg, sx, 1), (ug, sx, 1), (hid, sc, -1))):
            two = jnp.concatenate([rows[g, :, h, : fb // 2].reshape(2 * fb * F, LANES) for h in range(2)], axis=1)
            m = nt_dot(two, both_groups(cols, g))
            for h in range(2):
                result = []
                for upper in range(0, fb, 8):
                    sums = [jnp.zeros((F, LANES), jnp.float32)] * 2
                    for o in range(upper, min(upper + 8, fb)):
                        turn = o - upper
                        here = (top - lane) % 8 == turn
                        for q in range(2):
                            tile = m[(q * fb + o) * F : (q * fb + o + 1) * F, h * LANES : (h + 1) * LANES]
                            sums[q] = jnp.where(here, pltpu.roll(tile, turn, 0) if turn else tile, sums[q])
                    same = jnp.where(left, sums[0], sums[1])
                    cross = jnp.where(left, sums[1], sums[0])
                    turned = pltpu.roll(cross, LANES // 2, 1)
                    both = jnp.where(
                        left, same + pltpu.roll(same, LANES // 2, 1), turned - cross if sign > 0 else cross - turned
                    )
                    if h == 0:
                        both = jnp.where((lane % F == 0) & (g == 0), same, both)
                    result.append(both)
                d_ref[g, w * ROWS : (w + 1) * ROWS, h * LANES : (h + 1) * LANES] = jnp.concatenate(
                    result, axis=0
                ).astype(jnp.bfloat16)

    def sums_copy(n):
        rows = pl.ds(8 * n, 8)
        return pltpu.make_async_copy(d_ref.at[rows], d_out.at[rows], d_sem.at[n])

    @pl.loop(0, pairs // 8)
    def _(n):
        for u in range(8):
            weight_sums(8 * n + u)
        sums_copy(n).start()

    for n in range(pairs // 8):
        sums_copy(n).wait()
    for copy in stores:
        copy.wait()


def adjoint_kernel(fb, wg_in, wu_in, gg_in, ug_in, own_out, other_out, wg_ref, wu_ref, gg, ug, ra, rb, part, own_ref,
                   other_ref, in_sem, g_sem, out_sem):
    core = lax.axis_index("mp")
    db = 8
    per = db // 2
    pairs = gg.shape[0]
    half = pairs * PAIR
    weights = [
        pltpu.make_async_copy(src, dst, in_sem.at[n]) for n, (src, dst) in enumerate(((wg_in, wg_ref), (wu_in, wu_ref)))
    ]

    def group_copies(g):
        return [
            pltpu.make_async_copy(src.at[g], dst.at[g], g_sem.at[n, g])
            for n, (src, dst) in enumerate(((gg_in, gg), (ug_in, ug)))
        ]

    def results(n):
        rows = pl.ds(2 * n, 2)
        return [
            pltpu.make_async_copy(src.at[rows], dst.at[rows], out_sem.at[k, n])
            for k, (src, dst) in enumerate(((own_ref, own_out), (other_ref, other_out)))
        ]

    for copy in weights:
        copy.start()
    for g in range(pairs):
        for copy in group_copies(g):
            copy.start()
    for copy in weights:
        copy.wait()
    for source, adjoint in ((wg_ref, ra), (wu_ref, rb)):
        def read(o, at, source=source):
            if o >= fb:
                return jnp.zeros((db, LANES), jnp.float32)
            return source[o, :, at : at + LANES].astype(jnp.float32)

        def write(group, ri, tile, rows, adjoint=adjoint):
            at = (group * 2 + ri) * db
            adjoint[tile, at : at + db, :] = rows

        adjoint_rows(read, write, half)
    mask = diagonal()

    def mix(g, slot):
        spectrum = jnp.concatenate([blocks(*(ref[g, :, h].reshape(2 * LANES, LANES) for h in range(2))) for ref in (gg, ug)])
        wide = jnp.concatenate(
            [
                spread(
                    lambda r, h=h, tile=tile, ref=ref: ref[tile, pl.ds((2 * g + h) * 2 * db + r, F, stride=0), :],
                    2 * db,
                    mask,
                )
                for ref in (ra, rb)
                for h in range(2)
                for tile in range(2)
            ],
            axis=1,
        )
        part[slot] = side_by_side(dot(wide, spectrum).reshape(2, db, F, 2 * LANES))
        for ri in range(2):
            own_ref[g, ri] = part[slot, ri, pl.ds(core * per, per)]
            other_ref[g, ri] = part[slot, ri, pl.ds((1 - core) * per, per)].astype(jnp.bfloat16)

    @pl.loop(0, pairs // 2)
    def _(n):
        for u in range(2):
            for copy in group_copies(2 * n + u):
                copy.wait()
        for u in range(2):
            mix(2 * n + u, u)
        for copy in results(n):
            copy.start()

    for n in range(pairs // 2):
        for copy in results(n):
            copy.wait()


def input_kernel(qt_in, own_in, got_in, out_ref, qt_ref, own_ref, got_ref, in_sem):
    block = qt_ref.shape[0]
    copies = [
        pltpu.make_async_copy(src, dst, in_sem.at[n])
        for n, (src, dst) in enumerate(((qt_in, qt_ref), (own_in, own_ref), (got_in, got_ref)))
    ]
    for copy in copies:
        copy.start()
    for copy in copies:
        copy.wait()
    spectra = (own_ref[...] + got_ref[...].astype(jnp.float32)).astype(jnp.bfloat16)
    for j in range(0, own_ref.shape[2], 2):
        two = jnp.concatenate([spectra[:, :, j + u].reshape(block, LANES) for u in range(2)], axis=1)
        values = dot(qt_ref[...], two)
        for u in range(2):
            out_ref[:, (j + u) * block : (j + u + 1) * block] = values[:, u * LANES : (u + 1) * LANES].T.astype(jnp.bfloat16)


def straight(tile):
    halves = []
    lane = lax.broadcasted_iota(jnp.int32, (8, LANES), 1)
    for at in range(0, tile.shape[0], 8):
        half = tile[at : at + 8]
        for bit in (1, 2, 4):
            half = jnp.where((lane & bit) != 0, pltpu.roll(half, 8 - bit, 0), half)
        halves.append(half)
    return jnp.concatenate(halves, axis=0)


def reduce_kernel(r_ref, out_ref):
    for g in range(r_ref.shape[1]):
        for lanes in (slice(0, LANES), slice(LANES, 2 * LANES)):
            total = r_ref[0, g, :, lanes].astype(jnp.float32)
            for d in range(1, r_ref.shape[0]):
                total = total + r_ref[d, g, :, lanes].astype(jnp.float32)
            total = straight(total).astype(jnp.bfloat16)
            for d in range(out_ref.shape[0]):
                out_ref[d, g, :, lanes] = total


def entries(source, rows, part):
    tiles = []
    for i in range(16):
        lanes = slice((i % 2) * LANES, (i % 2 + 1) * LANES)
        tiles.append(source[part * 8 + i // 2, rows, lanes].astype(jnp.float32))
    return swap_blocks(tiles)


def factor(scale, part):
    lane = lax.broadcasted_iota(jnp.int32, (1, LANES), 1)
    return jnp.where((lane == 0) & (part == 0), scale, 2.0 * scale)


def layout_kernel(scale, fb, s_ref, gate_ref, up_ref, flat):
    half = s_ref.shape[0] * PAIR
    for w, target in enumerate((gate_ref, up_ref)):
        for part in range(half // LANES):
            tiles = entries(s_ref, slice(w * ROWS, (w + 1) * ROWS), part)
            for ri in range(2):
                at = ri * half + part * LANES
                for i in range(8):
                    flat[w, ri, pl.ds(i, fb, stride=8), :] = tiles[8 * ri + i][:fb] * factor(scale, part)
                target[:, at : at + LANES] = flat[w, ri]


def down_layout_kernel(scale, fb, own_ref, got_ref, down_ref):
    core = lax.axis_index("mp")
    half = own_ref.shape[0] * PAIR
    outputs = down_ref.shape[1]
    for source, h in ((own_ref, core), (got_ref, 1 - core)):
        for part in range(half // LANES):
            tiles = entries(source, slice(2 * ROWS, 3 * ROWS), part)
            for ri in range(2):
                at = ri * half + part * LANES
                for o in range(outputs):
                    rows = jnp.where(core == 0, tiles[8 * ri + o], tiles[8 * ri + outputs + o])
                    down_ref[pl.ds(h * fb, fb), o, at : at + LANES] = rows[:fb] * factor(scale, part)


ALL_VMEM = 67043328


VMEM = pl.BlockSpec(memory_space=pltpu.VMEM)
HBM = pl.BlockSpec(memory_space=pltpu.HBM)


def call(kernel, out_shape, args, scratch=(), limit=16 << 20, flops=0, moved=0, in_specs=None, out_specs=None):
    return pl.pallas_call(
        kernel,
        out_shape=out_shape,
        in_specs=in_specs or [VMEM] * len(args),
        out_specs=out_specs or jax.tree.map(lambda _: VMEM, out_shape),
        scratch_shapes=list(scratch),
        compiler_params=pltpu.CompilerParams(vmem_limit_bytes=limit),
        cost_estimate=pl.CostEstimate(flops=flops, bytes_accessed=moved, transcendentals=0),
    )(*args)


def shards(tokens, cotangent, gate_spectra, up_spectra, down_spectra):
    n_dp = lax.axis_size("dp")
    swap = [(0, 1), (1, 0)]
    fb, db, block = gate_spectra.shape
    assert db == 8 and fb <= ROWS and fb % 2 == 0 and tokens.shape[0] == LANES and lax.axis_size("mp") == 2
    half = block // 2
    pairs = half // PAIR
    groups = half // F
    per = db // 2
    bf16, f32 = jnp.bfloat16, jnp.float32
    shape = jax.ShapeDtypeStruct
    pt, qt, qf, pc, ps = transform_tables(block)
    norm = float(np.asarray(1.0 / math.sqrt(block), jnp.bfloat16))

    tokens_other = lax.ppermute(tokens, "mp", swap)
    cotangent_other = lax.ppermute(cotangent, "mp", swap)
    down_own = down_spectra.transpose(1, 0, 2)
    down_got = lax.ppermute(down_own, "mp", swap)

    inputs = (
        gate_spectra, up_spectra, pt, tokens, cotangent, down_own, down_got, tokens_other, cotangent_other, qf, pc, ps
    )
    buffers = [shape((2,) + down_own.shape, bf16) if n == 5 else a for n, a in enumerate(inputs) if n != 6]
    spec = shape((pairs, 2, 2, ROWS // 2, PAIR, LANES), bf16)
    d_all, gg, ug = call(
        functools.partial(main_kernel, fb, norm),
        (shape((pairs, 3 * ROWS, 2 * LANES), bf16), spec, spec),
        inputs,
        [pltpu.VMEM(a.shape, bf16) for a in buffers]
        + [pltpu.VMEM((pairs, 2, 2, db // 2, PAIR, LANES), bf16)] * 2
        + [pltpu.VMEM((fb, pairs, 2, PAIR, LANES), bf16)] * 3
        + [pltpu.VMEM(spec.shape, bf16)] * 3
        + [pltpu.VMEM((groups * 2 * ROWS, LANES), f32)] * 3
        + [pltpu.VMEM((2, 3, half, 2 * LANES), bf16)] * 2
        + [pltpu.VMEM((2, 3, F, 2 * LANES), f32), pltpu.VMEM((2, block // LANES, fb * db, LANES), f32)]
        + [pltpu.VMEM((2, block // LANES, 2 * fb * per, LANES), f32), pltpu.VMEM((pairs, 3 * ROWS, 2 * LANES), bf16)]
        + [pltpu.SemaphoreType.DMA((n,)) for n in (len(inputs), 2, pairs // 8)],
        limit=ALL_VMEM,
        flops=10**10,
        moved=10**7,
        in_specs=[HBM] * len(inputs),
        out_specs=(HBM, HBM, HBM),
    )

    direct = pairs % n_dp == 0
    if direct:
        share = pairs // n_dp
        got = lax.all_to_all(d_all.reshape(n_dp, share, 3 * ROWS, 2 * LANES), "dp", 0, 0, tiled=True)
    else:
        share = pairs
        got = lax.psum(d_all.astype(f32), "dp")[None]
    own, other = call(
        functools.partial(adjoint_kernel, fb),
        (shape((pairs, 2, per, PAIR, LANES), f32), shape((pairs, 2, per, PAIR, LANES), bf16)),
        (gate_spectra, up_spectra, gg, ug),
        [pltpu.VMEM(gate_spectra.shape, bf16)] * 2
        + [pltpu.VMEM(spec.shape, bf16)] * 2
        + [pltpu.VMEM((2, groups * 2 * db, LANES), f32)] * 2
        + [pltpu.VMEM((2, 2, db, PAIR, LANES), f32)]
        + [pltpu.VMEM((pairs, 2, per, PAIR, LANES), t) for t in (f32, bf16)]
        + [pltpu.SemaphoreType.DMA(n) for n in ((2,), (2, pairs), (2, pairs // 2))],
        limit=63 << 20,
        flops=2 * 10**9,
        moved=10**7,
        in_specs=[HBM] * 4,
        out_specs=(HBM, HBM),
    )
    total = call(reduce_kernel, shape((n_dp if direct else 1, share, 3 * ROWS, 2 * LANES), bf16), (got,), moved=10**6)
    total, own, other = lax.optimization_barrier((total, own, other))
    if direct:
        total = lax.all_to_all(total, "dp", 0, 0, tiled=True)
    partner = lax.ppermute(other, "mp", swap)
    grad_tokens = call(
        input_kernel,
        shape(tokens.shape, bf16),
        (qt, own, partner),
        [pltpu.VMEM(a.shape, a.dtype) for a in (qt, own, partner)] + [pltpu.SemaphoreType.DMA((3,))],
        limit=12 << 20,
        flops=5 * 10**8,
        moved=4 * 10**6,
        in_specs=[HBM] * 3,
    )
    total = total.reshape(pairs, 3 * ROWS, 2 * LANES)
    partner_sums = lax.ppermute(total, "mp", swap)
    scale = 1.0 / math.sqrt(tokens.shape[0] * n_dp)
    gate_grad, up_grad = call(
        functools.partial(layout_kernel, scale, fb),
        (shape((fb * db, block), f32),) * 2,
        (total,),
        [pltpu.VMEM((2, 2, fb * db, LANES), f32)],
        moved=10**6,
    )
    down_grad = call(
        functools.partial(down_layout_kernel, scale, fb),
        shape((2 * fb, per, block), f32),
        (total, partner_sums),
        moved=10**6,
    ).transpose(1, 0, 2)
    return (grad_tokens, gate_grad.reshape(fb, db, block), up_grad.reshape(fb, db, block), down_grad)


def solution(mesh):
    in_specs = (
        P(("groups", "dp"), "mp"),
        P(("groups", "dp"), "mp"),
        P("mp", None, None),
        P("mp", None, None),
        P("mp", None, None),
    )
    out_specs = (
        P(("groups", "dp"), "mp"),
        P(("groups", "mp"), None, None),
        P(("groups", "mp"), None, None),
        P(("groups", "mp"), None, None),
    )
    return jax.shard_map(shards, mesh=mesh, in_specs=in_specs, out_specs=out_specs, check_vma=False)
```

```python
import functools
import math

import jax
import jax.numpy as jnp
import numpy as np
from jax import lax
from jax.experimental import pallas as pl
from jax.experimental.pallas import tpu as pltpu
from jax.sharding import PartitionSpec as P


F = 8
PAIR = 2 * F
LANES = 128
ROWS = 16


def transform_tables(block):
    half = block // 2
    n = np.arange(block)
    k = np.arange(half)
    angles = ((n[:, None] * k[None, :]) % block).astype(np.float32) * np.float32(2.0 * math.pi / block)
    cosine = np.cos(angles.astype(np.float64)).astype(np.float32)
    sine = np.sin(angles.astype(np.float64)).astype(np.float32)
    parity = (1 - 2 * (n % 2)).astype(np.float32)
    norm = np.float32(1.0 / math.sqrt(block))
    forward = np.concatenate([cosine, parity[:, None], -sine[:, 1:]], axis=1) * norm
    doubling = np.where(k >= 1, 2.0, 1.0).astype(np.float32)
    inverse = np.concatenate([(cosine * doubling).T, parity[None, :], -2.0 * sine[:, 1:].T], axis=0) * norm
    order = np.arange(block).reshape(2, half // PAIR, PAIR).transpose(1, 0, 2).reshape(-1)
    extra = np.zeros((16, half), np.float32)
    folded = np.concatenate([np.arange(half), [half], np.arange(block - 1, half, -1)])
    forward_cos = np.concatenate([forward[:half, :half].T, extra], axis=0)
    forward_cos[half] = forward[:half, half]
    forward_sin = forward[:half, half:].T.copy()
    forward_sin[0] = 0.0
    natural = inverse.T[:, order]
    tables = (forward.T[order], natural, natural[folded], forward_cos, forward_sin)
    return [jnp.asarray(table, jnp.bfloat16) for table in tables]


def nt_dot(a, b):
    return lax.dot_general(a, b, (((1,), (1,)), ((), ())), preferred_element_type=jnp.float32)


def dot(a, b):
    return jnp.dot(a, b, preferred_element_type=jnp.float32)


def swap_blocks(tiles):
    tiles = list(tiles)
    lane_block = lax.broadcasted_iota(jnp.int32, tiles[0].shape, 1) // F
    step = len(tiles) // 2
    while step:
        high = (lane_block & step) != 0
        for i in range(len(tiles)):
            if i & step:
                continue
            low_tile, high_tile = tiles[i], tiles[i + step]
            tiles[i] = jnp.where(high, pltpu.roll(high_tile, F * step, 1), low_tile)
            tiles[i + step] = jnp.where(high, high_tile, pltpu.roll(low_tile, LANES - F * step, 1))
        step //= 2
    return tiles


def weight_rows(read, write, conj, half):
    for part in range(half // LANES):
        at = part * LANES
        tiles = swap_blocks([read(i, at) for i in range(8)] + [read(i, half + at) for i in range(8)])
        for i, tile in enumerate(tiles):
            lane = lax.broadcasted_iota(jnp.int32, tile.shape, 1)
            left = lane < LANES // 2
            turned = pltpu.roll(tile, LANES // 2, 1)
            if conj:
                real, imag = tile, jnp.where(left, -turned, turned)
            else:
                real, imag = jnp.where(left, tile, -tile), turned
            if part == 0 and i == 0:
                first = lane % F == 0
                real = jnp.where(first & ~left, 0.0, real)
                imag = jnp.where(first, jnp.where(left, 0.0, tile), imag)
            write(part * 16 + i, 0, real)
            write(part * 16 + i, 1, imag)


def adjoint_rows(read, write, half):
    for part in range(half // LANES):
        at = part * LANES
        re = swap_blocks([read(o, at) for o in range(16)])
        im = swap_blocks([read(o, half + at) for o in range(16)])
        for i in range(16):
            cross, wim = re[i], im[i]
            if part == 0 and i == 0:
                first = lax.broadcasted_iota(jnp.int32, wim.shape, 1) % F == 0
                cross = jnp.where(first, wim, cross)
                wim = jnp.where(first, 0.0, wim)
            write(part * 16 + i, 0, 0, re[i])
            write(part * 16 + i, 0, 1, wim)
            write(part * 16 + i, 1, 0, -wim)
            write(part * 16 + i, 1, 1, cross)


def diagonal():
    row = lax.broadcasted_iota(jnp.int32, (PAIR, LANES), 0)
    lane = lax.broadcasted_iota(jnp.int32, (PAIR, LANES), 1)
    return jnp.where(lane % F == row % F, 1.0, 0.0).astype(jnp.bfloat16)


def spread(read, count, mask):
    return jnp.concatenate(
        [jnp.concatenate([read(r), read(r + 1)], axis=0).astype(jnp.bfloat16) * mask for r in range(0, count, 2)], axis=0
    )


def blocks(first, second):
    zero = jnp.zeros_like(first)
    return jnp.concatenate(
        [jnp.concatenate([first, zero], axis=1), jnp.concatenate([zero, second], axis=1)], axis=0
    )


def side_by_side(values):
    return jnp.concatenate([values[..., :LANES], values[..., LANES:]], axis=-2)


def swiglu_back(gate, up, grad):
    sig = 1.0 / (1.0 + jnp.exp(-gate))
    gated = gate * sig
    slope = sig + gated * (1.0 - sig)
    return (
        (gated * up).astype(jnp.bfloat16),
        (grad * up * slope).astype(jnp.bfloat16),
        (grad * gated).astype(jnp.bfloat16),
    )


def main_kernel(fb, norm, wg_in, wu_in, pt_in, x_own_in, c_own_in, wd_own_in, wd_other_in, x_other_in, c_other_in,
                qf_in, pc_in, ps_in, d_out, gg_out, ug_out, wg_ref, wu_ref, pt_ref, x_own, c_own, wd_ref,
                x_other, c_other, qf_ref, pc_ref, ps_ref, sx, sc, gs, us, hs, hid, gg, ug, rg, ru, rd,
                sums_ref, diffs_ref, mids_ref, flat, flat_down, d_ref, in_sem, out_sem, d_sem):
    core = lax.axis_index("mp")
    db = 8
    per = db // 2
    block = pt_ref.shape[0]
    half = block // 2
    pairs = half // PAIR
    arrays = (
        (wg_in, wg_ref), (wu_in, wu_ref), (pt_in, pt_ref), (x_own_in, x_own), (c_own_in, c_own),
        (wd_own_in, wd_ref.at[core]), (wd_other_in, wd_ref.at[1 - core]),
        (x_other_in, x_other), (c_other_in, c_other),
        (qf_in, qf_ref), (pc_in, pc_ref), (ps_in, ps_ref),
    )
    copies = [pltpu.make_async_copy(src, dst, in_sem.at[n]) for n, (src, dst) in enumerate(arrays)]
    for copy in copies:
        copy.start()

    def to_spectra(source, target, first):
        rows = jnp.concatenate([source[:, j * block : (j + 1) * block] for j in range(per)], axis=0)
        result = nt_dot(pt_ref[...], rows).reshape(pairs, 2, 2, F, per * LANES)
        for j in range(0, per, 2):
            two = side_by_side(result[..., j * LANES : (j + 2) * LANES])
            target[:, :, :, first // 2 + j // 2] = two.astype(jnp.bfloat16)

    for n, (source, target) in enumerate(((wg_ref, rg), (wu_ref, ru))):
        copies[n].wait()
        if n:
            for copy in copies[2:5]:
                copy.wait()
            to_spectra(x_own, sx, core * per)
            to_spectra(c_own, sc, core * per)
        for tile in range(block // LANES):
            for o in range(fb):
                flat[n, tile, o * db : (o + 1) * db] = source[o, :, tile * LANES : (tile + 1) * LANES].astype(jnp.float32)

        def read(i, at, n=n):
            return flat[n, at // LANES, pl.ds(i, fb, stride=db), :]

        def write(group, ri, rows, target=target):
            at = (group * 2 + ri) * ROWS
            target[at : at + fb, :] = rows

        weight_rows(read, write, False, half)

    for copy in copies[5:9]:
        copy.wait()
    to_spectra(x_other, sx, (1 - core) * per)
    to_spectra(c_other, sc, (1 - core) * per)

    for side in range(2):
        for tile in range(block // LANES):
            rows = wd_ref[side, :, :, tile * LANES : (tile + 1) * LANES].astype(jnp.float32)
            flat_down[side, tile] = rows.reshape(2 * fb * per, LANES)

    def read_down(o, at):
        return flat_down[o // per, at // LANES, pl.ds(core * fb * per + o % per, fb, stride=per), :]

    def write_down(group, ri, rows):
        at = (group * 2 + ri) * ROWS
        rd[at : at + fb, :] = rows

    weight_rows(read_down, write_down, True, half)
    if fb < ROWS:
        for target in (gg, ug):
            target[:, :, :, fb // 2 :] = jnp.zeros((pairs, 2, 2, (ROWS - fb) // 2, PAIR, LANES), jnp.bfloat16)

    mask = diagonal()

    def both_groups(ref, g):
        return blocks(*(ref[g, :, h].reshape(LANES, LANES) for h in range(2)))

    def mix(g):
        for source, weights in ((sx, ((rg, gs), (ru, us))), (sc, ((rd, hs),))):
            spectrum = both_groups(source, g)
            for rows, target in weights:
                wide = jnp.concatenate(
                    [
                        jnp.concatenate(
                            [
                                spread(
                                    lambda o, h=h, ri=ri, rows=rows: rows[
                                        pl.ds(((2 * g + h) * 2 + ri) * ROWS + o, F, stride=0), :
                                    ],
                                    fb,
                                    mask,
                                )
                                for h in range(2)
                            ],
                            axis=1,
                        )
                        for ri in range(2)
                    ],
                    axis=0,
                )
                result = side_by_side(dot(wide, spectrum).reshape(2, fb, F, 2 * LANES)).astype(jnp.bfloat16)
                for ri in range(2):
                    target[:, g, ri] = result[ri]

    @pl.loop(0, pairs // 8)
    def _(n):
        for u in range(8):
            mix(8 * n + u)

    for copy in copies[9:]:
        copy.wait()
    top = lax.broadcasted_iota(jnp.int32, (F, LANES), 0)
    wide_top = lax.broadcasted_iota(jnp.int32, (F, 2 * LANES), 0)
    signed = jnp.where(wide_top % 2 == 0, norm, -norm)
    inner = jnp.where(lax.broadcasted_iota(jnp.int32, (PAIR, 2 * LANES), 0) == 0, 0.0, 1.0).astype(jnp.bfloat16)

    def set_row(values, row):
        return jnp.concatenate([jnp.where(wide_top == 0, row, values[:F]), values[F:]], axis=0)

    def add_tile(values, tile):
        return (values.reshape(-1, F, 2 * LANES) + tile[None]).reshape(values.shape)

    def to_values(pair):
        spectra = jnp.concatenate(
            [ref[2 * pair + u].reshape(block, LANES) for ref in (gs, us, hs) for u in range(2)], axis=1
        )
        return dot(qf_ref[...], spectra)

    def to_grads(values, slot):
        gate, up, grad = (values[:, v * 2 * LANES : (v + 1) * 2 * LANES] for v in range(3))
        for v, side in enumerate(swiglu_back(gate, up, grad)):
            near, far = side[:half], side[half:]
            mids_ref[slot, v] = far[:PAIR].astype(jnp.float32)[:F]
            sums_ref[slot, v, :PAIR] = near[:PAIR] + far[:PAIR] * inner
            sums_ref[slot, v, PAIR:] = near[PAIR:] + far[PAIR:]
            diffs_ref[slot, v] = near - far

    def to_grad_spectra(pair, slot):
        re = dot(pc_ref[...], jnp.concatenate([sums_ref[slot, v] for v in range(3)], axis=1))
        im = dot(ps_ref[...], jnp.concatenate([diffs_ref[slot, v] for v in range(3)], axis=1))
        for v, target in enumerate((hid, gg, ug)):
            lanes = slice(v * 2 * LANES, (v + 1) * 2 * LANES)
            middle = mids_ref[slot, v][:1]
            real = add_tile(re[:half, lanes], middle * signed)
            imag = set_row(im[:, lanes], re[half : half + 1, lanes] + middle * norm)
            for ri, both in enumerate((real, imag)):
                target[:, ri, :, pair] = side_by_side(both.reshape(pairs, 2, F, 2 * LANES)).astype(jnp.bfloat16)

    steps = fb // 2
    to_grads(to_values(0), 0)

    @pl.loop(0, (steps - 1) // 2)
    def _(n):
        for u in range(2):
            values = to_values(2 * n + u + 1)
            to_grad_spectra(2 * n + u, u)
            to_grads(values, 1 - u)

    if steps % 2 == 0:
        to_grad_spectra(steps - 2, 0)
        to_grads(to_values(steps - 1), 1)
    to_grad_spectra(steps - 1, 1 - steps % 2)

    stores = [
        pltpu.make_async_copy(src, dst, out_sem.at[n]) for n, (src, dst) in enumerate(((gg, gg_out), (ug, ug_out)))
    ]
    for copy in stores:
        copy.start()
    lane = lax.broadcasted_iota(jnp.int32, (F, LANES), 1)
    left = lane < LANES // 2

    def weight_sums(g):
        for w, (rows, cols, sign) in enumerate(((gg, sx, 1), (ug, sx, 1), (hid, sc, -1))):
            two = jnp.concatenate([rows[g, :, h, : fb // 2].reshape(2 * fb * F, LANES) for h in range(2)], axis=1)
            m = nt_dot(two, both_groups(cols, g))
            for h in range(2):
                result = []
                for upper in range(0, fb, 8):
                    sums = [jnp.zeros((F, LANES), jnp.float32)] * 2
                    for o in range(upper, min(upper + 8, fb)):
                        turn = o - upper
                        here = (top - lane) % 8 == turn
                        for q in range(2):
                            tile = m[(q * fb + o) * F : (q * fb + o + 1) * F, h * LANES : (h + 1) * LANES]
                            sums[q] = jnp.where(here, pltpu.roll(tile, turn, 0) if turn else tile, sums[q])
                    same = jnp.where(left, sums[0], sums[1])
                    cross = jnp.where(left, sums[1], sums[0])
                    turned = pltpu.roll(cross, LANES // 2, 1)
                    both = jnp.where(
                        left, same + pltpu.roll(same, LANES // 2, 1), turned - cross if sign > 0 else cross - turned
                    )
                    if h == 0:
                        both = jnp.where((lane % F == 0) & (g == 0), same, both)
                    result.append(both)
                d_ref[g, w * ROWS : (w + 1) * ROWS, h * LANES : (h + 1) * LANES] = jnp.concatenate(
                    result, axis=0
                ).astype(jnp.bfloat16)

    def sums_copy(n):
        rows = pl.ds(8 * n, 8)
        return pltpu.make_async_copy(d_ref.at[rows], d_out.at[rows], d_sem.at[n])

    @pl.loop(0, pairs // 8)
    def _(n):
        for u in range(8):
            weight_sums(8 * n + u)
        sums_copy(n).start()

    for n in range(pairs // 8):
        sums_copy(n).wait()
    for copy in stores:
        copy.wait()


def adjoint_kernel(fb, wg_in, wu_in, gg_in, ug_in, own_out, other_out, wg_ref, wu_ref, gg, ug, ra, rb, part, own_ref,
                   other_ref, in_sem, g_sem, out_sem):
    core = lax.axis_index("mp")
    db = 8
    per = db // 2
    pairs = gg.shape[0]
    half = pairs * PAIR
    weights = [
        pltpu.make_async_copy(src, dst, in_sem.at[n]) for n, (src, dst) in enumerate(((wg_in, wg_ref), (wu_in, wu_ref)))
    ]

    def group_copies(g):
        return [
            pltpu.make_async_copy(src.at[g], dst.at[g], g_sem.at[n, g])
            for n, (src, dst) in enumerate(((gg_in, gg), (ug_in, ug)))
        ]

    def results(n):
        rows = pl.ds(2 * n, 2)
        return [
            pltpu.make_async_copy(src.at[rows], dst.at[rows], out_sem.at[k, n])
            for k, (src, dst) in enumerate(((own_ref, own_out), (other_ref, other_out)))
        ]

    for copy in weights:
        copy.start()
    for g in range(pairs):
        for copy in group_copies(g):
            copy.start()
    for copy in weights:
        copy.wait()
    for source, adjoint in ((wg_ref, ra), (wu_ref, rb)):
        def read(o, at, source=source):
            if o >= fb:
                return jnp.zeros((db, LANES), jnp.float32)
            return source[o, :, at : at + LANES].astype(jnp.float32)

        def write(group, ri, tile, rows, adjoint=adjoint):
            at = (group * 2 + ri) * db
            adjoint[tile, at : at + db, :] = rows

        adjoint_rows(read, write, half)
    mask = diagonal()

    def mix(g, slot):
        spectrum = jnp.concatenate([blocks(*(ref[g, :, h].reshape(2 * LANES, LANES) for h in range(2))) for ref in (gg, ug)])
        wide = jnp.concatenate(
            [
                spread(
                    lambda r, h=h, tile=tile, ref=ref: ref[tile, pl.ds((2 * g + h) * 2 * db + r, F, stride=0), :],
                    2 * db,
                    mask,
                )
                for ref in (ra, rb)
                for h in range(2)
                for tile in range(2)
            ],
            axis=1,
        )
        part[slot] = side_by_side(dot(wide, spectrum).reshape(2, db, F, 2 * LANES))
        for ri in range(2):
            own_ref[g, ri] = part[slot, ri, pl.ds(core * per, per)]
            other_ref[g, ri] = part[slot, ri, pl.ds((1 - core) * per, per)].astype(jnp.bfloat16)

    @pl.loop(0, pairs // 2)
    def _(n):
        for u in range(2):
            for copy in group_copies(2 * n + u):
                copy.wait()
        for u in range(2):
            mix(2 * n + u, u)
        for copy in results(n):
            copy.start()

    for n in range(pairs // 2):
        for copy in results(n):
            copy.wait()


def input_kernel(qt_in, own_in, got_in, out_ref, qt_ref, own_ref, got_ref, in_sem):
    block = qt_ref.shape[0]
    copies = [
        pltpu.make_async_copy(src, dst, in_sem.at[n])
        for n, (src, dst) in enumerate(((qt_in, qt_ref), (own_in, own_ref), (got_in, got_ref)))
    ]
    for copy in copies:
        copy.start()
    for copy in copies:
        copy.wait()
    spectra = (own_ref[...] + got_ref[...].astype(jnp.float32)).astype(jnp.bfloat16)
    for j in range(0, own_ref.shape[2], 2):
        two = jnp.concatenate([spectra[:, :, j + u].reshape(block, LANES) for u in range(2)], axis=1)
        values = dot(qt_ref[...], two)
        for u in range(2):
            out_ref[:, (j + u) * block : (j + u + 1) * block] = values[:, u * LANES : (u + 1) * LANES].T.astype(jnp.bfloat16)


def straight(tile):
    halves = []
    lane = lax.broadcasted_iota(jnp.int32, (8, LANES), 1)
    for at in range(0, tile.shape[0], 8):
        half = tile[at : at + 8]
        for bit in (1, 2, 4):
            half = jnp.where((lane & bit) != 0, pltpu.roll(half, 8 - bit, 0), half)
        halves.append(half)
    return jnp.concatenate(halves, axis=0)


def reduce_kernel(r_ref, out_ref):
    for g in range(r_ref.shape[1]):
        for lanes in (slice(0, LANES), slice(LANES, 2 * LANES)):
            total = r_ref[0, g, :, lanes].astype(jnp.float32)
            for d in range(1, r_ref.shape[0]):
                total = total + r_ref[d, g, :, lanes].astype(jnp.float32)
            total = straight(total).astype(jnp.bfloat16)
            for d in range(out_ref.shape[0]):
                out_ref[d, g, :, lanes] = total


def entries(source, rows, part):
    tiles = []
    for i in range(16):
        lanes = slice((i % 2) * LANES, (i % 2 + 1) * LANES)
        tiles.append(source[part * 8 + i // 2, rows, lanes].astype(jnp.float32))
    return swap_blocks(tiles)


def factor(scale, part):
    lane = lax.broadcasted_iota(jnp.int32, (1, LANES), 1)
    return jnp.where((lane == 0) & (part == 0), scale, 2.0 * scale)


def layout_kernel(scale, fb, s_ref, gate_out, up_out, gate_ref, up_ref, flat, out_sem):
    half = s_ref.shape[0] * PAIR
    stores = [
        pltpu.make_async_copy(src, dst, out_sem.at[w]) for w, (src, dst) in enumerate(((gate_ref, gate_out), (up_ref, up_out)))
    ]
    for w, target in enumerate((gate_ref, up_ref)):
        for part in range(half // LANES):
            tiles = entries(s_ref, slice(w * ROWS, (w + 1) * ROWS), part)
            for ri in range(2):
                at = ri * half + part * LANES
                for i in range(8):
                    flat[w, ri, pl.ds(i, fb, stride=8), :] = tiles[8 * ri + i][:fb] * factor(scale, part)
                target[:, at : at + LANES] = flat[w, ri]
        stores[w].start()
    for copy in stores:
        copy.wait()


def down_layout_kernel(scale, fb, own_ref, got_ref, down_ref):
    core = lax.axis_index("mp")
    half = own_ref.shape[0] * PAIR
    outputs = down_ref.shape[1]
    for source, h in ((own_ref, core), (got_ref, 1 - core)):
        for part in range(half // LANES):
            tiles = entries(source, slice(2 * ROWS, 3 * ROWS), part)
            for ri in range(2):
                at = ri * half + part * LANES
                for o in range(outputs):
                    rows = jnp.where(core == 0, tiles[8 * ri + o], tiles[8 * ri + outputs + o])
                    down_ref[pl.ds(h * fb, fb), o, at : at + LANES] = rows[:fb] * factor(scale, part)


ALL_VMEM = 67043328


VMEM = pl.BlockSpec(memory_space=pltpu.VMEM)
HBM = pl.BlockSpec(memory_space=pltpu.HBM)


def call(kernel, out_shape, args, scratch=(), limit=16 << 20, flops=0, moved=0, in_specs=None, out_specs=None):
    return pl.pallas_call(
        kernel,
        out_shape=out_shape,
        in_specs=in_specs or [VMEM] * len(args),
        out_specs=out_specs or jax.tree.map(lambda _: VMEM, out_shape),
        scratch_shapes=list(scratch),
        compiler_params=pltpu.CompilerParams(vmem_limit_bytes=limit),
        cost_estimate=pl.CostEstimate(flops=flops, bytes_accessed=moved, transcendentals=0),
    )(*args)


def shards(tokens, cotangent, gate_spectra, up_spectra, down_spectra):
    n_dp = lax.axis_size("dp")
    swap = [(0, 1), (1, 0)]
    fb, db, block = gate_spectra.shape
    assert db == 8 and fb <= ROWS and fb % 2 == 0 and tokens.shape[0] == LANES and lax.axis_size("mp") == 2
    half = block // 2
    pairs = half // PAIR
    groups = half // F
    per = db // 2
    bf16, f32 = jnp.bfloat16, jnp.float32
    shape = jax.ShapeDtypeStruct
    pt, qt, qf, pc, ps = transform_tables(block)
    norm = float(np.asarray(1.0 / math.sqrt(block), jnp.bfloat16))

    tokens_other = lax.ppermute(tokens, "mp", swap)
    cotangent_other = lax.ppermute(cotangent, "mp", swap)
    down_own = down_spectra.transpose(1, 0, 2)
    down_got = lax.ppermute(down_own, "mp", swap)

    inputs = (
        gate_spectra, up_spectra, pt, tokens, cotangent, down_own, down_got, tokens_other, cotangent_other, qf, pc, ps
    )
    buffers = [shape((2,) + down_own.shape, bf16) if n == 5 else a for n, a in enumerate(inputs) if n != 6]
    spec = shape((pairs, 2, 2, ROWS // 2, PAIR, LANES), bf16)
    d_all, gg, ug = call(
        functools.partial(main_kernel, fb, norm),
        (shape((pairs, 3 * ROWS, 2 * LANES), bf16), spec, spec),
        inputs,
        [pltpu.VMEM(a.shape, bf16) for a in buffers]
        + [pltpu.VMEM((pairs, 2, 2, db // 2, PAIR, LANES), bf16)] * 2
        + [pltpu.VMEM((fb, pairs, 2, PAIR, LANES), bf16)] * 3
        + [pltpu.VMEM(spec.shape, bf16)] * 3
        + [pltpu.VMEM((groups * 2 * ROWS, LANES), f32)] * 3
        + [pltpu.VMEM((2, 3, half, 2 * LANES), bf16)] * 2
        + [pltpu.VMEM((2, 3, F, 2 * LANES), f32), pltpu.VMEM((2, block // LANES, fb * db, LANES), f32)]
        + [pltpu.VMEM((2, block // LANES, 2 * fb * per, LANES), f32), pltpu.VMEM((pairs, 3 * ROWS, 2 * LANES), bf16)]
        + [pltpu.SemaphoreType.DMA((n,)) for n in (len(inputs), 2, pairs // 8)],
        limit=ALL_VMEM,
        flops=10**10,
        moved=10**7,
        in_specs=[HBM] * len(inputs),
        out_specs=(HBM, HBM, HBM),
    )

    direct = pairs % n_dp == 0
    if direct:
        share = pairs // n_dp
        got = lax.all_to_all(d_all.reshape(n_dp, share, 3 * ROWS, 2 * LANES), "dp", 0, 0, tiled=True)
    else:
        share = pairs
        got = lax.psum(d_all.astype(f32), "dp")[None]
    own, other = call(
        functools.partial(adjoint_kernel, fb),
        (shape((pairs, 2, per, PAIR, LANES), f32), shape((pairs, 2, per, PAIR, LANES), bf16)),
        (gate_spectra, up_spectra, gg, ug),
        [pltpu.VMEM(gate_spectra.shape, bf16)] * 2
        + [pltpu.VMEM(spec.shape, bf16)] * 2
        + [pltpu.VMEM((2, groups * 2 * db, LANES), f32)] * 2
        + [pltpu.VMEM((2, 2, db, PAIR, LANES), f32)]
        + [pltpu.VMEM((pairs, 2, per, PAIR, LANES), t) for t in (f32, bf16)]
        + [pltpu.SemaphoreType.DMA(n) for n in ((2,), (2, pairs), (2, pairs // 2))],
        limit=63 << 20,
        flops=2 * 10**9,
        moved=10**7,
        in_specs=[HBM] * 4,
        out_specs=(HBM, HBM),
    )
    total = call(reduce_kernel, shape((n_dp if direct else 1, share, 3 * ROWS, 2 * LANES), bf16), (got,), moved=10**6)
    total, own, other = lax.optimization_barrier((total, own, other))
    if direct:
        total = lax.all_to_all(total, "dp", 0, 0, tiled=True)
    partner = lax.ppermute(other, "mp", swap)
    grad_tokens = call(
        input_kernel,
        shape(tokens.shape, bf16),
        (qt, own, partner),
        [pltpu.VMEM(a.shape, a.dtype) for a in (qt, own, partner)] + [pltpu.SemaphoreType.DMA((3,))],
        limit=12 << 20,
        flops=5 * 10**8,
        moved=4 * 10**6,
        in_specs=[HBM] * 3,
    )
    total = total.reshape(pairs, 3 * ROWS, 2 * LANES)
    partner_sums = lax.ppermute(total, "mp", swap)
    scale = 1.0 / math.sqrt(tokens.shape[0] * n_dp)
    gate_grad, up_grad = call(
        functools.partial(layout_kernel, scale, fb),
        (shape((fb * db, block), f32),) * 2,
        (total,),
        [pltpu.VMEM((fb * db, block), f32)] * 2
        + [pltpu.VMEM((2, 2, fb * db, LANES), f32), pltpu.SemaphoreType.DMA((2,))],
        moved=10**6,
        out_specs=(HBM,) * 2,
    )
    down_grad = call(
        functools.partial(down_layout_kernel, scale, fb),
        shape((2 * fb, per, block), f32),
        (total, partner_sums),
        moved=10**6,
    ).transpose(1, 0, 2)
    return (grad_tokens, gate_grad.reshape(fb, db, block), up_grad.reshape(fb, db, block), down_grad)


def solution(mesh):
    in_specs = (
        P(("groups", "dp"), "mp"),
        P(("groups", "dp"), "mp"),
        P("mp", None, None),
        P("mp", None, None),
        P("mp", None, None),
    )
    out_specs = (
        P(("groups", "dp"), "mp"),
        P(("groups", "mp"), None, None),
        P(("groups", "mp"), None, None),
        P(("groups", "mp"), None, None),
    )
    return jax.shard_map(shards, mesh=mesh, in_specs=in_specs, out_specs=out_specs, check_vma=False)
```

```python
import functools
import math

import jax
import jax.numpy as jnp
import numpy as np
from jax import lax
from jax.experimental import pallas as pl
from jax.experimental.pallas import tpu as pltpu
from jax.sharding import PartitionSpec as P


F = 8
PAIR = 2 * F
LANES = 128
ROWS = 16


def transform_tables(block):
    half = block // 2
    n = np.arange(block)
    k = np.arange(half)
    angles = ((n[:, None] * k[None, :]) % block).astype(np.float32) * np.float32(2.0 * math.pi / block)
    cosine = np.cos(angles.astype(np.float64)).astype(np.float32)
    sine = np.sin(angles.astype(np.float64)).astype(np.float32)
    parity = (1 - 2 * (n % 2)).astype(np.float32)
    norm = np.float32(1.0 / math.sqrt(block))
    forward = np.concatenate([cosine, parity[:, None], -sine[:, 1:]], axis=1) * norm
    doubling = np.where(k >= 1, 2.0, 1.0).astype(np.float32)
    inverse = np.concatenate([(cosine * doubling).T, parity[None, :], -2.0 * sine[:, 1:].T], axis=0) * norm
    order = np.arange(block).reshape(2, half // PAIR, PAIR).transpose(1, 0, 2).reshape(-1)
    extra = np.zeros((16, half), np.float32)
    folded = np.concatenate([np.arange(half), [half], np.arange(block - 1, half, -1)])
    forward_cos = np.concatenate([forward[:half, :half].T, extra], axis=0)
    forward_cos[half] = forward[:half, half]
    forward_sin = forward[:half, half:].T.copy()
    forward_sin[0] = 0.0
    natural = inverse.T[:, order]
    tables = (forward.T[order], natural, natural[folded], forward_cos, forward_sin)
    return [jnp.asarray(table, jnp.bfloat16) for table in tables]


def nt_dot(a, b):
    return lax.dot_general(a, b, (((1,), (1,)), ((), ())), preferred_element_type=jnp.float32)


def dot(a, b):
    return jnp.dot(a, b, preferred_element_type=jnp.float32)


def swap_blocks(tiles):
    tiles = list(tiles)
    lane_block = lax.broadcasted_iota(jnp.int32, tiles[0].shape, 1) // F
    step = len(tiles) // 2
    while step:
        high = (lane_block & step) != 0
        for i in range(len(tiles)):
            if i & step:
                continue
            low_tile, high_tile = tiles[i], tiles[i + step]
            tiles[i] = jnp.where(high, pltpu.roll(high_tile, F * step, 1), low_tile)
            tiles[i + step] = jnp.where(high, high_tile, pltpu.roll(low_tile, LANES - F * step, 1))
        step //= 2
    return tiles


def weight_rows(read, write, conj, half):
    for part in range(half // LANES):
        at = part * LANES
        tiles = swap_blocks([read(i, at) for i in range(8)] + [read(i, half + at) for i in range(8)])
        for i, tile in enumerate(tiles):
            lane = lax.broadcasted_iota(jnp.int32, tile.shape, 1)
            left = lane < LANES // 2
            turned = pltpu.roll(tile, LANES // 2, 1)
            if conj:
                real, imag = tile, jnp.where(left, -turned, turned)
            else:
                real, imag = jnp.where(left, tile, -tile), turned
            if part == 0 and i == 0:
                first = lane % F == 0
                real = jnp.where(first & ~left, 0.0, real)
                imag = jnp.where(first, jnp.where(left, 0.0, tile), imag)
            write(part * 16 + i, 0, real)
            write(part * 16 + i, 1, imag)


def adjoint_rows(read, write, half):
    for part in range(half // LANES):
        at = part * LANES
        re = swap_blocks([read(o, at) for o in range(16)])
        im = swap_blocks([read(o, half + at) for o in range(16)])
        for i in range(16):
            cross, wim = re[i], im[i]
            if part == 0 and i == 0:
                first = lax.broadcasted_iota(jnp.int32, wim.shape, 1) % F == 0
                cross = jnp.where(first, wim, cross)
                wim = jnp.where(first, 0.0, wim)
            write(part * 16 + i, 0, 0, re[i])
            write(part * 16 + i, 0, 1, wim)
            write(part * 16 + i, 1, 0, -wim)
            write(part * 16 + i, 1, 1, cross)


def diagonal():
    row = lax.broadcasted_iota(jnp.int32, (PAIR, LANES), 0)
    lane = lax.broadcasted_iota(jnp.int32, (PAIR, LANES), 1)
    return jnp.where(lane % F == row % F, 1.0, 0.0).astype(jnp.bfloat16)


def spread(read, count, mask):
    return jnp.concatenate(
        [jnp.concatenate([read(r), read(r + 1)], axis=0).astype(jnp.bfloat16) * mask for r in range(0, count, 2)], axis=0
    )


def blocks(first, second):
    zero = jnp.zeros_like(first)
    return jnp.concatenate(
        [jnp.concatenate([first, zero], axis=1), jnp.concatenate([zero, second], axis=1)], axis=0
    )


def side_by_side(values):
    return jnp.concatenate([values[..., :LANES], values[..., LANES:]], axis=-2)


def swiglu_back(gate, up, grad):
    sig = 1.0 / (1.0 + jnp.exp(-gate))
    gated = gate * sig
    slope = sig + gated * (1.0 - sig)
    return (
        (gated * up).astype(jnp.bfloat16),
        (grad * up * slope).astype(jnp.bfloat16),
        (grad * gated).astype(jnp.bfloat16),
    )


def main_kernel(fb, norm, wg_in, wu_in, pt_in, x_own_in, c_own_in, wd_own_in, wd_other_in, x_other_in, c_other_in,
                qf_in, pc_in, ps_in, d_out, gg_out, ug_out, wg_ref, wu_ref, pt_ref, x_own, c_own, wd_ref,
                x_other, c_other, qf_ref, pc_ref, ps_ref, sx, sc, gs, us, hs, hid, gg, ug, rg, ru, rd,
                sums_ref, diffs_ref, mids_ref, flat, flat_down, d_ref, in_sem, out_sem, d_sem):
    core = lax.axis_index("mp")
    db = 8
    per = db // 2
    block = pt_ref.shape[0]
    half = block // 2
    pairs = half // PAIR
    arrays = (
        (wg_in, wg_ref), (wu_in, wu_ref), (pt_in, pt_ref), (x_own_in, x_own), (c_own_in, c_own),
        (wd_own_in, wd_ref.at[core]), (wd_other_in, wd_ref.at[1 - core]),
        (x_other_in, x_other), (c_other_in, c_other),
        (qf_in, qf_ref), (pc_in, pc_ref), (ps_in, ps_ref),
    )
    copies = [pltpu.make_async_copy(src, dst, in_sem.at[n]) for n, (src, dst) in enumerate(arrays)]
    for copy in copies:
        copy.start()

    def to_spectra(source, target, first):
        rows = jnp.concatenate([source[:, j * block : (j + 1) * block] for j in range(per)], axis=0)
        result = nt_dot(pt_ref[...], rows).reshape(pairs, 2, 2, F, per * LANES)
        for j in range(0, per, 2):
            two = side_by_side(result[..., j * LANES : (j + 2) * LANES])
            target[:, :, :, first // 2 + j // 2] = two.astype(jnp.bfloat16)

    for n, (source, target) in enumerate(((wg_ref, rg), (wu_ref, ru))):
        copies[n].wait()
        if n:
            for copy in copies[2:5]:
                copy.wait()
            to_spectra(x_own, sx, core * per)
            to_spectra(c_own, sc, core * per)
        for tile in range(block // LANES):
            for o in range(fb):
                flat[n, tile, o * db : (o + 1) * db] = source[o, :, tile * LANES : (tile + 1) * LANES].astype(jnp.float32)

        def read(i, at, n=n):
            return flat[n, at // LANES, pl.ds(i, fb, stride=db), :]

        def write(group, ri, rows, target=target):
            at = (group * 2 + ri) * ROWS
            target[at : at + fb, :] = rows

        weight_rows(read, write, False, half)

    for copy in copies[5:9]:
        copy.wait()
    to_spectra(x_other, sx, (1 - core) * per)
    to_spectra(c_other, sc, (1 - core) * per)

    for side in range(2):
        for tile in range(block // LANES):
            rows = wd_ref[side, :, :, tile * LANES : (tile + 1) * LANES].astype(jnp.float32)
            flat_down[side, tile, : 2 * fb * per] = rows.reshape(2 * fb * per, LANES)

    def read_down(o, at):
        return flat_down[o // per, at // LANES, pl.ds(core * fb * per + o % per, fb, stride=per), :]

    def write_down(group, ri, rows):
        at = (group * 2 + ri) * ROWS
        rd[at : at + fb, :] = rows

    weight_rows(read_down, write_down, True, half)
    if fb < ROWS:
        for target in (gg, ug):
            target[:, :, :, fb // 2 :] = jnp.zeros((pairs, 2, 2, (ROWS - fb) // 2, PAIR, LANES), jnp.bfloat16)

    mask = diagonal()

    def both_groups(ref, g):
        return blocks(*(ref[g, :, h].reshape(LANES, LANES) for h in range(2)))

    def mix(g):
        for source, weights in ((sx, ((rg, gs), (ru, us))), (sc, ((rd, hs),))):
            spectrum = both_groups(source, g)
            for rows, target in weights:
                wide = jnp.concatenate(
                    [
                        jnp.concatenate(
                            [
                                spread(
                                    lambda o, h=h, ri=ri, rows=rows: rows[
                                        pl.ds(((2 * g + h) * 2 + ri) * ROWS + o, F, stride=0), :
                                    ],
                                    fb,
                                    mask,
                                )
                                for h in range(2)
                            ],
                            axis=1,
                        )
                        for ri in range(2)
                    ],
                    axis=0,
                )
                result = side_by_side(dot(wide, spectrum).reshape(2, fb, F, 2 * LANES)).astype(jnp.bfloat16)
                for ri in range(2):
                    target[:, g, ri] = result[ri]

    @pl.loop(0, pairs // 8)
    def _(n):
        for u in range(8):
            mix(8 * n + u)

    for copy in copies[9:]:
        copy.wait()
    top = lax.broadcasted_iota(jnp.int32, (F, LANES), 0)
    wide_top = lax.broadcasted_iota(jnp.int32, (F, 2 * LANES), 0)
    signed = jnp.where(wide_top % 2 == 0, norm, -norm)
    inner = jnp.where(lax.broadcasted_iota(jnp.int32, (PAIR, 2 * LANES), 0) == 0, 0.0, 1.0).astype(jnp.bfloat16)

    def set_row(values, row):
        return jnp.concatenate([jnp.where(wide_top == 0, row, values[:F]), values[F:]], axis=0)

    def add_tile(values, tile):
        return (values.reshape(-1, F, 2 * LANES) + tile[None]).reshape(values.shape)

    def to_values(pair):
        spectra = jnp.concatenate(
            [ref[2 * pair + u].reshape(block, LANES) for ref in (gs, us, hs) for u in range(2)], axis=1
        )
        return dot(qf_ref[...], spectra)

    def to_grads(values, slot):
        gate, up, grad = (values[:, v * 2 * LANES : (v + 1) * 2 * LANES] for v in range(3))
        for v, side in enumerate(swiglu_back(gate, up, grad)):
            near, far = side[:half], side[half:]
            mids_ref[slot, v] = far[:PAIR].astype(jnp.float32)[:F]
            sums_ref[slot, v, :PAIR] = near[:PAIR] + far[:PAIR] * inner
            sums_ref[slot, v, PAIR:] = near[PAIR:] + far[PAIR:]
            diffs_ref[slot, v] = near - far

    def to_grad_spectra(pair, slot):
        re = dot(pc_ref[...], jnp.concatenate([sums_ref[slot, v] for v in range(3)], axis=1))
        im = dot(ps_ref[...], jnp.concatenate([diffs_ref[slot, v] for v in range(3)], axis=1))
        for v, target in enumerate((hid, gg, ug)):
            lanes = slice(v * 2 * LANES, (v + 1) * 2 * LANES)
            middle = mids_ref[slot, v][:1]
            real = add_tile(re[:half, lanes], middle * signed)
            imag = set_row(im[:, lanes], re[half : half + 1, lanes] + middle * norm)
            for ri, both in enumerate((real, imag)):
                target[:, ri, :, pair] = side_by_side(both.reshape(pairs, 2, F, 2 * LANES)).astype(jnp.bfloat16)

    steps = fb // 2
    to_grads(to_values(0), 0)

    @pl.loop(0, (steps - 1) // 2)
    def _(n):
        for u in range(2):
            values = to_values(2 * n + u + 1)
            to_grad_spectra(2 * n + u, u)
            to_grads(values, 1 - u)

    if steps % 2 == 0:
        to_grad_spectra(steps - 2, 0)
        to_grads(to_values(steps - 1), 1)
    to_grad_spectra(steps - 1, 1 - steps % 2)

    stores = [
        pltpu.make_async_copy(src, dst, out_sem.at[n]) for n, (src, dst) in enumerate(((gg, gg_out), (ug, ug_out)))
    ]
    for copy in stores:
        copy.start()
    lane = lax.broadcasted_iota(jnp.int32, (F, LANES), 1)
    left = lane < LANES // 2

    def weight_sums(g):
        for w, (rows, cols, sign) in enumerate(((gg, sx, 1), (ug, sx, 1), (hid, sc, -1))):
            two = jnp.concatenate([rows[g, :, h, : fb // 2].reshape(2 * fb * F, LANES) for h in range(2)], axis=1)
            m = nt_dot(two, both_groups(cols, g))
            for h in range(2):
                result = []
                for upper in range(0, fb, 8):
                    sums = [jnp.zeros((F, LANES), jnp.float32)] * 2
                    for o in range(upper, min(upper + 8, fb)):
                        turn = o - upper
                        here = (top - lane) % 8 == turn
                        for q in range(2):
                            tile = m[(q * fb + o) * F : (q * fb + o + 1) * F, h * LANES : (h + 1) * LANES]
                            sums[q] = jnp.where(here, pltpu.roll(tile, turn, 0) if turn else tile, sums[q])
                    same = jnp.where(left, sums[0], sums[1])
                    cross = jnp.where(left, sums[1], sums[0])
                    turned = pltpu.roll(cross, LANES // 2, 1)
                    both = jnp.where(
                        left, same + pltpu.roll(same, LANES // 2, 1), turned - cross if sign > 0 else cross - turned
                    )
                    if h == 0:
                        both = jnp.where((lane % F == 0) & (g == 0), same, both)
                    result.append(both)
                d_ref[g, w * ROWS : (w + 1) * ROWS, h * LANES : (h + 1) * LANES] = jnp.concatenate(
                    result, axis=0
                ).astype(jnp.bfloat16)

    def sums_copy(n):
        rows = pl.ds(8 * n, 8)
        return pltpu.make_async_copy(d_ref.at[rows], d_out.at[rows], d_sem.at[n])

    @pl.loop(0, pairs // 8)
    def _(n):
        for u in range(8):
            weight_sums(8 * n + u)
        sums_copy(n).start()

    for n in range(pairs // 8):
        sums_copy(n).wait()
    for copy in stores:
        copy.wait()


def adjoint_kernel(fb, wg_in, wu_in, gg_in, ug_in, own_out, other_out, wg_ref, wu_ref, gg, ug, ra, rb, part, own_ref,
                   other_ref, in_sem, g_sem, out_sem):
    core = lax.axis_index("mp")
    db = 8
    per = db // 2
    pairs = gg.shape[0]
    half = pairs * PAIR
    weights = [
        pltpu.make_async_copy(src, dst, in_sem.at[n]) for n, (src, dst) in enumerate(((wg_in, wg_ref), (wu_in, wu_ref)))
    ]

    def group_copies(g):
        return [
            pltpu.make_async_copy(src.at[g], dst.at[g], g_sem.at[n, g])
            for n, (src, dst) in enumerate(((gg_in, gg), (ug_in, ug)))
        ]

    def results(n):
        rows = pl.ds(2 * n, 2)
        return [
            pltpu.make_async_copy(src.at[rows], dst.at[rows], out_sem.at[k, n])
            for k, (src, dst) in enumerate(((own_ref, own_out), (other_ref, other_out)))
        ]

    for copy in weights:
        copy.start()
    for g in range(pairs):
        for copy in group_copies(g):
            copy.start()
    for copy in weights:
        copy.wait()
    for source, adjoint in ((wg_ref, ra), (wu_ref, rb)):
        def read(o, at, source=source):
            if o >= fb:
                return jnp.zeros((db, LANES), jnp.float32)
            return source[o, :, at : at + LANES].astype(jnp.float32)

        def write(group, ri, tile, rows, adjoint=adjoint):
            at = (group * 2 + ri) * db
            adjoint[tile, at : at + db, :] = rows

        adjoint_rows(read, write, half)
    mask = diagonal()

    def mix(g, slot):
        spectrum = jnp.concatenate([blocks(*(ref[g, :, h].reshape(2 * LANES, LANES) for h in range(2))) for ref in (gg, ug)])
        wide = jnp.concatenate(
            [
                spread(
                    lambda r, h=h, tile=tile, ref=ref: ref[tile, pl.ds((2 * g + h) * 2 * db + r, F, stride=0), :],
                    2 * db,
                    mask,
                )
                for ref in (ra, rb)
                for h in range(2)
                for tile in range(2)
            ],
            axis=1,
        )
        part[slot] = side_by_side(dot(wide, spectrum).reshape(2, db, F, 2 * LANES))
        for ri in range(2):
            own_ref[g, ri] = part[slot, ri, pl.ds(core * per, per)]
            other_ref[g, ri] = part[slot, ri, pl.ds((1 - core) * per, per)].astype(jnp.bfloat16)

    @pl.loop(0, pairs // 2)
    def _(n):
        for u in range(2):
            for copy in group_copies(2 * n + u):
                copy.wait()
        for u in range(2):
            mix(2 * n + u, u)
        for copy in results(n):
            copy.start()

    for n in range(pairs // 2):
        for copy in results(n):
            copy.wait()


def input_kernel(qt_in, own_in, got_in, out_ref, qt_ref, own_ref, got_ref, in_sem):
    block = qt_ref.shape[0]
    copies = [
        pltpu.make_async_copy(src, dst, in_sem.at[n])
        for n, (src, dst) in enumerate(((qt_in, qt_ref), (own_in, own_ref), (got_in, got_ref)))
    ]
    for copy in copies:
        copy.start()
    for copy in copies:
        copy.wait()
    spectra = (own_ref[...] + got_ref[...].astype(jnp.float32)).astype(jnp.bfloat16)
    for j in range(0, own_ref.shape[2], 2):
        two = jnp.concatenate([spectra[:, :, j + u].reshape(block, LANES) for u in range(2)], axis=1)
        values = dot(qt_ref[...], two)
        for u in range(2):
            out_ref[:, (j + u) * block : (j + u + 1) * block] = values[:, u * LANES : (u + 1) * LANES].T.astype(jnp.bfloat16)


def straight(tile):
    halves = []
    lane = lax.broadcasted_iota(jnp.int32, (8, LANES), 1)
    for at in range(0, tile.shape[0], 8):
        half = tile[at : at + 8]
        for bit in (1, 2, 4):
            half = jnp.where((lane & bit) != 0, pltpu.roll(half, 8 - bit, 0), half)
        halves.append(half)
    return jnp.concatenate(halves, axis=0)


def reduce_kernel(r_ref, out_ref):
    for g in range(r_ref.shape[1]):
        for lanes in (slice(0, LANES), slice(LANES, 2 * LANES)):
            total = r_ref[0, g, :, lanes].astype(jnp.float32)
            for d in range(1, r_ref.shape[0]):
                total = total + r_ref[d, g, :, lanes].astype(jnp.float32)
            total = straight(total).astype(jnp.bfloat16)
            for d in range(out_ref.shape[0]):
                out_ref[d, g, :, lanes] = total


def entries(source, rows, part):
    tiles = []
    for i in range(16):
        lanes = slice((i % 2) * LANES, (i % 2 + 1) * LANES)
        tiles.append(source[part * 8 + i // 2, rows, lanes].astype(jnp.float32))
    return swap_blocks(tiles)


def factor(scale, part):
    lane = lax.broadcasted_iota(jnp.int32, (1, LANES), 1)
    return jnp.where((lane == 0) & (part == 0), scale, 2.0 * scale)


def layout_kernel(scale, fb, s_ref, gate_out, up_out, gate_ref, up_ref, flat, out_sem):
    half = s_ref.shape[0] * PAIR
    stores = [
        pltpu.make_async_copy(src, dst, out_sem.at[w]) for w, (src, dst) in enumerate(((gate_ref, gate_out), (up_ref, up_out)))
    ]
    for w, target in enumerate((gate_ref, up_ref)):
        for part in range(half // LANES):
            tiles = entries(s_ref, slice(w * ROWS, (w + 1) * ROWS), part)
            for ri in range(2):
                at = ri * half + part * LANES
                for i in range(8):
                    flat[w, ri, pl.ds(i, fb, stride=8), :] = tiles[8 * ri + i][:fb] * factor(scale, part)
                target[:, at : at + LANES] = flat[w, ri, : 8 * fb]
        stores[w].start()
    for copy in stores:
        copy.wait()


def down_layout_kernel(scale, fb, own_ref, got_ref, down_ref):
    core = lax.axis_index("mp")
    half = own_ref.shape[0] * PAIR
    outputs = down_ref.shape[1]
    for source, h in ((own_ref, core), (got_ref, 1 - core)):
        for part in range(half // LANES):
            tiles = entries(source, slice(2 * ROWS, 3 * ROWS), part)
            for ri in range(2):
                at = ri * half + part * LANES
                for o in range(outputs):
                    rows = jnp.where(core == 0, tiles[8 * ri + o], tiles[8 * ri + outputs + o])
                    down_ref[pl.ds(h * fb, fb), o, at : at + LANES] = rows[:fb] * factor(scale, part)


ALL_VMEM = 67043328


VMEM = pl.BlockSpec(memory_space=pltpu.VMEM)
HBM = pl.BlockSpec(memory_space=pltpu.HBM)


def call(kernel, out_shape, args, scratch=(), limit=16 << 20, flops=0, moved=0, in_specs=None, out_specs=None):
    return pl.pallas_call(
        kernel,
        out_shape=out_shape,
        in_specs=in_specs or [VMEM] * len(args),
        out_specs=out_specs or jax.tree.map(lambda _: VMEM, out_shape),
        scratch_shapes=list(scratch),
        compiler_params=pltpu.CompilerParams(vmem_limit_bytes=limit),
        cost_estimate=pl.CostEstimate(flops=flops, bytes_accessed=moved, transcendentals=0),
    )(*args)


def shards(tokens, cotangent, gate_spectra, up_spectra, down_spectra):
    n_dp = lax.axis_size("dp")
    swap = [(0, 1), (1, 0)]
    fb, db, block = gate_spectra.shape
    assert db == 8 and fb <= ROWS and fb % 2 == 0 and tokens.shape[0] == LANES and lax.axis_size("mp") == 2
    half = block // 2
    pairs = half // PAIR
    groups = half // F
    per = db // 2
    bf16, f32 = jnp.bfloat16, jnp.float32
    shape = jax.ShapeDtypeStruct
    pt, qt, qf, pc, ps = transform_tables(block)
    norm = float(np.asarray(1.0 / math.sqrt(block), jnp.bfloat16))

    tokens_other = lax.ppermute(tokens, "mp", swap)
    cotangent_other = lax.ppermute(cotangent, "mp", swap)
    down_own = down_spectra.transpose(1, 0, 2)
    down_got = lax.ppermute(down_own, "mp", swap)

    inputs = (
        gate_spectra, up_spectra, pt, tokens, cotangent, down_own, down_got, tokens_other, cotangent_other, qf, pc, ps
    )
    buffers = [shape((2,) + down_own.shape, bf16) if n == 5 else a for n, a in enumerate(inputs) if n != 6]
    spec = shape((pairs, 2, 2, ROWS // 2, PAIR, LANES), bf16)
    d_all, gg, ug = call(
        functools.partial(main_kernel, fb, norm),
        (shape((pairs, 3 * ROWS, 2 * LANES), bf16), spec, spec),
        inputs,
        [pltpu.VMEM(a.shape, bf16) for a in buffers]
        + [pltpu.VMEM((pairs, 2, 2, db // 2, PAIR, LANES), bf16)] * 2
        + [pltpu.VMEM((fb, pairs, 2, PAIR, LANES), bf16)] * 3
        + [pltpu.VMEM(spec.shape, bf16)] * 3
        + [pltpu.VMEM((groups * 2 * ROWS + F, LANES), f32)] * 3
        + [pltpu.VMEM((2, 3, half, 2 * LANES), bf16)] * 2
        + [pltpu.VMEM((2, 3, F, 2 * LANES), f32), pltpu.VMEM((2, block // LANES, ROWS * db, LANES), f32)]
        + [pltpu.VMEM((2, block // LANES, 2 * ROWS * per, LANES), f32), pltpu.VMEM((pairs, 3 * ROWS, 2 * LANES), bf16)]
        + [pltpu.SemaphoreType.DMA((n,)) for n in (len(inputs), 2, pairs // 8)],
        limit=ALL_VMEM,
        flops=10**10,
        moved=10**7,
        in_specs=[HBM] * len(inputs),
        out_specs=(HBM, HBM, HBM),
    )

    direct = pairs % n_dp == 0
    if direct:
        share = pairs // n_dp
        got = lax.all_to_all(d_all.reshape(n_dp, share, 3 * ROWS, 2 * LANES), "dp", 0, 0, tiled=True)
    else:
        share = pairs
        got = lax.psum(d_all.astype(f32), "dp")[None]
    own, other = call(
        functools.partial(adjoint_kernel, fb),
        (shape((pairs, 2, per, PAIR, LANES), f32), shape((pairs, 2, per, PAIR, LANES), bf16)),
        (gate_spectra, up_spectra, gg, ug),
        [pltpu.VMEM(gate_spectra.shape, bf16)] * 2
        + [pltpu.VMEM(spec.shape, bf16)] * 2
        + [pltpu.VMEM((2, groups * 2 * db + F, LANES), f32)] * 2
        + [pltpu.VMEM((2, 2, db, PAIR, LANES), f32)]
        + [pltpu.VMEM((pairs, 2, per, PAIR, LANES), t) for t in (f32, bf16)]
        + [pltpu.SemaphoreType.DMA(n) for n in ((2,), (2, pairs), (2, pairs // 2))],
        limit=63 << 20,
        flops=2 * 10**9,
        moved=10**7,
        in_specs=[HBM] * 4,
        out_specs=(HBM, HBM),
    )
    total = call(reduce_kernel, shape((n_dp if direct else 1, share, 3 * ROWS, 2 * LANES), bf16), (got,), moved=10**6)
    total, own, other = lax.optimization_barrier((total, own, other))
    if direct:
        total = lax.all_to_all(total, "dp", 0, 0, tiled=True)
    partner = lax.ppermute(other, "mp", swap)
    grad_tokens = call(
        input_kernel,
        shape(tokens.shape, bf16),
        (qt, own, partner),
        [pltpu.VMEM(a.shape, a.dtype) for a in (qt, own, partner)] + [pltpu.SemaphoreType.DMA((3,))],
        limit=12 << 20,
        flops=5 * 10**8,
        moved=4 * 10**6,
        in_specs=[HBM] * 3,
    )
    total = total.reshape(pairs, 3 * ROWS, 2 * LANES)
    partner_sums = lax.ppermute(total, "mp", swap)
    scale = 1.0 / math.sqrt(tokens.shape[0] * n_dp)
    gate_grad, up_grad = call(
        functools.partial(layout_kernel, scale, fb),
        (shape((fb * db, block), f32),) * 2,
        (total,),
        [pltpu.VMEM((fb * db, block), f32)] * 2
        + [pltpu.VMEM((2, 2, ROWS * db, LANES), f32), pltpu.SemaphoreType.DMA((2,))],
        moved=10**6,
        out_specs=(HBM,) * 2,
    )
    down_grad = call(
        functools.partial(down_layout_kernel, scale, fb),
        shape((2 * fb, per, block), f32),
        (total, partner_sums),
        moved=10**6,
    ).transpose(1, 0, 2)
    return (grad_tokens, gate_grad.reshape(fb, db, block), up_grad.reshape(fb, db, block), down_grad)


def solution(mesh):
    in_specs = (
        P(("groups", "dp"), "mp"),
        P(("groups", "dp"), "mp"),
        P("mp", None, None),
        P("mp", None, None),
        P("mp", None, None),
    )
    out_specs = (
        P(("groups", "dp"), "mp"),
        P(("groups", "mp"), None, None),
        P(("groups", "mp"), None, None),
        P(("groups", "mp"), None, None),
    )
    return jax.shard_map(shards, mesh=mesh, in_specs=in_specs, out_specs=out_specs, check_vma=False)
```
